32 devices in a mesh: shard: 16 (over z, x, core), replica: 2 (over y).
Axes of the slice: x: 2, y: 2, z: 4, core: 2. Of those that a mesh axis runs over, the one named last changes fastest.
Arguments:
- x_in: bfloat16 [2, 8192, 768], P('replica', 'shard'), may hold values from -6 to 6
- seq_units: int32 [2, 16], P('replica'), may hold values from 1 to 64, 512 in all within a row
- deal: int32 [2, 16], P('replica'), may hold values from 0 to 15, each once within a row
- gain_attn: float32 [768], replicated, may hold values from 0.1 to 1.9
- w_query: bfloat16 [768, 768], P('shard'), may hold values from -0.4375 to 0.4375
- w_key: bfloat16 [768, 768], P('shard'), may hold values from -0.21875 to 0.21875
- w_value: bfloat16 [768, 768], P('shard'), may hold values from -0.21875 to 0.21875
- w_out: bfloat16 [768, 768], P('shard'), may hold values from -0.875 to 0.875
- gain_ffn: float32 [768], replicated, may hold values from 0.1 to 1.9
- w_gate: bfloat16 [768, 2048], P('shard'), may hold values from -0.21875 to 0.21875
- w_up: bfloat16 [768, 2048], P('shard'), may hold values from -0.21875 to 0.21875
- w_down: bfloat16 [2048, 768], P('shard'), may hold values from -0.125 to 0.125
- d_out: bfloat16 [2, 16, 1024, 768], P('replica', 'shard'), may hold values from -6 to 6
Outputs:
- layer_out: bfloat16 [2, 16, 1024, 768], P('replica', 'shard')
- grad_x: bfloat16 [2, 8192, 768], P('replica', 'shard')
- grad_gain_attn: float32 [768], P('shard')
- grad_gain_ffn: float32 [768], P('shard')
- grad_w_query: float32 [768, 768], P('shard')
- grad_w_key: float32 [768, 768], P('shard')
- grad_w_value: float32 [768, 768], P('shard')
- grad_w_out: float32 [768, 768], P('shard')
- grad_w_gate: float32 [768, 2048], P('shard')
- grad_w_up: float32 [768, 2048], P('shard')
- grad_w_down: float32 [2048, 768], P('shard')
The draws below stay inside these ranges and needn't reach their ends.
Inputs may be any that keep to these rules, and one draw needn't show every extreme that they name: `seq_units`: each group's 16 entries sum to 512. `deal`: each group's row names every sequence 0 to 15 once.
All inputs are finite; a program needn't handle non-finite values.
Results may differ from the reference program's by a relative error of at most 0.023.
Values may be sent and summed in bfloat16 or wider, within the bound.
No kernel may reach another device: no remote copies, remote signals or barrier semaphores. Data moves between devices by JAX's collectives and lax.ppermute only.
A program may use at most 320 MiB of HBM per device.

```python
import math
import jax
import jax.numpy as jnp
import numpy as np
from jax import lax

D = 768
H = 12
HD = 64
FF = 2048
MAXLEN = 1024
TOK_DEV = 512
UNIT_MAX = 64
GTOK = 8192
N_SHARD = 16
N_REPLICA = 2


def steps_of(key, dims, shards, low, high):
    gain, own = 1.0, jax.random.fold_in(key, 6)
    for dim, parts in shards:
        heights = jnp.exp(jax.random.uniform(jax.random.fold_in(own, dim), (parts,), jnp.float32, low / len(shards), high / len(shards)))
        gain = gain * jnp.repeat(heights, dims[dim] // parts).reshape([-1 if axis == dim else 1 for axis in range(len(dims))])
    return gain


def length_profile(number_of, total, bound, slope):
    loads = [(1 << 20) // math.isqrt(grade ** slope) + 1 for grade in range(2, number_of + 1)]
    spare, given = total - bound - (number_of - 1), [1] * (number_of - 1)
    while spare > 0:
        candidates = [i for i in range(number_of - 1) if given[i] < bound]
        mass, left = sum([loads[i] for i in candidates]), spare
        for i in candidates:
            addition = min(bound - given[i], max(1, left * loads[i] // mass), spare)
            given[i] = given[i] + addition
            spare = spare - addition
    return np.array([bound] + given)


def uneven(own_key, amount, total, limit, skew):
    if amount == 2:
        one = jax.random.randint(own_key, (), max(1, total - limit), min(limit, total - 1) + 1)
        return jnp.stack([one, total - one])
    sizes = jnp.asarray(length_profile(amount, total, limit, skew), jnp.int32)
    pairs = (amount - 1) // 2
    giver, sink = sizes[1:1 + 2 * pairs:2], sizes[2:2 + 2 * pairs:2]
    margin = jnp.minimum(giver - 1, limit - sink)
    passed = jax.random.randint(jax.random.fold_in(own_key, 1), (pairs,), 0, 1 << 20) % (margin + 1)
    sizes = sizes.at[1:1 + 2 * pairs:2].set(giver - passed).at[2:2 + 2 * pairs:2].set(sink + passed)
    return sizes[jax.random.permutation(jax.random.fold_in(own_key, 2), amount)]


def scatter_about(stream_key, dims, scale, limit, pieces=(), kind=jnp.bfloat16):
    drawn = scale * jax.random.normal(stream_key, dims, jnp.float32)
    if pieces:
        drawn = drawn * steps_of(stream_key, dims, pieces, -0.22, 0.18)
    return jnp.clip(drawn, -limit, limit).astype(kind)


def setup_inputs(seed: int = 0) -> dict:
    seeds = jax.random.split(jax.random.key(seed), 14)
    x_in = scatter_about(seeds[0], (N_REPLICA, GTOK, D), 1.0, 6.0, ((0, 2), (1, 16)))
    seq_units = jax.vmap(lambda own: uneven(own, N_SHARD, TOK_DEV, UNIT_MAX, 2))(jax.random.split(seeds[1], N_REPLICA)).reshape((N_REPLICA, N_SHARD)).astype(jnp.int32)
    deal = jax.vmap(lambda own: jax.random.permutation(own, N_SHARD))(jax.random.split(seeds[2], N_REPLICA)).reshape((N_REPLICA, N_SHARD)).astype(jnp.int32)
    gain_attn = jnp.clip(1.0 + 0.18 * jax.random.normal(seeds[3], (D,), jnp.float32), 0.1, 1.9)
    w_query = scatter_about(seeds[4], (D, D), (D // 4) ** -0.5, 0.4375, ((0, 16),))
    w_key = scatter_about(seeds[5], (D, D), D ** -0.5, 0.21875, ((0, 16),))
    w_value = scatter_about(seeds[6], (D, D), D ** -0.5, 0.21875, ((0, 16),))
    w_out = scatter_about(seeds[7], (D, D), (D // 16) ** -0.5, 0.875, ((0, 16),))
    gain_ffn = jnp.clip(1.0 + 0.18 * jax.random.normal(seeds[8], (D,), jnp.float32), 0.1, 1.9)
    w_gate = scatter_about(seeds[9], (D, FF), D ** -0.5, 0.21875, ((0, 16),))
    w_up = scatter_about(seeds[10], (D, FF), D ** -0.5, 0.21875, ((0, 16),))
    w_down = scatter_about(seeds[11], (FF, D), FF ** -0.5, 0.125, ((0, 16),))
    d_out = scatter_about(seeds[12], (N_REPLICA, N_SHARD, MAXLEN, D), 1.0, 6.0, ((0, 2), (1, 16)))
    return {"x_in": x_in, "seq_units": seq_units, "deal": deal, "gain_attn": gain_attn, "w_query": w_query, "w_key": w_key, "w_value": w_value, "w_out": w_out, "gain_ffn": gain_ffn, "w_gate": w_gate, "w_up": w_up, "w_down": w_down, "d_out": d_out}


norm_eps = 1e-06
neg_big = -1e+30
highest = lax.Precision.HIGHEST

@jax.custom_vjp
def low(v):
    return lax.optimization_barrier(v.astype(jnp.bfloat16)).astype(jnp.float32)

@jax.custom_vjp
def low_back(v):
    return v

def low_keep(v):
    return (low(v), None)

def low_pass(kept, grad):
    return (grad,)

def back_keep(v):
    return (v, None)

def back_low(kept, grad):
    return (low(grad),)
low.defvjp(low_keep, low_pass)
low_back.defvjp(back_keep, back_low)

def norm_rows(tok_rows, gain_vec):
    return tok_rows * lax.rsqrt(lax.optimization_barrier(jnp.mean(tok_rows * tok_rows, axis=-1, keepdims=True)) + norm_eps) * gain_vec

def mat_mul(lhs_mat, rhs_mat):
    return jnp.dot(lhs_mat, rhs_mat, precision=highest)

def attend(queries, keys_all, values_all, live_keys):
    total_rows = queries.shape[0]
    row_block = min(512, total_rows)
    key_heads = keys_all.reshape(total_rows, H, HD)
    value_heads = values_all.reshape(total_rows, H, HD)

    def one_block(query_block):
        query_heads = query_block.reshape(row_block, H, HD)
        raw_scores = jnp.einsum('qhd,khd->hqk', query_heads, key_heads, precision=highest) * HD ** (-0.5)
        scores = low_back(jnp.where(live_keys[None, None, :], raw_scores, neg_big))
        prob_vals = low(jax.nn.softmax(scores, axis=-1))
        mixed_rows = jnp.einsum('hqk,khd->qhd', prob_vals, value_heads, precision=highest)
        return mixed_rows.reshape(row_block, H * HD)
    blocks_out = lax.map(jax.checkpoint(one_block), queries.reshape(total_rows // row_block, row_block, H * HD))
    return blocks_out.reshape(total_rows, H * HD)

def slot_layer(tok_rows, live_rows, gain_attn, w_query, w_key, w_value, w_out, gain_ffn, w_gate, w_up, w_down):
    normed_one = low(norm_rows(tok_rows, gain_attn))
    queries = low_back(low(mat_mul(normed_one, w_query)))
    keys_all = low_back(low(mat_mul(normed_one, w_key)))
    values_all = low_back(low(mat_mul(normed_one, w_value)))
    mixed_rows = low_back(low(attend(queries, keys_all, values_all, live_rows)))
    attn_part = low_back(mat_mul(mixed_rows, w_out))
    hidden_res = tok_rows + attn_part
    normed_two = low(norm_rows(hidden_res, gain_ffn))
    gate_vals = low_back(mat_mul(normed_two, w_gate))
    up_vals = low_back(mat_mul(normed_two, w_up))
    act_vals = low(jax.nn.gelu(gate_vals, approximate=True) * up_vals)
    ffn_part = low_back(mat_mul(act_vals, w_down))
    return jnp.where(live_rows[:, None], hidden_res + ffn_part, 0.0)

def reference(x_in, seq_units, deal, gain_attn, w_query, w_key, w_value, w_out, gain_ffn, w_gate, w_up, w_down, d_out):
    offsets = jnp.cumsum(seq_units, axis=1) - seq_units
    counts = jnp.take_along_axis(seq_units, deal, axis=1)
    starts = jnp.take_along_axis(offsets, deal, axis=1)
    inner_idx = jnp.arange(UNIT_MAX, dtype=jnp.int32)
    source_idx = jnp.arange(N_SHARD, dtype=jnp.int32)
    row_index = (source_idx[None, None, :, None] * TOK_DEV + starts[:, :, None, None] + jnp.minimum(inner_idx[None, None, None, :], counts[:, :, None, None] - 1)).astype(jnp.int32)
    live_all = jnp.broadcast_to(inner_idx[None, None, None, :] < counts[:, :, None, None], row_index.shape)
    live_all = live_all.reshape(N_REPLICA * N_SHARD, MAXLEN)
    row_index = row_index.reshape(N_REPLICA, N_SHARD * MAXLEN)
    weight_list = (gain_attn.astype(jnp.float32), w_query.astype(jnp.float32), w_key.astype(jnp.float32), w_value.astype(jnp.float32), w_out.astype(jnp.float32), gain_ffn.astype(jnp.float32), w_gate.astype(jnp.float32), w_up.astype(jnp.float32), w_down.astype(jnp.float32))

    def forward(tokens_all, *weight_vals):
        picked = jax.vmap(lambda group_rows, group_index: group_rows[group_index])(tokens_all, row_index)
        picked = jnp.where(live_all.reshape(N_REPLICA, N_SHARD * MAXLEN)[:, :, None], picked, 0.0)
        picked = picked.reshape(N_REPLICA * N_SHARD, MAXLEN, D)

        def step_fn(carry, item):
            return (carry, jax.checkpoint(slot_layer)(item[0], item[1], *weight_vals))
        _, outs_all = lax.scan(step_fn, jnp.float32(0.0), (picked, live_all))
        return outs_all
    result, pullback = jax.vjp(forward, x_in.astype(jnp.float32), *weight_list)
    grads = pullback(d_out.astype(jnp.float32).reshape(N_REPLICA * N_SHARD, MAXLEN, D))
    return (result.reshape(N_REPLICA, N_SHARD, MAXLEN, D).astype(jnp.bfloat16), grads[0].astype(jnp.bfloat16), grads[1], grads[6], grads[2], grads[3], grads[4], grads[5], grads[7], grads[8], grads[9])
```

```python
import functools

import jax
import jax.numpy as jnp
from jax import lax
from jax.experimental import pallas as pl
from jax.experimental.pallas import tpu as pltpu
from jax.sharding import PartitionSpec as P

H = 12
HD = 64
LANES = 256
GAIN_ROWS = 16

norm_eps = 1e-06
neg_big = -1e30
bf16 = jnp.bfloat16
f32 = jnp.float32


def rms_scale(tok_rows, gain_vec):
    inverse = lax.rsqrt(jnp.mean(tok_rows * tok_rows, axis=-1, keepdims=True) + norm_eps)
    return tok_rows * inverse * gain_vec


def gelu_mix(gate_vals, up_vals):
    return jax.nn.gelu(gate_vals, approximate=True) * up_vals


def left_dot(lhs_mat, rhs_mat):
    return lax.dot_general(
        lhs_mat, rhs_mat, (((0,), (0,)), ((), ())), preferred_element_type=jnp.float32
    )


def right_dot(lhs_mat, rhs_mat):
    return lax.dot_general(
        lhs_mat, rhs_mat, (((1,), (1,)), ((), ())), preferred_element_type=jnp.float32
    )


def plain_dot(lhs_mat, rhs_mat):
    return jnp.dot(lhs_mat, rhs_mat, preferred_element_type=jnp.float32)


def slot_start(units_ref, order_ref, slot, shard_count):
    wanted = order_ref[0, slot]
    start = jnp.int32(0)
    count = jnp.int32(0)
    for k in range(shard_count):
        units = units_ref[0, k]
        start = start + jnp.where(k < wanted, units, 0)
        count = count + jnp.where(k == wanted, units, 0)
    return start, count


def deal_kernel(units_ref, order_ref, rows_ref, out_ref):
    shard_count, unit_max, _ = out_ref.shape
    given = rows_ref.shape[0]
    row = lax.broadcasted_iota(jnp.int32, (unit_max, given), 0)
    col = lax.broadcasted_iota(jnp.int32, (unit_max, given), 1)

    def step(slot, carry):
        start, count = slot_start(units_ref, order_ref, slot, shard_count)
        pick = jnp.where((col - start == row) & (row < count), 1.0, 0.0).astype(bf16)
        out_ref[slot] = plain_dot(pick, rows_ref[...]).astype(bf16)
        return carry

    lax.fori_loop(0, shard_count, step, 0)


def undeal_kernel(units_ref, order_ref, back_ref, out_ref, pick_ref):
    shard_count, unit_max, width = back_ref.shape
    given = out_ref.shape[0]
    row = lax.broadcasted_iota(jnp.int32, (unit_max, given), 0)
    col = lax.broadcasted_iota(jnp.int32, (unit_max, given), 1)

    def step(slot, carry):
        start, count = slot_start(units_ref, order_ref, slot, shard_count)
        pick = jnp.where((col - start == row) & (row < count), 1.0, 0.0).astype(bf16)
        pick_ref[pl.ds(pl.multiple_of(slot * unit_max, unit_max), unit_max), :] = pick
        return carry

    lax.fori_loop(0, shard_count, step, 0)
    whole = back_ref[...].reshape(shard_count * unit_max, width)
    out_ref[...] = left_dot(pick_ref[...], whole).astype(bf16)


def smem():
    return pl.BlockSpec(memory_space=pltpu.SMEM)


def vmem():
    return pl.BlockSpec(memory_space=pltpu.VMEM)


def deal_rows(units, order, rows, shard_count, unit_max):
    return pl.pallas_call(
        deal_kernel,
        out_shape=jax.ShapeDtypeStruct((shard_count, unit_max, rows.shape[1]), bf16),
        in_specs=[smem(), smem(), vmem()],
        out_specs=vmem(),
        name="deal_rows",
    )(units, order, rows)


def undeal_rows(units, order, back, given):
    shard_count, unit_max, width = back.shape
    return pl.pallas_call(
        undeal_kernel,
        out_shape=jax.ShapeDtypeStruct((given, width), bf16),
        in_specs=[smem(), smem(), vmem()],
        out_specs=vmem(),
        scratch_shapes=[pltpu.VMEM((shard_count * unit_max, given), bf16)],
        name="undeal_rows",
    )(units, order, back)


def attend_forward(queries, keys_all, values_all, live_keys):
    total_rows = queries.shape[0]
    row_block = min(512, total_rows)
    factor = HD ** (-0.5)
    key_heads = keys_all.reshape(total_rows, H, HD)
    value_heads = values_all.reshape(total_rows, H, HD)
    mixed_list = []
    stat_list = []
    for row_begin in range(0, total_rows, row_block):
        query_heads = queries[row_begin : row_begin + row_block].reshape(row_block, H, HD)
        scores = (
            jnp.einsum("qhd,khd->hqk", query_heads, key_heads, preferred_element_type=jnp.float32)
            * factor
        )
        scores = jnp.where(live_keys[None, None, :], scores, neg_big)
        row_max = jnp.max(scores, axis=-1, keepdims=True)
        exp_vals = jnp.exp(scores - row_max)
        row_total = jnp.sum(exp_vals, axis=-1, keepdims=True)
        prob_vals = (exp_vals / row_total).astype(jnp.bfloat16)
        mixed_rows = jnp.einsum(
            "hqk,khd->qhd", prob_vals, value_heads, preferred_element_type=jnp.float32
        )
        mixed_list.append(mixed_rows.reshape(row_block, H * HD))
        stat_list.append(row_max + jnp.log(row_total))
    return (jnp.concatenate(mixed_list, axis=0), jnp.concatenate(stat_list, axis=1))


def attend_backward(queries, keys_all, values_all, live_keys, log_totals, grad_mixed):
    total_rows = queries.shape[0]
    row_block = min(512, total_rows)
    factor = HD ** (-0.5)
    key_heads = keys_all.reshape(total_rows, H, HD)
    value_heads = values_all.reshape(total_rows, H, HD)
    grad_keys = jnp.zeros((total_rows, H, HD), jnp.float32)
    grad_values = jnp.zeros((total_rows, H, HD), jnp.float32)
    query_list = []
    for row_begin in range(0, total_rows, row_block):
        query_heads = queries[row_begin : row_begin + row_block].reshape(row_block, H, HD)
        grad_heads = grad_mixed[row_begin : row_begin + row_block].reshape(row_block, H, HD)
        scores = (
            jnp.einsum("qhd,khd->hqk", query_heads, key_heads, preferred_element_type=jnp.float32)
            * factor
        )
        scores = jnp.where(live_keys[None, None, :], scores, neg_big)
        prob_vals = jnp.exp(scores - log_totals[:, row_begin : row_begin + row_block])
        grad_probs = jnp.einsum(
            "qhd,khd->hqk", grad_heads, value_heads, preferred_element_type=jnp.float32
        )
        row_dot = jnp.sum(prob_vals * grad_probs, axis=-1, keepdims=True)
        grad_scores = (prob_vals * (grad_probs - row_dot)).astype(jnp.bfloat16)
        grad_query = (
            jnp.einsum("hqk,khd->qhd", grad_scores, key_heads, preferred_element_type=jnp.float32)
            * factor
        )
        query_list.append(grad_query.reshape(row_block, H * HD))
        grad_keys = (
            grad_keys
            + jnp.einsum(
                "hqk,qhd->khd", grad_scores, query_heads, preferred_element_type=jnp.float32
            )
            * factor
        )
        grad_values = grad_values + jnp.einsum(
            "hqk,qhd->khd",
            prob_vals.astype(jnp.bfloat16),
            grad_heads,
            preferred_element_type=jnp.float32,
        )
    return (
        jnp.concatenate(query_list, axis=0),
        grad_keys.reshape(total_rows, H * HD),
        grad_values.reshape(total_rows, H * HD),
    )


def to_blocks(mat, parts):
    rows = mat.shape[0] // parts
    cols = mat.shape[1] // LANES
    split = mat.reshape(parts, rows, cols, LANES).transpose(0, 2, 1, 3)
    return split.reshape(parts, cols * rows, LANES)


def from_blocks(packed, rows):
    parts, total, _ = packed.shape
    cols = total // rows
    split = packed.reshape(parts, cols, rows, LANES).transpose(0, 2, 1, 3)
    return split.reshape(parts * rows, cols * LANES)


def gather_packed(mats):
    packed = jnp.concatenate([to_blocks(m, 1)[0] for m in mats], axis=0)
    count = lax.axis_size("shard")
    whole = lax.all_gather(packed, "shard", axis=0, tiled=True)
    whole = whole.reshape(count, packed.shape[0], LANES)
    out = []
    begin = 0
    for m in mats:
        size = m.shape[0] * (m.shape[1] // LANES)
        out.append(from_blocks(whole[:, begin : begin + size], m.shape[0]))
        begin += size
    return out


def replica_sum(part):
    count = lax.axis_size("replica")
    step = 1
    while step < count:
        other = lax.ppermute(part, "replica", [(i, i ^ step) for i in range(count)])
        part = (part.astype(f32) + other.astype(f32)).astype(bf16)
        step *= 2
    return part


def scatter_packed(mats, gain):
    count = lax.axis_size("shard")
    own = gain.shape[0] // count
    gain_rows = jnp.pad(
        gain.astype(bf16).reshape(count, 1, own), ((0, 0), (0, GAIN_ROWS - 1), (0, LANES - own))
    )
    packed = jnp.concatenate([to_blocks(m.astype(bf16), count) for m in mats] + [gain_rows], axis=1)
    flat = packed.reshape(-1, LANES)
    share = lax.psum_scatter(flat, "shard", scatter_dimension=0, tiled=True)
    total = replica_sum(share).astype(f32)
    out = []
    begin = 0
    for m in mats:
        rows = m.shape[0] // count
        size = rows * (m.shape[1] // LANES)
        out.append(from_blocks(total[None, begin : begin + size], rows))
        begin += size
    out.append(total[begin, :own])
    return out


def shards(
    x_in,
    seq_units,
    deal,
    gain_attn,
    w_query,
    w_key,
    w_value,
    w_out,
    gain_ffn,
    w_gate,
    w_up,
    w_down,
    d_out,
):
    shard_count = lax.axis_size("shard")
    my_index = lax.axis_index("shard")
    given, width = x_in.shape[1:]
    span = d_out.shape[2]
    unit_max = span // shard_count
    units_row = seq_units[0]
    order_row = deal[0]
    slot_ids = jnp.arange(shard_count, dtype=jnp.int32)
    inner_idx = jnp.arange(unit_max, dtype=jnp.int32)
    outgoing = deal_rows(seq_units, deal, x_in[0], shard_count, unit_max)
    arrived = lax.all_to_all(outgoing, "shard", split_axis=0, concat_axis=0, tiled=True)
    own_seq = jnp.sum(jnp.where(slot_ids == my_index, order_row, 0))
    own_count = jnp.sum(jnp.where(slot_ids == own_seq, units_row, 0))
    live_rows = jnp.broadcast_to(inner_idx[None, :] < own_count, (shard_count, unit_max)).reshape(
        span
    )
    wq_full, wk_full, wv_full, wo_full = gather_packed((w_query, w_key, w_value, w_out))
    wg_full, wu_full, wd_full = gather_packed((w_gate, w_up, w_down))
    tok_float = arrived.reshape(span, width).astype(jnp.float32)
    normed_one_f, norm_one_back = jax.vjp(rms_scale, tok_float, gain_attn)
    normed_one = normed_one_f.astype(jnp.bfloat16)
    queries = plain_dot(normed_one, wq_full).astype(jnp.bfloat16)
    keys_all = plain_dot(normed_one, wk_full).astype(jnp.bfloat16)
    values_all = plain_dot(normed_one, wv_full).astype(jnp.bfloat16)
    mixed_f, log_totals = attend_forward(queries, keys_all, values_all, live_rows)
    mixed_rows = mixed_f.astype(jnp.bfloat16)
    hidden_res = tok_float + plain_dot(mixed_rows, wo_full)
    normed_two_f, norm_two_back = jax.vjp(rms_scale, hidden_res, gain_ffn)
    normed_two = normed_two_f.astype(jnp.bfloat16)
    gate_vals = plain_dot(normed_two, wg_full)
    up_vals = plain_dot(normed_two, wu_full)
    act_f, mix_back = jax.vjp(gelu_mix, gate_vals, up_vals)
    act_vals = act_f.astype(jnp.bfloat16)
    result = jnp.where(live_rows[:, None], hidden_res + plain_dot(act_vals, wd_full), 0.0)
    layer_out = result.astype(jnp.bfloat16).reshape(1, 1, span, width)
    grad_y = jnp.where(live_rows[:, None], d_out[0, 0].astype(jnp.float32), 0.0)
    grad_ffn_b = grad_y.astype(jnp.bfloat16)
    grad_down = left_dot(act_vals, grad_ffn_b)
    grad_act = right_dot(grad_ffn_b, wd_full)
    grad_gate_f, grad_up_f = mix_back(grad_act)
    grad_gate_b = grad_gate_f.astype(jnp.bfloat16)
    grad_up_b = grad_up_f.astype(jnp.bfloat16)
    grad_wg = left_dot(normed_two, grad_gate_b)
    grad_wu = left_dot(normed_two, grad_up_b)
    grad_n2 = right_dot(grad_gate_b, wg_full) + right_dot(grad_up_b, wu_full)
    grad_h_norm, grad_gain_two = norm_two_back(grad_n2)
    out_wg, out_wu, out_wd, out_gain_two = scatter_packed((grad_wg, grad_wu, grad_down), grad_gain_two)
    grad_hidden = grad_y + grad_h_norm
    grad_attn_b = grad_hidden.astype(jnp.bfloat16)
    grad_wo = left_dot(mixed_rows, grad_attn_b)
    grad_mixed = right_dot(grad_attn_b, wo_full).astype(jnp.bfloat16)
    grad_q_f, grad_k_f, grad_v_f = attend_backward(
        queries, keys_all, values_all, live_rows, log_totals, grad_mixed
    )
    grad_q_b = grad_q_f.astype(jnp.bfloat16)
    grad_k_b = grad_k_f.astype(jnp.bfloat16)
    grad_v_b = grad_v_f.astype(jnp.bfloat16)
    grad_wq = left_dot(normed_one, grad_q_b)
    grad_wk = left_dot(normed_one, grad_k_b)
    grad_wv = left_dot(normed_one, grad_v_b)
    grad_n1 = (
        right_dot(grad_q_b, wq_full) + right_dot(grad_k_b, wk_full) + right_dot(grad_v_b, wv_full)
    )
    grad_x_norm, grad_gain_one = norm_one_back(grad_n1)
    grad_tokens = (
        (grad_hidden + grad_x_norm).astype(jnp.bfloat16).reshape(shard_count, unit_max, width)
    )
    returned = lax.all_to_all(grad_tokens, "shard", split_axis=0, concat_axis=0, tiled=True)
    grad_x = undeal_rows(seq_units, deal, returned, given)[None]
    out_wq, out_wk, out_wv, out_wo, out_gain_one = scatter_packed(
        (grad_wq, grad_wk, grad_wv, grad_wo), grad_gain_one
    )
    return (
        layer_out,
        grad_x,
        out_gain_one,
        out_gain_two,
        out_wq,
        out_wk,
        out_wv,
        out_wo,
        out_wg,
        out_wu,
        out_wd,
    )


def solution(mesh):
    return jax.shard_map(
        shards,
        mesh=mesh,
        in_specs=(
            P("replica", "shard", None),
            P("replica", None),
            P("replica", None),
            P(),
            P("shard", None),
            P("shard", None),
            P("shard", None),
            P("shard", None),
            P(),
            P("shard", None),
            P("shard", None),
            P("shard", None),
            P("replica", "shard", None, None),
        ),
        out_specs=(
            P("replica", "shard", None, None),
            P("replica", "shard", None),
            P("shard"),
            P("shard"),
            P("shard", None),
            P("shard", None),
            P("shard", None),
            P("shard", None),
            P("shard", None),
            P("shard", None),
            P("shard", None),
        ),
        check_vma=False,
    )
```

```python
import functools

import jax
import jax.numpy as jnp
from jax import lax
from jax.experimental import pallas as pl
from jax.experimental.pallas import tpu as pltpu
from jax.sharding import PartitionSpec as P

H = 12
HD = 64
LANES = 256
GAIN_ROWS = 16

norm_eps = 1e-06
neg_big = -1e30
bf16 = jnp.bfloat16
f32 = jnp.float32


def left_dot(lhs_mat, rhs_mat):
    return lax.dot_general(
        lhs_mat, rhs_mat, (((0,), (0,)), ((), ())), preferred_element_type=jnp.float32
    )


def right_dot(lhs_mat, rhs_mat):
    return lax.dot_general(
        lhs_mat, rhs_mat, (((1,), (1,)), ((), ())), preferred_element_type=jnp.float32
    )


def plain_dot(lhs_mat, rhs_mat):
    return jnp.dot(lhs_mat, rhs_mat, preferred_element_type=jnp.float32)


def slot_start(units_ref, order_ref, slot, shard_count):
    wanted = order_ref[0, slot]
    start = jnp.int32(0)
    count = jnp.int32(0)
    for k in range(shard_count):
        units = units_ref[0, k]
        start = start + jnp.where(k < wanted, units, 0)
        count = count + jnp.where(k == wanted, units, 0)
    return start, count


def deal_kernel(units_ref, order_ref, rows_ref, out_ref):
    shard_count, unit_max, _ = out_ref.shape
    given = rows_ref.shape[0]
    row = lax.broadcasted_iota(jnp.int32, (unit_max, given), 0)
    col = lax.broadcasted_iota(jnp.int32, (unit_max, given), 1)

    def step(slot, carry):
        start, count = slot_start(units_ref, order_ref, slot, shard_count)
        pick = jnp.where((col - start == row) & (row < count), 1.0, 0.0).astype(bf16)
        out_ref[slot] = plain_dot(pick, rows_ref[...]).astype(bf16)
        return carry

    lax.fori_loop(0, shard_count, step, 0)


def undeal_kernel(units_ref, order_ref, back_ref, out_ref, pick_ref):
    shard_count, unit_max, width = back_ref.shape
    given = out_ref.shape[0]
    row = lax.broadcasted_iota(jnp.int32, (unit_max, given), 0)
    col = lax.broadcasted_iota(jnp.int32, (unit_max, given), 1)

    def step(slot, carry):
        start, count = slot_start(units_ref, order_ref, slot, shard_count)
        pick = jnp.where((col - start == row) & (row < count), 1.0, 0.0).astype(bf16)
        pick_ref[pl.ds(pl.multiple_of(slot * unit_max, unit_max), unit_max), :] = pick
        return carry

    lax.fori_loop(0, shard_count, step, 0)
    whole = back_ref[...].reshape(shard_count * unit_max, width)
    out_ref[...] = left_dot(pick_ref[...], whole).astype(bf16)


def smem():
    return pl.BlockSpec(memory_space=pltpu.SMEM)


def vmem():
    return pl.BlockSpec(memory_space=pltpu.VMEM)


def deal_rows(units, order, rows, shard_count, unit_max):
    return pl.pallas_call(
        deal_kernel,
        out_shape=jax.ShapeDtypeStruct((shard_count, unit_max, rows.shape[1]), bf16),
        in_specs=[smem(), smem(), vmem()],
        out_specs=vmem(),
        name="deal_rows",
    )(units, order, rows)


def undeal_rows(units, order, back, given):
    shard_count, unit_max, width = back.shape
    return pl.pallas_call(
        undeal_kernel,
        out_shape=jax.ShapeDtypeStruct((given, width), bf16),
        in_specs=[smem(), smem(), vmem()],
        out_specs=vmem(),
        scratch_shapes=[pltpu.VMEM((shard_count * unit_max, given), bf16)],
        name="undeal_rows",
    )(units, order, back)


def const_block(shape):
    zeros = (0,) * len(shape)
    return pl.BlockSpec(shape, lambda *_: zeros)


def params():
    return pltpu.CompilerParams(vmem_limit_bytes=60 << 20)


def cost(flops, moved, trans=0):
    return pl.CostEstimate(flops=flops, bytes_accessed=moved, transcendentals=trans)


def inverse_rms(rows):
    return lax.rsqrt(jnp.mean(rows * rows, axis=-1, keepdims=True) + norm_eps)


def whole_block(ref):
    parts, rows, lanes = ref.shape
    return ref[...].reshape(parts * rows, lanes)


def qkv_kernel(x_ref, gain_ref, w_ref, n1_ref, qkv_ref):
    block = pl.program_id(0)

    @pl.when(block == 0)
    def _():
        rows = x_ref[...].astype(f32)
        n1_ref[...] = (rows * inverse_rms(rows) * gain_ref[...]).astype(bf16)

    factor = jnp.where(block < n1_ref.shape[1] // LANES, HD ** (-0.5), 1.0)
    made = plain_dot(n1_ref[...], whole_block(w_ref)).astype(bf16).astype(f32)
    qkv_ref[...] = (made * factor).astype(bf16)


def make_qkv(tokens, gain, packed, rows):
    span, width = tokens.shape
    parts = packed.shape[0]
    blocks = 3 * width // LANES
    return pl.pallas_call(
        qkv_kernel,
        grid=(blocks,),
        out_shape=(
            jax.ShapeDtypeStruct((span, width), bf16),
            jax.ShapeDtypeStruct((span, 3 * width), bf16),
        ),
        in_specs=[
            const_block((span, width)),
            const_block((1, width)),
            pl.BlockSpec((parts, rows, LANES), lambda j: (0, j, 0)),
        ],
        out_specs=(
            const_block((span, width)),
            pl.BlockSpec((span, LANES), lambda j: (0, j)),
        ),
        compiler_params=params(),
        cost_estimate=cost(6 * span * width * width, 14 << 20),
        name="make_qkv",
    )(tokens, gain, packed)


def live_bias(count, span, unit_max):
    row = lax.broadcasted_iota(jnp.int32, (span, 2 * HD), 0)
    return jnp.where(lax.rem(row, unit_max) < count, 0.0, neg_big).astype(bf16)


def head_keys(keys, bias, lane, head):
    inside = (lane // HD) == head
    return jnp.where(inside, keys, jnp.where(lane == (1 - head) * HD, bias, jnp.zeros_like(keys)))


def head_queries(queries, lane, head):
    inside = (lane // HD) == head
    one = jnp.where(lane == (1 - head) * HD, 1.0, 0.0).astype(bf16)
    return jnp.where(inside, queries, one)


def attend_kernel(unit_max, chunk, count_ref, q_ref, k_ref, v_ref, o_ref, lse_ref, kb_ref, vt_ref):
    span = q_ref.shape[0]
    pair = 2 * HD
    lane = lax.broadcasted_iota(jnp.int32, (span, pair), 1)
    bias = live_bias(count_ref[0], span, unit_max)
    keys = k_ref[...]
    values_t = v_ref[...].T
    for head in range(2):
        kb_ref[head] = head_keys(keys, bias, lane, head)
        vt_ref[head, :HD] = values_t[head * HD : (head + 1) * HD]
        vt_ref[head, HD:] = jnp.ones((vt_ref.shape[1] - HD, span), bf16)
    lane_c = lane[:chunk]
    for begin in range(0, span, chunk):
        queries = q_ref[begin : begin + chunk, :]
        mixed = []
        for head in range(2):
            scores = right_dot(kb_ref[head], head_queries(queries, lane_c, head))
            top = jnp.max(scores, axis=0, keepdims=True)
            probs = jnp.exp(scores - top).astype(bf16)
            both = plain_dot(vt_ref[head], probs)
            total = both[HD : HD + 1]
            mixed.append(both[:HD] * (1.0 / total))
            lse_ref[0, head : head + 1, begin : begin + chunk] = top + jnp.log(total)
        o_ref[begin : begin + chunk, :] = jnp.concatenate(mixed, axis=0).T.astype(bf16)


def attend_forward(count, qkv, unit_max):
    span = qkv.shape[0]
    width = qkv.shape[1] // 3
    pair = 2 * HD
    pairs = width // pair

    def block(first):
        return pl.BlockSpec((span, pair), lambda p: (0, first + p))

    return pl.pallas_call(
        functools.partial(attend_kernel, unit_max, 512),
        grid=(pairs,),
        out_shape=(
            jax.ShapeDtypeStruct((span, width), bf16),
            jax.ShapeDtypeStruct((pairs, 8, span), f32),
        ),
        in_specs=[smem(), block(0), block(pairs), block(2 * pairs)],
        out_specs=(block(0), pl.BlockSpec((1, 8, span), lambda p: (p, 0, 0))),
        scratch_shapes=[
            pltpu.VMEM((2, span, pair), bf16),
            pltpu.VMEM((2, HD + 16, span), bf16),
        ],
        compiler_params=params(),
        cost_estimate=cost(4 * span * span * width, 8 << 20, span * span * H),
        name="attend_forward",
    )(count, qkv, qkv, qkv)


def out_kernel(x_ref, o_ref, w_ref, gain_ref, h_ref, n2_ref):
    parts, total, lanes = w_ref.shape
    width = h_ref.shape[1]
    rows = width // parts
    for c in range(width // lanes):
        weight = w_ref[:, c * rows : (c + 1) * rows, :].reshape(width, lanes)
        cols = slice(c * lanes, (c + 1) * lanes)
        h_ref[:, cols] = x_ref[:, cols].astype(f32) + plain_dot(o_ref[...], weight)
    hidden = h_ref[...]
    n2_ref[...] = (hidden * inverse_rms(hidden) * gain_ref[...]).astype(bf16)


def out_project(tokens, mixed, packed, gain, rows):
    span, width = tokens.shape
    parts = packed.shape[0]
    blocks = width // LANES
    return pl.pallas_call(
        out_kernel,
        grid=(1,),
        out_shape=(
            jax.ShapeDtypeStruct((span, width), f32),
            jax.ShapeDtypeStruct((span, width), bf16),
        ),
        in_specs=[
            const_block((span, width)),
            const_block((span, width)),
            pl.BlockSpec((parts, blocks * rows, LANES), lambda i: (0, 3, 0)),
            const_block((1, width)),
        ],
        out_specs=(const_block((span, width)), const_block((span, width))),
        compiler_params=params(),
        cost_estimate=cost(2 * span * width * width, 9 << 20),
        name="out_project",
    )(tokens, mixed, packed, gain)


def spread_gain(total, parts):
    width = total.shape[1]
    own = width // parts
    shape = (parts, GAIN_ROWS, LANES)
    part = lax.broadcasted_iota(jnp.int32, shape, 0)
    row = lax.broadcasted_iota(jnp.int32, shape, 1)
    place = row * LANES + lax.broadcasted_iota(jnp.int32, shape, 2)
    mine = (place >= part * own) & (place < (part + 1) * own)
    out = jnp.zeros(shape, f32)
    for c in range(width // LANES):
        piece = jnp.broadcast_to(total[:, c * LANES : (c + 1) * LANES][None], shape)
        out = jnp.where((row == c) & mine, piece, out)
    return out.astype(bf16)


def ffn_kernel(
    unit_max,
    count_ref,
    h_ref,
    n2_ref,
    d_ref,
    gain_ref,
    wg_ref,
    wu_ref,
    wd_ref,
    out_ref,
    gh_ref,
    ghb_ref,
    pack_ref,
    gb_ref,
    y_ref,
    gn_ref,
    stage_gate,
    stage_up,
    stage_down,
    stage_gain,
    sems,
):
    step = pl.program_id(0)
    steps = pl.num_programs(0)
    slot = lax.rem(step, 2)
    span, width = h_ref.shape
    parts, rows, _ = wg_ref.shape
    few, down_all, _ = wd_ref.shape
    cols = width // LANES
    down = down_all // cols
    ff_blocks = steps

    def copies(which, at):
        return (
            pltpu.make_async_copy(
                stage_gate.at[at],
                pack_ref.at[:, pl.ds(pl.multiple_of(which * rows, 8), rows), :],
                sems.at[0, at],
            ),
            pltpu.make_async_copy(
                stage_up.at[at],
                pack_ref.at[:, pl.ds(pl.multiple_of((ff_blocks + which) * rows, 8), rows), :],
                sems.at[1, at],
            ),
            pltpu.make_async_copy(
                stage_down.at[at],
                pack_ref.at[pl.ds(which * few, few), pl.ds(2 * ff_blocks * rows, down_all), :],
                sems.at[2, at],
            ),
        )

    row = lax.broadcasted_iota(jnp.int32, (span, 1), 0)
    live = lax.rem(row, unit_max) < count_ref[0]

    @pl.when(step == 0)
    def _():
        gb_ref[...] = jnp.where(live, d_ref[...].astype(f32), 0.0).astype(bf16)

    @pl.when(step >= 2)
    def _():
        for copy in copies(step - 2, slot):
            copy.wait()

    n2 = n2_ref[...]
    gb = gb_ref[...]
    w_gate = whole_block(wg_ref)
    w_up = whole_block(wu_ref)
    gate = plain_dot(n2, w_gate)
    up = plain_dot(n2, w_up)
    downs = [
        wd_ref[:, c * down : (c + 1) * down, :].reshape(few * down, LANES) for c in range(cols)
    ]
    g_act = right_dot(gb[:, :LANES], downs[0])
    for c in range(1, cols):
        g_act += right_dot(gb[:, c * LANES : (c + 1) * LANES], downs[c])
    c0 = 0.7978845608028654
    c1 = 0.044715
    square = gate * gate
    tang = jnp.tanh(c0 * gate * (1.0 + c1 * square))
    half = 0.5 * (1.0 + tang)
    gelu = gate * half
    slope = half + (0.5 * c0) * gate * (1.0 - tang * tang) * (1.0 + (3.0 * c1) * square)
    act = (gelu * up).astype(bf16)
    g_gate = (g_act * up * slope).astype(bf16)
    g_up = (g_act * gelu).astype(bf16)
    for c in range(cols):
        place = slice(c * LANES, (c + 1) * LANES)
        add = plain_dot(act, downs[c])
        grad = right_dot(g_gate, w_gate[place]) + right_dot(g_up, w_up[place])
        wide = left_dot(act, gb[:, place]).astype(bf16).reshape(few, down, LANES)
        stage_down[slot, :, c * down : (c + 1) * down, :] = wide

        @pl.when(step == 0)
        def _():
            y_ref[:, place] = add
            gn_ref[:, place] = grad

        @pl.when(step > 0)
        def _():
            y_ref[:, place] += add
            gn_ref[:, place] += grad

    stage_gate[slot] = left_dot(n2, g_gate).astype(bf16).reshape(parts, rows, LANES)
    stage_up[slot] = left_dot(n2, g_up).astype(bf16).reshape(parts, rows, LANES)
    for copy in copies(step, slot):
        copy.start()

    @pl.when(step == steps - 1)
    def _():
        hidden = h_ref[...]
        out_ref[...] = jnp.where(live, hidden + y_ref[...], 0.0).astype(bf16)
        inv = inverse_rms(hidden)
        grad = gn_ref[...]
        scaled = hidden * inv
        total = jnp.sum(grad * scaled, axis=0, keepdims=True)
        stage_gain[...] = spread_gain(total, parts)
        last = pltpu.make_async_copy(
            stage_gain,
            pack_ref.at[:, pl.ds(2 * ff_blocks * rows + down_all, GAIN_ROWS), :],
            sems.at[3, 0],
        )
        last.start()
        weighted = grad * gain_ref[...]
        mean = jnp.mean(scaled * weighted, axis=-1, keepdims=True)
        g_h = gb_ref[...].astype(f32) + inv * (weighted - scaled * mean)
        gh_ref[...] = g_h
        ghb_ref[...] = g_h.astype(bf16)
        for copy in copies(step - 1, 1 - slot) + copies(step, slot):
            copy.wait()
        last.wait()


def ffn_both(count, hidden, normed, d_rows, gain, packed, unit_max, rows, down):
    span, width = hidden.shape
    parts = packed.shape[0]
    ff = parts * down
    blocks = ff // LANES
    cols = width // LANES
    few = LANES // down
    moved = 2 * blocks * rows + cols * down
    full = const_block((span, width))
    return pl.pallas_call(
        functools.partial(ffn_kernel, unit_max),
        grid=(blocks,),
        out_shape=(
            jax.ShapeDtypeStruct((span, width), bf16),
            jax.ShapeDtypeStruct((span, width), f32),
            jax.ShapeDtypeStruct((span, width), bf16),
            jax.ShapeDtypeStruct((parts, moved + GAIN_ROWS, LANES), bf16),
        ),
        in_specs=[
            smem(),
            full,
            full,
            full,
            const_block((1, width)),
            pl.BlockSpec((parts, rows, LANES), lambda j: (0, j, 0)),
            pl.BlockSpec((parts, rows, LANES), lambda j: (0, blocks + j, 0)),
            pl.BlockSpec((few, cols * down, LANES), lambda j: (j, 2 * blocks * rows // (cols * down), 0)),
        ],
        out_specs=(full, full, full, pl.BlockSpec(memory_space=pl.ANY)),
        scratch_shapes=[
            pltpu.VMEM((span, width), bf16),
            pltpu.VMEM((span, width), f32),
            pltpu.VMEM((span, width), f32),
            pltpu.VMEM((2, parts, rows, LANES), bf16),
            pltpu.VMEM((2, parts, rows, LANES), bf16),
            pltpu.VMEM((2, few, cols * down, LANES), bf16),
            pltpu.VMEM((parts, GAIN_ROWS, LANES), bf16),
            pltpu.SemaphoreType.DMA((4, 2)),
        ],
        compiler_params=params(),
        cost_estimate=cost(18 * span * width * ff, 36 << 20, span * ff),
        name="ffn_both",
    )(count, hidden, normed, d_rows, gain, packed, packed, packed)


def attend_back_kernel(
    unit_max,
    chunk,
    count_ref,
    q_ref,
    k_ref,
    v_ref,
    o_ref,
    lse_ref,
    n1_ref,
    x_ref,
    gh_ref,
    ghb_ref,
    gain_ref,
    wq_ref,
    wk_ref,
    wv_ref,
    wo_ref,
    gx_ref,
    pack_ref,
    wo_s,
    do_s,
    delta_s,
    kt_s,
    dqt_s,
    dk_s,
    dv_s,
    gn_s,
    stage,
    stage_gain,
    sems,
    gain_sem,
):
    step = pl.program_id(0)
    steps = pl.num_programs(0)
    span, width = x_ref.shape
    parts, rows, _ = wq_ref.shape
    cols = width // LANES
    pair = 2 * HD
    heads = LANES // HD
    lane = lax.broadcasted_iota(jnp.int32, (span, pair), 1)
    lane_c = lane[:chunk]
    mine = pl.ds(pl.multiple_of(step * LANES, LANES), LANES)

    def copies(which):
        return [
            pltpu.make_async_copy(
                stage.at[m],
                pack_ref.at[:, pl.ds(pl.multiple_of((m * cols + which) * rows, 8), rows), :],
                sems.at[m],
            )
            for m in range(4)
        ]

    @pl.when(step == 0)
    def _():
        for c in range(cols):
            wo_s[c] = wo_ref[:, c * rows : (c + 1) * rows, :].reshape(width, LANES)

    g_o = right_dot(ghb_ref[:, :LANES], wo_s[0, mine, :])
    for c in range(1, cols):
        g_o += right_dot(ghb_ref[:, c * LANES : (c + 1) * LANES], wo_s[c, mine, :])
    g_o = g_o.astype(bf16)
    do_s[...] = g_o
    prod = g_o.astype(f32) * o_ref[:, mine].astype(f32)
    high = prod.astype(bf16)
    low = (prod - high.astype(f32)).astype(bf16)
    picker = jnp.where(
        lax.broadcasted_iota(jnp.int32, (8, LANES), 1) // HD
        == lax.broadcasted_iota(jnp.int32, (8, LANES), 0),
        1.0,
        0.0,
    ).astype(bf16)
    delta_s[...] = right_dot(picker, high) + right_dot(picker, low)
    kt_s[...] = k_ref[...].T
    dk_s[...] = jnp.zeros_like(dk_s)
    dv_s[...] = jnp.zeros_like(dv_s)
    bias = live_bias(count_ref[0], span, unit_max)

    def one_head(head, carry):
        half = head // 2
        sub = lax.rem(head, 2)
        side = pl.ds(pl.multiple_of(half * pair, pair), pair)
        inside = (lane // HD) == sub
        inside_c = (lane_c // HD) == sub
        zero = jnp.zeros((), bf16)
        keys = head_keys(k_ref[:, side], bias, lane, sub)
        values = jnp.where(inside, v_ref[:, side], zero)
        keys_t = kt_s[pl.ds(pl.multiple_of(head * HD, HD), HD), :]
        d_k = None
        d_v = None
        for begin in range(0, span, chunk):
            part = slice(begin, begin + chunk)
            queries = q_ref[part, side]
            grads = do_s[part, side]
            scores = right_dot(keys, head_queries(queries, lane_c, sub))
            probs = jnp.exp(scores - lse_ref[half, pl.ds(sub, 1), part])
            d_probs = right_dot(values, grads)
            d_scores = (probs * (d_probs - delta_s[pl.ds(head, 1), part])).astype(bf16)
            add_v = plain_dot(probs.astype(bf16), jnp.where(inside_c, grads, zero))
            add_k = plain_dot(d_scores, jnp.where(inside_c, queries, zero))
            d_v = add_v if d_v is None else d_v + add_v
            d_k = add_k if d_k is None else d_k + add_k
            dqt_s[pl.ds(pl.multiple_of(head * HD, HD), HD), part] = plain_dot(keys_t, d_scores)
        dk_s[:, side] += d_k
        dv_s[:, side] += d_v
        return carry

    lax.fori_loop(0, heads, one_head, 0)
    d_q = (dqt_s[...].T * (HD ** (-0.5))).astype(bf16)
    d_k = dk_s[...].astype(bf16)
    d_v = dv_s[...].astype(bf16)

    add = (
        right_dot(d_q, whole_block(wq_ref))
        + right_dot(d_k, whole_block(wk_ref))
        + right_dot(d_v, whole_block(wv_ref))
    )

    @pl.when(step == 0)
    def _():
        gn_s[...] = add

    @pl.when(step > 0)
    def _():
        gn_s[...] += add
        for copy in copies(step - 1):
            copy.wait()

    n1 = n1_ref[...]
    for m, grad in enumerate((d_q, d_k, d_v)):
        stage[m] = left_dot(n1, grad).astype(bf16).reshape(parts, rows, LANES)
    stage[3] = left_dot(o_ref[...], ghb_ref[:, mine]).astype(bf16).reshape(parts, rows, LANES)
    for copy in copies(step):
        copy.start()

    @pl.when(step == steps - 1)
    def _():
        tokens = x_ref[...].astype(f32)
        inv = inverse_rms(tokens)
        grad = gn_s[...]
        scaled = tokens * inv
        total = jnp.sum(grad * scaled, axis=0, keepdims=True)
        stage_gain[...] = spread_gain(total, parts)
        last = pltpu.make_async_copy(
            stage_gain, pack_ref.at[:, pl.ds(4 * cols * rows, GAIN_ROWS), :], gain_sem.at[0]
        )
        last.start()
        weighted = grad * gain_ref[...]
        mean = jnp.mean(scaled * weighted, axis=-1, keepdims=True)
        gx_ref[...] = (gh_ref[...] + inv * (weighted - scaled * mean)).astype(bf16)
        for copy in copies(step):
            copy.wait()
        last.wait()


def attend_back(count, qkv, mixed, lse, n1, tokens, g_h, g_hb, gain, packed, unit_max, rows):
    span, width = tokens.shape
    parts = packed.shape[0]
    cols = width // LANES
    full = const_block((span, width))

    def block(first):
        return pl.BlockSpec((span, LANES), lambda p: (0, first + p))

    def weight(first):
        return pl.BlockSpec((parts, rows, LANES), lambda p: (0, first + p, 0))

    return pl.pallas_call(
        functools.partial(attend_back_kernel, unit_max, 512),
        grid=(cols,),
        out_shape=(
            jax.ShapeDtypeStruct((span, width), bf16),
            jax.ShapeDtypeStruct((parts, 4 * cols * rows + GAIN_ROWS, LANES), bf16),
        ),
        in_specs=[
            smem(),
            block(0),
            block(cols),
            block(2 * cols),
            full,
            pl.BlockSpec((2, 8, span), lambda p: (p, 0, 0)),
            full,
            full,
            full,
            full,
            const_block((1, width)),
            weight(0),
            weight(cols),
            weight(2 * cols),
            pl.BlockSpec((parts, cols * rows, LANES), lambda p: (0, 3, 0)),
        ],
        out_specs=(full, pl.BlockSpec(memory_space=pl.ANY)),
        scratch_shapes=[
            pltpu.VMEM((cols, width, LANES), bf16),
            pltpu.VMEM((span, LANES), bf16),
            pltpu.VMEM((8, span), f32),
            pltpu.VMEM((LANES, span), bf16),
            pltpu.VMEM((LANES, span), f32),
            pltpu.VMEM((span, LANES), f32),
            pltpu.VMEM((span, LANES), f32),
            pltpu.VMEM((span, width), f32),
            pltpu.VMEM((4, parts, rows, LANES), bf16),
            pltpu.VMEM((parts, GAIN_ROWS, LANES), bf16),
            pltpu.SemaphoreType.DMA((4,)),
            pltpu.SemaphoreType.DMA((1,)),
        ],
        compiler_params=params(),
        cost_estimate=cost(10 * span * span * width + 16 * span * width * width, 24 << 20, span * span * H),
        name="attend_back",
    )(count, qkv, qkv, qkv, mixed, lse, n1, tokens, g_h, g_hb, gain, packed, packed, packed, packed)


def finish_kernel(layout, own, gain_cols, me_ref, mine_ref, other_ref, *outs):
    begin = 0
    for (rows, blocks), out_ref in zip(layout, outs[:-1]):
        for c in range(blocks):
            at = slice(begin, begin + rows)
            out_ref[:, c * LANES : (c + 1) * LANES] = mine_ref[at].astype(f32) + other_ref[at].astype(f32)
            begin += rows
    at = slice(begin, begin + GAIN_ROWS)
    row = lax.broadcasted_iota(jnp.int32, (GAIN_ROWS, own), 0)
    from_lane = lax.broadcasted_iota(jnp.int32, (LANES, own), 0)
    to_lane = lax.broadcasted_iota(jnp.int32, (LANES, own), 1)
    total = jnp.zeros((GAIN_ROWS, own), f32)
    for c in range(gain_cols):
        pick = jnp.where(from_lane + c * LANES == to_lane + me_ref[0] * own, 1.0, 0.0).astype(bf16)
        found = plain_dot(mine_ref[at], pick) + plain_dot(other_ref[at], pick)
        total += jnp.where(row == c, found, 0.0)
    outs[-1][...] = jnp.sum(total, axis=0, keepdims=True)


def finish(packed, layout, own):
    parts = packed.shape[0]
    flat = packed.reshape(-1, LANES)
    share = lax.psum_scatter(flat, "shard", scatter_dimension=0, tiled=True)
    count = lax.axis_size("replica")
    step = 1
    other = jnp.zeros_like(share)
    while step < count:
        if step > 1:
            share = (share.astype(f32) + other.astype(f32)).astype(bf16)
        other = lax.ppermute(share, "replica", [(i, i ^ step) for i in range(count)])
        step *= 2
    me = lax.axis_index("shard").reshape(1)
    outs = pl.pallas_call(
        functools.partial(finish_kernel, layout, own, parts * own // LANES),
        out_shape=tuple(jax.ShapeDtypeStruct((r, b * LANES), f32) for r, b in layout)
        + (jax.ShapeDtypeStruct((1, own), f32),),
        in_specs=[smem(), vmem(), vmem()],
        out_specs=(vmem(),) * (len(layout) + 1),
        compiler_params=params(),
        cost_estimate=cost(0, 4 << 20),
        name="finish",
    )(me, share, other)
    return outs[:-1] + (outs[-1][0],)


def to_blocks(mat, parts):
    rows = mat.shape[0] // parts
    cols = mat.shape[1] // LANES
    split = mat.reshape(parts, rows, cols, LANES).transpose(0, 2, 1, 3)
    return split.reshape(parts, cols * rows, LANES)


def gather_packed(mats):
    packed = jnp.concatenate([to_blocks(m, 1)[0] for m in mats], axis=0)
    whole = lax.all_gather(packed, "shard", axis=0, tiled=True)
    return whole.reshape(-1, packed.shape[0], LANES)


def shards(
    x_in,
    seq_units,
    deal,
    gain_attn,
    w_query,
    w_key,
    w_value,
    w_out,
    gain_ffn,
    w_gate,
    w_up,
    w_down,
    d_out,
):
    shard_count = lax.axis_size("shard")
    my_index = lax.axis_index("shard")
    given, width = x_in.shape[1:]
    span = d_out.shape[2]
    unit_max = span // shard_count
    rows = w_query.shape[0]
    down = w_down.shape[0]
    slot_ids = jnp.arange(shard_count, dtype=jnp.int32)
    outgoing = deal_rows(seq_units, deal, x_in[0], shard_count, unit_max)
    arrived = lax.all_to_all(outgoing, "shard", split_axis=0, concat_axis=0, tiled=True)
    own_seq = jnp.sum(jnp.where(slot_ids == my_index, deal[0], 0))
    count = jnp.sum(jnp.where(slot_ids == own_seq, seq_units[0], 0)).reshape(1)
    attn_pack = gather_packed((w_query, w_key, w_value, w_out))
    ffn_pack = gather_packed((w_gate, w_up, w_down))
    tokens = arrived.reshape(span, width)
    gain_one = gain_attn.reshape(1, width)
    gain_two = gain_ffn.reshape(1, width)
    n1, qkv = make_qkv(tokens, gain_one, attn_pack, rows)
    mixed, lse = attend_forward(count, qkv, unit_max)
    hidden, n2 = out_project(tokens, mixed, attn_pack, gain_two, rows)
    layer_out, g_h, g_hb, ffn_grads = ffn_both(
        count, hidden, n2, d_out[0, 0], gain_two, ffn_pack, unit_max, rows, down
    )
    own = width // shard_count
    cols = width // LANES
    wide = w_gate.shape[1] // LANES
    out_wg, out_wu, out_wd, out_gain_two = finish(
        ffn_grads, ((rows, wide), (rows, wide), (down, cols)), own
    )
    g_x, attn_grads = attend_back(
        count, qkv, mixed, lse, n1, tokens, g_h, g_hb, gain_one, attn_pack, unit_max, rows
    )
    returned = lax.all_to_all(
        g_x.reshape(shard_count, unit_max, width), "shard", split_axis=0, concat_axis=0, tiled=True
    )
    grad_x = undeal_rows(seq_units, deal, returned, given)[None]
    out_wq, out_wk, out_wv, out_wo, out_gain_one = finish(attn_grads, ((rows, cols),) * 4, own)
    return (
        layer_out.reshape(1, 1, span, width),
        grad_x,
        out_gain_one,
        out_gain_two,
        out_wq,
        out_wk,
        out_wv,
        out_wo,
        out_wg,
        out_wu,
        out_wd,
    )


def solution(mesh):
    return jax.shard_map(
        shards,
        mesh=mesh,
        in_specs=(
            P("replica", "shard", None),
            P("replica", None),
            P("replica", None),
            P(),
            P("shard", None),
            P("shard", None),
            P("shard", None),
            P("shard", None),
            P(),
            P("shard", None),
            P("shard", None),
            P("shard", None),
            P("replica", "shard", None, None),
        ),
        out_specs=(
            P("replica", "shard", None, None),
            P("replica", "shard", None),
            P("shard"),
            P("shard"),
            P("shard", None),
            P("shard", None),
            P("shard", None),
            P("shard", None),
            P("shard", None),
            P("shard", None),
            P("shard", None),
        ),
        check_vma=False,
    )
```

```python
import functools

import jax
import jax.numpy as jnp
from jax import lax
from jax.experimental import pallas as pl
from jax.experimental.pallas import tpu as pltpu
from jax.sharding import PartitionSpec as P

H = 12
HD = 64
LANES = 256
GAIN_ROWS = 16

norm_eps = 1e-06
neg_big = -1e30
bf16 = jnp.bfloat16
f32 = jnp.float32


def left_dot(lhs_mat, rhs_mat):
    return lax.dot_general(
        lhs_mat, rhs_mat, (((0,), (0,)), ((), ())), preferred_element_type=jnp.float32
    )


def right_dot(lhs_mat, rhs_mat):
    return lax.dot_general(
        lhs_mat, rhs_mat, (((1,), (1,)), ((), ())), preferred_element_type=jnp.float32
    )


def plain_dot(lhs_mat, rhs_mat):
    return jnp.dot(lhs_mat, rhs_mat, preferred_element_type=jnp.float32)


def slot_start(units_ref, order_ref, slot, shard_count):
    wanted = order_ref[0, slot]
    start = jnp.int32(0)
    count = jnp.int32(0)
    for k in range(shard_count):
        units = units_ref[0, k]
        start = start + jnp.where(k < wanted, units, 0)
        count = count + jnp.where(k == wanted, units, 0)
    return start, count


def deal_kernel(units_ref, order_ref, rows_ref, out_ref):
    shard_count, unit_max, _ = out_ref.shape
    given = rows_ref.shape[0]
    row = lax.broadcasted_iota(jnp.int32, (unit_max, given), 0)
    col = lax.broadcasted_iota(jnp.int32, (unit_max, given), 1)

    def step(slot, carry):
        start, count = slot_start(units_ref, order_ref, slot, shard_count)
        pick = jnp.where((col - start == row) & (row < count), 1.0, 0.0).astype(bf16)
        out_ref[slot] = plain_dot(pick, rows_ref[...]).astype(bf16)
        return carry

    lax.fori_loop(0, shard_count, step, 0)


def undeal_kernel(units_ref, order_ref, back_ref, out_ref, pick_ref):
    shard_count, unit_max, width = back_ref.shape
    given = out_ref.shape[0]
    row = lax.broadcasted_iota(jnp.int32, (unit_max, given), 0)
    col = lax.broadcasted_iota(jnp.int32, (unit_max, given), 1)

    def step(slot, carry):
        start, count = slot_start(units_ref, order_ref, slot, shard_count)
        pick = jnp.where((col - start == row) & (row < count), 1.0, 0.0).astype(bf16)
        pick_ref[pl.ds(pl.multiple_of(slot * unit_max, unit_max), unit_max), :] = pick
        return carry

    lax.fori_loop(0, shard_count, step, 0)
    whole = back_ref[...].reshape(shard_count * unit_max, width)
    out_ref[...] = left_dot(pick_ref[...], whole).astype(bf16)


def smem():
    return pl.BlockSpec(memory_space=pltpu.SMEM)


def vmem():
    return pl.BlockSpec(memory_space=pltpu.VMEM)


def deal_rows(units, order, rows, shard_count, unit_max):
    return pl.pallas_call(
        deal_kernel,
        out_shape=jax.ShapeDtypeStruct((shard_count, unit_max, rows.shape[1]), bf16),
        in_specs=[smem(), smem(), vmem()],
        out_specs=vmem(),
        name="deal_rows",
    )(units, order, rows)


def undeal_rows(units, order, back, given):
    shard_count, unit_max, width = back.shape
    return pl.pallas_call(
        undeal_kernel,
        out_shape=jax.ShapeDtypeStruct((given, width), bf16),
        in_specs=[smem(), smem(), vmem()],
        out_specs=vmem(),
        scratch_shapes=[pltpu.VMEM((shard_count * unit_max, given), bf16)],
        name="undeal_rows",
    )(units, order, back)


def const_block(shape):
    zeros = (0,) * len(shape)
    return pl.BlockSpec(shape, lambda *_: zeros)


def params():
    return pltpu.CompilerParams(vmem_limit_bytes=60 << 20)


def cost(flops, moved, trans=0):
    return pl.CostEstimate(flops=flops, bytes_accessed=moved, transcendentals=trans)


def inverse_rms(rows):
    return lax.rsqrt(jnp.mean(rows * rows, axis=-1, keepdims=True) + norm_eps)


def whole_block(ref):
    parts, rows, lanes = ref.shape
    return ref[...].reshape(parts * rows, lanes)


def qkv_kernel(x_ref, gain_ref, w_ref, n1_ref, qkv_ref):
    block = pl.program_id(0)

    @pl.when(block == 0)
    def _():
        rows = x_ref[...].astype(f32)
        n1_ref[...] = (rows * inverse_rms(rows) * gain_ref[...]).astype(bf16)

    factor = jnp.where(block < n1_ref.shape[1] // LANES, HD ** (-0.5), 1.0)
    made = plain_dot(n1_ref[...], whole_block(w_ref)).astype(bf16).astype(f32)
    qkv_ref[...] = (made * factor).astype(bf16)


def make_qkv(tokens, gain, packed, rows):
    span, width = tokens.shape
    parts = packed.shape[0]
    blocks = 3 * width // LANES
    return pl.pallas_call(
        qkv_kernel,
        grid=(blocks,),
        out_shape=(
            jax.ShapeDtypeStruct((span, width), bf16),
            jax.ShapeDtypeStruct((span, 3 * width), bf16),
        ),
        in_specs=[
            const_block((span, width)),
            const_block((1, width)),
            pl.BlockSpec((parts, rows, LANES), lambda j: (0, j, 0)),
        ],
        out_specs=(
            const_block((span, width)),
            pl.BlockSpec((span, LANES), lambda j: (0, j)),
        ),
        compiler_params=params(),
        cost_estimate=cost(6 * span * width * width, 14 << 20),
        name="make_qkv",
    )(tokens, gain, packed)


def live_bias(count, span, unit_max):
    row = lax.broadcasted_iota(jnp.int32, (span, 2 * HD), 0)
    return jnp.where(lax.rem(row, unit_max) < count, 0.0, neg_big).astype(bf16)


def head_keys(keys, bias, lane, head):
    inside = (lane // HD) == head
    return jnp.where(inside, keys, jnp.where(lane == (1 - head) * HD, bias, jnp.zeros_like(keys)))


def head_queries(queries, lane, head):
    inside = (lane // HD) == head
    one = jnp.where(lane == (1 - head) * HD, 1.0, 0.0).astype(bf16)
    return jnp.where(inside, queries, one)


def attend_kernel(unit_max, chunk, count_ref, q_ref, k_ref, v_ref, o_ref, lse_ref, kb_ref, vt_ref):
    span = q_ref.shape[0]
    pair = 2 * HD
    lane = lax.broadcasted_iota(jnp.int32, (span, pair), 1)
    bias = live_bias(count_ref[0], span, unit_max)
    keys = k_ref[...]
    values_t = v_ref[...].T
    for head in range(2):
        kb_ref[head] = head_keys(keys, bias, lane, head)
        vt_ref[head, :HD] = values_t[head * HD : (head + 1) * HD]
        vt_ref[head, HD:] = jnp.ones((vt_ref.shape[1] - HD, span), bf16)
    lane_c = lane[:chunk]
    for begin in range(0, span, chunk):
        queries = q_ref[begin : begin + chunk, :]
        mixed = []
        for head in range(2):
            scores = right_dot(kb_ref[head], head_queries(queries, lane_c, head))
            top = jnp.max(scores, axis=0, keepdims=True)
            probs = jnp.exp(scores - top).astype(bf16)
            both = plain_dot(vt_ref[head], probs)
            total = both[HD : HD + 1]
            mixed.append(both[:HD] * (1.0 / total))
            lse_ref[0, head : head + 1, begin : begin + chunk] = top + jnp.log(total)
        o_ref[begin : begin + chunk, :] = jnp.concatenate(mixed, axis=0).T.astype(bf16)


def attend_forward(count, qkv, unit_max):
    span = qkv.shape[0]
    width = qkv.shape[1] // 3
    pair = 2 * HD
    pairs = width // pair

    def block(first):
        return pl.BlockSpec((span, pair), lambda p: (0, first + p))

    return pl.pallas_call(
        functools.partial(attend_kernel, unit_max, 512),
        grid=(pairs,),
        out_shape=(
            jax.ShapeDtypeStruct((span, width), bf16),
            jax.ShapeDtypeStruct((pairs, 8, span), f32),
        ),
        in_specs=[smem(), block(0), block(pairs), block(2 * pairs)],
        out_specs=(block(0), pl.BlockSpec((1, 8, span), lambda p: (p, 0, 0))),
        scratch_shapes=[
            pltpu.VMEM((2, span, pair), bf16),
            pltpu.VMEM((2, HD + 16, span), bf16),
        ],
        compiler_params=params(),
        cost_estimate=cost(4 * span * span * width, 8 << 20, span * span * H),
        name="attend_forward",
    )(count, qkv, qkv, qkv)


def out_kernel(x_ref, o_ref, w_ref, gain_ref, h_ref, n2_ref):
    parts, total, lanes = w_ref.shape
    width = h_ref.shape[1]
    rows = width // parts
    for c in range(width // lanes):
        weight = w_ref[:, c * rows : (c + 1) * rows, :].reshape(width, lanes)
        cols = slice(c * lanes, (c + 1) * lanes)
        h_ref[:, cols] = x_ref[:, cols].astype(f32) + plain_dot(o_ref[...], weight)
    hidden = h_ref[...]
    n2_ref[...] = (hidden * inverse_rms(hidden) * gain_ref[...]).astype(bf16)


def out_project(tokens, mixed, packed, gain, rows):
    span, width = tokens.shape
    parts = packed.shape[0]
    blocks = width // LANES
    return pl.pallas_call(
        out_kernel,
        grid=(1,),
        out_shape=(
            jax.ShapeDtypeStruct((span, width), f32),
            jax.ShapeDtypeStruct((span, width), bf16),
        ),
        in_specs=[
            const_block((span, width)),
            const_block((span, width)),
            pl.BlockSpec((parts, blocks * rows, LANES), lambda i: (0, 3, 0)),
            const_block((1, width)),
        ],
        out_specs=(const_block((span, width)), const_block((span, width))),
        compiler_params=params(),
        cost_estimate=cost(2 * span * width * width, 9 << 20),
        name="out_project",
    )(tokens, mixed, packed, gain)


def spread_gain(total, parts):
    width = total.shape[1]
    own = width // parts
    shape = (parts, GAIN_ROWS, LANES)
    part = lax.broadcasted_iota(jnp.int32, shape, 0)
    row = lax.broadcasted_iota(jnp.int32, shape, 1)
    place = row * LANES + lax.broadcasted_iota(jnp.int32, shape, 2)
    mine = (place >= part * own) & (place < (part + 1) * own)
    out = jnp.zeros(shape, f32)
    for c in range(width // LANES):
        piece = jnp.broadcast_to(total[:, c * LANES : (c + 1) * LANES][None], shape)
        out = jnp.where((row == c) & mine, piece, out)
    return out.astype(bf16)


def ffn_kernel(
    unit_max,
    count_ref,
    h_ref,
    n2_ref,
    d_ref,
    gain_ref,
    wg_ref,
    wu_ref,
    wd_ref,
    out_ref,
    gh_ref,
    ghb_ref,
    pack_ref,
    gb_ref,
    y_ref,
    gn_ref,
    stage_gate,
    stage_up,
    stage_down,
    stage_gain,
    sems,
):
    step = pl.program_id(0)
    steps = pl.num_programs(0)
    slot = lax.rem(step, 2)
    span, width = h_ref.shape
    parts, rows, _ = wg_ref.shape
    few, down_all, _ = wd_ref.shape
    cols = width // LANES
    down = down_all // cols
    ff_blocks = steps

    def copies(which, at):
        return (
            pltpu.make_async_copy(
                stage_gate.at[at],
                pack_ref.at[:, pl.ds(pl.multiple_of(which * rows, 8), rows), :],
                sems.at[0, at],
            ),
            pltpu.make_async_copy(
                stage_up.at[at],
                pack_ref.at[:, pl.ds(pl.multiple_of((ff_blocks + which) * rows, 8), rows), :],
                sems.at[1, at],
            ),
            pltpu.make_async_copy(
                stage_down.at[at],
                pack_ref.at[pl.ds(which * few, few), pl.ds(2 * ff_blocks * rows, down_all), :],
                sems.at[2, at],
            ),
        )

    row = lax.broadcasted_iota(jnp.int32, (span, 1), 0)
    live = lax.rem(row, unit_max) < count_ref[0]

    @pl.when(step == 0)
    def _():
        gb_ref[...] = jnp.where(live, d_ref[...].astype(f32), 0.0).astype(bf16)

    @pl.when(step >= 2)
    def _():
        for copy in copies(step - 2, slot):
            copy.wait()

    n2 = n2_ref[...]
    gb = gb_ref[...]
    w_gate = whole_block(wg_ref)
    w_up = whole_block(wu_ref)
    gate = plain_dot(n2, w_gate)
    up = plain_dot(n2, w_up)
    downs = [
        wd_ref[:, c * down : (c + 1) * down, :].reshape(few * down, LANES) for c in range(cols)
    ]
    g_act = right_dot(gb[:, :LANES], downs[0])
    for c in range(1, cols):
        g_act += right_dot(gb[:, c * LANES : (c + 1) * LANES], downs[c])
    c0 = 0.7978845608028654
    c1 = 0.044715
    square = gate * gate
    tang = jnp.tanh(c0 * gate * (1.0 + c1 * square))
    half = 0.5 * (1.0 + tang)
    gelu = gate * half
    slope = half + (0.5 * c0) * gate * (1.0 - tang * tang) * (1.0 + (3.0 * c1) * square)
    act = (gelu * up).astype(bf16)
    g_gate = (g_act * up * slope).astype(bf16)
    g_up = (g_act * gelu).astype(bf16)
    for c in range(cols):
        place = slice(c * LANES, (c + 1) * LANES)
        add = plain_dot(act, downs[c])
        grad = right_dot(g_gate, w_gate[place]) + right_dot(g_up, w_up[place])
        wide = left_dot(act, gb[:, place]).astype(bf16).reshape(few, down, LANES)
        stage_down[slot, :, c * down : (c + 1) * down, :] = wide

        @pl.when(step == 0)
        def _():
            y_ref[:, place] = add
            gn_ref[:, place] = grad

        @pl.when(step > 0)
        def _():
            y_ref[:, place] += add
            gn_ref[:, place] += grad

    stage_gate[slot] = left_dot(n2, g_gate).astype(bf16).reshape(parts, rows, LANES)
    stage_up[slot] = left_dot(n2, g_up).astype(bf16).reshape(parts, rows, LANES)
    for copy in copies(step, slot):
        copy.start()

    @pl.when(step == steps - 1)
    def _():
        hidden = h_ref[...]
        out_ref[...] = jnp.where(live, hidden + y_ref[...], 0.0).astype(bf16)
        inv = inverse_rms(hidden)
        grad = gn_ref[...]
        scaled = hidden * inv
        total = jnp.sum(grad * scaled, axis=0, keepdims=True)
        stage_gain[...] = spread_gain(total, parts)
        last = pltpu.make_async_copy(
            stage_gain,
            pack_ref.at[:, pl.ds(2 * ff_blocks * rows + down_all, GAIN_ROWS), :],
            sems.at[3, 0],
        )
        last.start()
        weighted = grad * gain_ref[...]
        mean = jnp.mean(scaled * weighted, axis=-1, keepdims=True)
        g_h = gb_ref[...].astype(f32) + inv * (weighted - scaled * mean)
        gh_ref[...] = g_h
        ghb_ref[...] = g_h.astype(bf16)
        for copy in copies(step - 1, 1 - slot) + copies(step, slot):
            copy.wait()
        last.wait()


def ffn_both(count, hidden, normed, d_rows, gain, packed, unit_max, rows, down):
    span, width = hidden.shape
    parts = packed.shape[0]
    ff = parts * down
    blocks = ff // LANES
    cols = width // LANES
    few = LANES // down
    moved = 2 * blocks * rows + cols * down
    full = const_block((span, width))
    return pl.pallas_call(
        functools.partial(ffn_kernel, unit_max),
        grid=(blocks,),
        out_shape=(
            jax.ShapeDtypeStruct((span, width), bf16),
            jax.ShapeDtypeStruct((span, width), f32),
            jax.ShapeDtypeStruct((span, width), bf16),
            jax.ShapeDtypeStruct((parts, moved + GAIN_ROWS, LANES), bf16),
        ),
        in_specs=[
            smem(),
            full,
            full,
            full,
            const_block((1, width)),
            pl.BlockSpec((parts, rows, LANES), lambda j: (0, j, 0)),
            pl.BlockSpec((parts, rows, LANES), lambda j: (0, blocks + j, 0)),
            pl.BlockSpec((few, cols * down, LANES), lambda j: (j, 2 * blocks * rows // (cols * down), 0)),
        ],
        out_specs=(full, full, full, pl.BlockSpec(memory_space=pl.ANY)),
        scratch_shapes=[
            pltpu.VMEM((span, width), bf16),
            pltpu.VMEM((span, width), f32),
            pltpu.VMEM((span, width), f32),
            pltpu.VMEM((2, parts, rows, LANES), bf16),
            pltpu.VMEM((2, parts, rows, LANES), bf16),
            pltpu.VMEM((2, few, cols * down, LANES), bf16),
            pltpu.VMEM((parts, GAIN_ROWS, LANES), bf16),
            pltpu.SemaphoreType.DMA((4, 2)),
        ],
        compiler_params=params(),
        cost_estimate=cost(18 * span * width * ff, 36 << 20, span * ff),
        name="ffn_both",
    )(count, hidden, normed, d_rows, gain, packed, packed, packed)


def attend_back_kernel(
    unit_max,
    chunk,
    count_ref,
    place_ref,
    q_ref,
    k_ref,
    v_ref,
    o_ref,
    lse_ref,
    n1_ref,
    x_ref,
    gh_ref,
    ghb_ref,
    gain_ref,
    wq_ref,
    wk_ref,
    wv_ref,
    wo_ref,
    gx_ref,
    keep_ref,
    send_ref,
    wo_s,
    do_s,
    delta_s,
    kt_s,
    dqt_s,
    dk_s,
    dv_s,
    gn_s,
    stage,
    stage_gain,
    sems,
    gain_sem,
):
    step = pl.program_id(0)
    steps = pl.num_programs(0)
    span, width = x_ref.shape
    parts, rows, _ = wq_ref.shape
    cols = width // LANES
    pair = 2 * HD
    heads = LANES // HD
    lane = lax.broadcasted_iota(jnp.int32, (span, pair), 1)
    lane_c = lane[:chunk]
    mine = pl.ds(pl.multiple_of(step * LANES, LANES), LANES)

    half_parts = parts // 2

    def copies(which):
        return [
            pltpu.make_async_copy(
                stage.at[m, pl.ds(side * half_parts, half_parts)],
                to_ref.at[:, pl.ds(pl.multiple_of((m * cols + which) * rows, 8), rows), :],
                sems.at[m, side],
            )
            for m in range(4)
            for side, to_ref in enumerate((keep_ref, send_ref))
        ]

    def put(m, grad):
        for part in range(parts):
            stage[m, place_ref[part]] = grad[part * rows : (part + 1) * rows].astype(bf16)

    @pl.when(step == 0)
    def _():
        for c in range(cols):
            wo_s[c] = wo_ref[:, c * rows : (c + 1) * rows, :].reshape(width, LANES)

    g_o = right_dot(ghb_ref[:, :LANES], wo_s[0, mine, :])
    for c in range(1, cols):
        g_o += right_dot(ghb_ref[:, c * LANES : (c + 1) * LANES], wo_s[c, mine, :])
    g_o = g_o.astype(bf16)
    do_s[...] = g_o
    prod = g_o.astype(f32) * o_ref[:, mine].astype(f32)
    high = prod.astype(bf16)
    low = (prod - high.astype(f32)).astype(bf16)
    picker = jnp.where(
        lax.broadcasted_iota(jnp.int32, (8, LANES), 1) // HD
        == lax.broadcasted_iota(jnp.int32, (8, LANES), 0),
        1.0,
        0.0,
    ).astype(bf16)
    delta_s[...] = right_dot(picker, high) + right_dot(picker, low)
    kt_s[...] = k_ref[...].T
    dk_s[...] = jnp.zeros_like(dk_s)
    dv_s[...] = jnp.zeros_like(dv_s)
    bias = live_bias(count_ref[0], span, unit_max)

    def one_head(head, carry):
        half = head // 2
        sub = lax.rem(head, 2)
        side = pl.ds(pl.multiple_of(half * pair, pair), pair)
        inside = (lane // HD) == sub
        inside_c = (lane_c // HD) == sub
        zero = jnp.zeros((), bf16)
        keys = head_keys(k_ref[:, side], bias, lane, sub)
        values = jnp.where(inside, v_ref[:, side], zero)
        keys_t = kt_s[pl.ds(pl.multiple_of(head * HD, HD), HD), :]
        d_k = None
        d_v = None
        for begin in range(0, span, chunk):
            part = slice(begin, begin + chunk)
            queries = q_ref[part, side]
            grads = do_s[part, side]
            scores = right_dot(keys, head_queries(queries, lane_c, sub))
            probs = jnp.exp(scores - lse_ref[half, pl.ds(sub, 1), part])
            d_probs = right_dot(values, grads)
            d_scores = (probs * (d_probs - delta_s[pl.ds(head, 1), part])).astype(bf16)
            add_v = plain_dot(probs.astype(bf16), jnp.where(inside_c, grads, zero))
            add_k = plain_dot(d_scores, jnp.where(inside_c, queries, zero))
            d_v = add_v if d_v is None else d_v + add_v
            d_k = add_k if d_k is None else d_k + add_k
            dqt_s[pl.ds(pl.multiple_of(head * HD, HD), HD), part] = plain_dot(keys_t, d_scores)
        dk_s[:, side] += d_k
        dv_s[:, side] += d_v
        return carry

    lax.fori_loop(0, heads, one_head, 0)
    d_q = (dqt_s[...].T * (HD ** (-0.5))).astype(bf16)
    d_k = dk_s[...].astype(bf16)
    d_v = dv_s[...].astype(bf16)

    add = (
        right_dot(d_q, whole_block(wq_ref))
        + right_dot(d_k, whole_block(wk_ref))
        + right_dot(d_v, whole_block(wv_ref))
    )

    @pl.when(step == 0)
    def _():
        gn_s[...] = add

    @pl.when(step > 0)
    def _():
        gn_s[...] += add
        for copy in copies(step - 1):
            copy.wait()

    n1 = n1_ref[...]
    for m, grad in enumerate((d_q, d_k, d_v)):
        put(m, left_dot(n1, grad))
    put(3, left_dot(o_ref[...], ghb_ref[:, mine]))
    for copy in copies(step):
        copy.start()

    @pl.when(step == steps - 1)
    def _():
        tokens = x_ref[...].astype(f32)
        inv = inverse_rms(tokens)
        grad = gn_s[...]
        scaled = tokens * inv
        total = jnp.sum(grad * scaled, axis=0, keepdims=True)
        spread = spread_gain(total, parts)
        for part in range(parts):
            stage_gain[place_ref[part]] = spread[part]
        last = [
            pltpu.make_async_copy(
                stage_gain.at[pl.ds(side * half_parts, half_parts)],
                to_ref.at[:, pl.ds(4 * cols * rows, GAIN_ROWS), :],
                gain_sem.at[side],
            )
            for side, to_ref in enumerate((keep_ref, send_ref))
        ]
        for copy in last:
            copy.start()
        weighted = grad * gain_ref[...]
        mean = jnp.mean(scaled * weighted, axis=-1, keepdims=True)
        gx_ref[...] = (gh_ref[...] + inv * (weighted - scaled * mean)).astype(bf16)
        for copy in copies(step) + last:
            copy.wait()


def attend_back(count, place, qkv, mixed, lse, n1, tokens, g_h, g_hb, gain, packed, unit_max, rows):
    span, width = tokens.shape
    parts = packed.shape[0]
    cols = width // LANES
    full = const_block((span, width))

    def block(first):
        return pl.BlockSpec((span, LANES), lambda p: (0, first + p))

    def weight(first):
        return pl.BlockSpec((parts, rows, LANES), lambda p: (0, first + p, 0))

    return pl.pallas_call(
        functools.partial(attend_back_kernel, unit_max, 512),
        grid=(cols,),
        out_shape=(
            jax.ShapeDtypeStruct((span, width), bf16),
            jax.ShapeDtypeStruct((parts // 2, 4 * cols * rows + GAIN_ROWS, LANES), bf16),
            jax.ShapeDtypeStruct((parts // 2, 4 * cols * rows + GAIN_ROWS, LANES), bf16),
        ),
        in_specs=[
            smem(),
            smem(),
            block(0),
            block(cols),
            block(2 * cols),
            full,
            pl.BlockSpec((2, 8, span), lambda p: (p, 0, 0)),
            full,
            full,
            full,
            full,
            const_block((1, width)),
            weight(0),
            weight(cols),
            weight(2 * cols),
            pl.BlockSpec((parts, cols * rows, LANES), lambda p: (0, 3, 0)),
        ],
        out_specs=(full, pl.BlockSpec(memory_space=pl.ANY), pl.BlockSpec(memory_space=pl.ANY)),
        scratch_shapes=[
            pltpu.VMEM((cols, width, LANES), bf16),
            pltpu.VMEM((span, LANES), bf16),
            pltpu.VMEM((8, span), f32),
            pltpu.VMEM((LANES, span), bf16),
            pltpu.VMEM((LANES, span), f32),
            pltpu.VMEM((span, LANES), f32),
            pltpu.VMEM((span, LANES), f32),
            pltpu.VMEM((span, width), f32),
            pltpu.VMEM((4, parts, rows, LANES), bf16),
            pltpu.VMEM((parts, GAIN_ROWS, LANES), bf16),
            pltpu.SemaphoreType.DMA((4, 2)),
            pltpu.SemaphoreType.DMA((2,)),
        ],
        compiler_params=params(),
        cost_estimate=cost(10 * span * span * width + 16 * span * width * width, 24 << 20, span * span * H),
        name="attend_back",
    )(count, place, qkv, qkv, qkv, mixed, lse, n1, tokens, g_h, g_hb, gain, packed, packed, packed, packed)


def finish_kernel(layout, own, gain_cols, me_ref, mine_ref, other_ref, *outs):
    begin = 0
    for (rows, blocks), out_ref in zip(layout, outs[:-1]):
        for c in range(blocks):
            at = slice(begin, begin + rows)
            out_ref[:, c * LANES : (c + 1) * LANES] = mine_ref[at].astype(f32) + other_ref[at].astype(f32)
            begin += rows
    at = slice(begin, begin + GAIN_ROWS)
    row = lax.broadcasted_iota(jnp.int32, (GAIN_ROWS, own), 0)
    from_lane = lax.broadcasted_iota(jnp.int32, (LANES, own), 0)
    to_lane = lax.broadcasted_iota(jnp.int32, (LANES, own), 1)
    total = jnp.zeros((GAIN_ROWS, own), f32)
    for c in range(gain_cols):
        pick = jnp.where(from_lane + c * LANES == to_lane + me_ref[0] * own, 1.0, 0.0).astype(bf16)
        found = plain_dot(mine_ref[at], pick) + plain_dot(other_ref[at], pick)
        total += jnp.where(row == c, found, 0.0)
    outs[-1][...] = jnp.sum(total, axis=0, keepdims=True)


def relative_places(shard_count):
    along = shard_count // 4
    mine = lax.axis_index("shard")
    part = jnp.arange(shard_count, dtype=jnp.int32)
    core = lax.rem(part, 2) ^ lax.rem(mine, 2)
    side = lax.rem(part // 2, 2) ^ lax.rem(mine // 2, 2)
    steps = lax.rem(part // 4 - mine // 4 + along, along)
    return (core * 2 + side) * along + steps


def to_core(value):
    count = lax.axis_size("shard")
    return lax.ppermute(value, "shard", [(i, i ^ 1) for i in range(count)])


def to_side(value):
    count = lax.axis_size("shard")
    return lax.ppermute(value, "shard", [(i, i ^ 2) for i in range(count)])


def along_z(value, step):
    count = lax.axis_size("shard")
    return lax.ppermute(value, "shard", [(i, (i + 4 * step) % count) for i in range(count)])


def scatter_queue(packed):
    return lax.psum_scatter(packed.reshape(-1, LANES), "shard", scatter_dimension=0, tiled=True)


def scatter_permute(keep, send):
    along = keep.shape[0] // 2
    came = to_core(send)
    pass_on = (keep[along:].astype(f32) + came[along:].astype(f32)).astype(bf16)
    crossed = to_side(pass_on)
    column = (keep[:along].astype(f32) + came[:along].astype(f32) + crossed.astype(f32)).astype(bf16)
    found = [along_z(column[k], k) for k in range(1, along)]
    total = column[0].astype(f32)
    for piece in found:
        total = total + piece.astype(f32)
    return total.astype(bf16)


def finish(share, layout, own, parts):
    count = lax.axis_size("replica")
    step = 1
    other = jnp.zeros_like(share)
    while step < count:
        if step > 1:
            share = (share.astype(f32) + other.astype(f32)).astype(bf16)
        other = lax.ppermute(share, "replica", [(i, i ^ step) for i in range(count)])
        step *= 2
    me = lax.axis_index("shard").reshape(1)
    outs = pl.pallas_call(
        functools.partial(finish_kernel, layout, own, parts * own // LANES),
        out_shape=tuple(jax.ShapeDtypeStruct((r, b * LANES), f32) for r, b in layout)
        + (jax.ShapeDtypeStruct((1, own), f32),),
        in_specs=[smem(), vmem(), vmem()],
        out_specs=(vmem(),) * (len(layout) + 1),
        compiler_params=params(),
        cost_estimate=cost(0, 4 << 20),
        name="finish",
    )(me, share, other)
    return outs[:-1] + (outs[-1][0],)


def to_blocks(mat, parts):
    rows = mat.shape[0] // parts
    cols = mat.shape[1] // LANES
    split = mat.reshape(parts, rows, cols, LANES).transpose(0, 2, 1, 3)
    return split.reshape(parts, cols * rows, LANES)


def gather_packed(mats):
    packed = jnp.concatenate([to_blocks(m, 1)[0] for m in mats], axis=0)
    whole = lax.all_gather(packed, "shard", axis=0, tiled=True)
    return whole.reshape(-1, packed.shape[0], LANES)


def shards(
    x_in,
    seq_units,
    deal,
    gain_attn,
    w_query,
    w_key,
    w_value,
    w_out,
    gain_ffn,
    w_gate,
    w_up,
    w_down,
    d_out,
):
    shard_count = lax.axis_size("shard")
    my_index = lax.axis_index("shard")
    given, width = x_in.shape[1:]
    span = d_out.shape[2]
    unit_max = span // shard_count
    rows = w_query.shape[0]
    down = w_down.shape[0]
    slot_ids = jnp.arange(shard_count, dtype=jnp.int32)
    outgoing = deal_rows(seq_units, deal, x_in[0], shard_count, unit_max)
    arrived = lax.all_to_all(outgoing, "shard", split_axis=0, concat_axis=0, tiled=True)
    own_seq = jnp.sum(jnp.where(slot_ids == my_index, deal[0], 0))
    count = jnp.sum(jnp.where(slot_ids == own_seq, seq_units[0], 0)).reshape(1)
    attn_pack = gather_packed((w_query, w_key, w_value, w_out))
    ffn_pack = gather_packed((w_gate, w_up, w_down))
    tokens = arrived.reshape(span, width)
    gain_one = gain_attn.reshape(1, width)
    gain_two = gain_ffn.reshape(1, width)
    n1, qkv = make_qkv(tokens, gain_one, attn_pack, rows)
    mixed, lse = attend_forward(count, qkv, unit_max)
    hidden, n2 = out_project(tokens, mixed, attn_pack, gain_two, rows)
    layer_out, g_h, g_hb, ffn_grads = ffn_both(
        count, hidden, n2, d_out[0, 0], gain_two, ffn_pack, unit_max, rows, down
    )
    own = width // shard_count
    cols = width // LANES
    wide = w_gate.shape[1] // LANES
    ffn_share = scatter_queue(ffn_grads)
    place = relative_places(shard_count)
    g_x, keep, send = attend_back(
        count, place, qkv, mixed, lse, n1, tokens, g_h, g_hb, gain_one, attn_pack, unit_max, rows
    )
    returned = lax.all_to_all(
        g_x.reshape(shard_count, unit_max, width), "shard", split_axis=0, concat_axis=0, tiled=True
    )
    grad_x = undeal_rows(seq_units, deal, returned, given)[None]
    attn_share = scatter_permute(keep, send)
    out_wq, out_wk, out_wv, out_wo, out_gain_one = finish(
        attn_share, ((rows, cols),) * 4, own, shard_count
    )
    out_wg, out_wu, out_wd, out_gain_two = finish(
        ffn_share, ((rows, wide), (rows, wide), (down, cols)), own, shard_count
    )
    return (
        layer_out.reshape(1, 1, span, width),
        grad_x,
        out_gain_one,
        out_gain_two,
        out_wq,
        out_wk,
        out_wv,
        out_wo,
        out_wg,
        out_wu,
        out_wd,
    )


def solution(mesh):
    return jax.shard_map(
        shards,
        mesh=mesh,
        in_specs=(
            P("replica", "shard", None),
            P("replica", None),
            P("replica", None),
            P(),
            P("shard", None),
            P("shard", None),
            P("shard", None),
            P("shard", None),
            P(),
            P("shard", None),
            P("shard", None),
            P("shard", None),
            P("replica", "shard", None, None),
        ),
        out_specs=(
            P("replica", "shard", None, None),
            P("replica", "shard", None),
            P("shard"),
            P("shard"),
            P("shard", None),
            P("shard", None),
            P("shard", None),
            P("shard", None),
            P("shard", None),
            P("shard", None),
            P("shard", None),
        ),
        check_vma=False,
    )
```

```python
import functools

import jax
import jax.numpy as jnp
from jax import lax
from jax.experimental import pallas as pl
from jax.experimental.pallas import tpu as pltpu
from jax.sharding import PartitionSpec as P

H = 12
HD = 64
LANES = 256
GAIN_ROWS = 16

norm_eps = 1e-06
neg_big = -1e30
bf16 = jnp.bfloat16
f32 = jnp.float32


def left_dot(lhs_mat, rhs_mat):
    return lax.dot_general(
        lhs_mat, rhs_mat, (((0,), (0,)), ((), ())), preferred_element_type=jnp.float32
    )


def right_dot(lhs_mat, rhs_mat):
    return lax.dot_general(
        lhs_mat, rhs_mat, (((1,), (1,)), ((), ())), preferred_element_type=jnp.float32
    )


def plain_dot(lhs_mat, rhs_mat):
    return jnp.dot(lhs_mat, rhs_mat, preferred_element_type=jnp.float32)


def slot_start(units_ref, order_ref, slot, shard_count):
    wanted = order_ref[0, slot]
    start = jnp.int32(0)
    count = jnp.int32(0)
    for k in range(shard_count):
        units = units_ref[0, k]
        start = start + jnp.where(k < wanted, units, 0)
        count = count + jnp.where(k == wanted, units, 0)
    return start, count


def pick_rows(units_ref, order_ref, pick_ref, shard_count, unit_max):
    given = pick_ref.shape[1]
    row = lax.broadcasted_iota(jnp.int32, (unit_max, given), 0)
    ahead = lax.broadcasted_iota(jnp.int32, (unit_max, given), 1) - row

    def step(slot, carry):
        start, count = slot_start(units_ref, order_ref, slot, shard_count)
        pick = jnp.where((ahead == start) & (row < count), 1.0, 0.0).astype(bf16)
        pick_ref[pl.ds(pl.multiple_of(slot * unit_max, unit_max), unit_max), :] = pick
        return carry

    lax.fori_loop(0, shard_count, step, 0)


def deal_kernel(units_ref, order_ref, rows_ref, out_ref, pick_ref):
    shard_count, unit_max, width = out_ref.shape
    pick_rows(units_ref, order_ref, pick_ref, shard_count, unit_max)
    found = plain_dot(pick_ref[...], rows_ref[...]).astype(bf16)
    out_ref[...] = found.reshape(shard_count, unit_max, width)


def undeal_kernel(units_ref, order_ref, back_ref, out_ref, pick_ref):
    shard_count, unit_max, width = back_ref.shape
    pick_rows(units_ref, order_ref, pick_ref, shard_count, unit_max)
    whole = back_ref[...].reshape(shard_count * unit_max, width)
    out_ref[...] = left_dot(pick_ref[...], whole).astype(bf16)


def smem():
    return pl.BlockSpec(memory_space=pltpu.SMEM)


def vmem():
    return pl.BlockSpec(memory_space=pltpu.VMEM)


def deal_rows(units, order, rows, shard_count, unit_max):
    return pl.pallas_call(
        deal_kernel,
        out_shape=jax.ShapeDtypeStruct((shard_count, unit_max, rows.shape[1]), bf16),
        in_specs=[smem(), smem(), vmem()],
        out_specs=vmem(),
        scratch_shapes=[pltpu.VMEM((shard_count * unit_max, rows.shape[0]), bf16)],
        name="deal_rows",
    )(units, order, rows)


def undeal_rows(units, order, back, given):
    shard_count, unit_max, width = back.shape
    return pl.pallas_call(
        undeal_kernel,
        out_shape=jax.ShapeDtypeStruct((given, width), bf16),
        in_specs=[smem(), smem(), vmem()],
        out_specs=vmem(),
        scratch_shapes=[pltpu.VMEM((shard_count * unit_max, given), bf16)],
        name="undeal_rows",
    )(units, order, back)


def const_block(shape):
    zeros = (0,) * len(shape)
    return pl.BlockSpec(shape, lambda *_: zeros)


def params():
    return pltpu.CompilerParams(vmem_limit_bytes=60 << 20)


def cost(flops, moved, trans=0):
    return pl.CostEstimate(flops=flops, bytes_accessed=moved, transcendentals=trans)


def inverse_rms(rows):
    return lax.rsqrt(jnp.mean(rows * rows, axis=-1, keepdims=True) + norm_eps)


def whole_block(ref):
    parts, rows, lanes = ref.shape
    return ref[...].reshape(parts * rows, lanes)


def qkv_kernel(me_ref, x_ref, gain_ref, a_ref, b_ref, fa_ref, fb_ref, n1_ref, qkv_ref, w_ref):
    block = pl.program_id(0)
    along = a_ref.shape[0]
    width = n1_ref.shape[1]
    me = me_ref[0]
    core = lax.rem(me, 2)
    side = lax.rem(lax.div(me, 2), 2)
    height = lax.div(me, 4)

    @pl.when(block == 0)
    def _():
        rows = x_ref[...].astype(f32)
        n1_ref[...] = (rows * inverse_rms(rows) * gain_ref[...]).astype(bf16)

    for step in range(along):
        there = lax.rem(height - step + along, along) * 4
        w_ref[there + 2 * side + core] = a_ref[step]
        w_ref[there + 2 * side + 1 - core] = fa_ref[step]
        w_ref[there + 2 * (1 - side) + core] = b_ref[step]
        w_ref[there + 2 * (1 - side) + 1 - core] = fb_ref[step]

    @pl.when(block < 3 * width // LANES)
    def _():
        factor = jnp.where(block < width // LANES, HD ** (-0.5), 1.0)
        made = plain_dot(n1_ref[...], whole_block(w_ref)).astype(bf16).astype(f32)
        qkv_ref[...] = (made * factor).astype(bf16)


def make_qkv(me, tokens, gain, pieces, rows):
    span, width = tokens.shape
    along = pieces[0].shape[0]
    blocks = 3 * width // LANES
    everything = 4 * width // LANES
    piece = pl.BlockSpec((along, rows, LANES), lambda j: (0, j, 0))
    return pl.pallas_call(
        qkv_kernel,
        grid=(everything,),
        out_shape=(
            jax.ShapeDtypeStruct((span, width), bf16),
            jax.ShapeDtypeStruct((span, 3 * width), bf16),
            jax.ShapeDtypeStruct((4 * along, everything * rows, LANES), bf16),
        ),
        in_specs=[
            smem(),
            const_block((span, width)),
            const_block((1, width)),
            piece,
            piece,
            piece,
            piece,
        ],
        out_specs=(
            const_block((span, width)),
            pl.BlockSpec((span, LANES), lambda j: (0, jnp.minimum(j, blocks - 1))),
            pl.BlockSpec((4 * along, rows, LANES), lambda j: (0, j, 0)),
        ),
        compiler_params=params(),
        cost_estimate=cost(6 * span * width * width, 14 << 20),
        name="make_qkv",
    )(me, tokens, gain, *pieces)


def live_bias(count, span, unit_max):
    row = lax.broadcasted_iota(jnp.int32, (span, 2 * HD), 0)
    return jnp.where(lax.rem(row, unit_max) < count, 0.0, neg_big).astype(bf16)


def head_keys(keys, bias, lane, head):
    inside = (lane // HD) == head
    return jnp.where(inside, keys, jnp.where(lane == (1 - head) * HD, bias, jnp.zeros_like(keys)))


def head_queries(queries, lane, head):
    inside = (lane // HD) == head
    one = jnp.where(lane == (1 - head) * HD, 1.0, 0.0).astype(bf16)
    return jnp.where(inside, queries, one)


def attend_kernel(unit_max, chunk, count_ref, q_ref, k_ref, v_ref, o_ref, lse_ref, kb_ref, vt_ref):
    span = q_ref.shape[0]
    pair = 2 * HD
    lane = lax.broadcasted_iota(jnp.int32, (span, pair), 1)
    bias = live_bias(count_ref[0], span, unit_max)
    keys = k_ref[...]
    values_t = v_ref[...].T
    for head in range(2):
        kb_ref[head] = head_keys(keys, bias, lane, head)
        vt_ref[head, :HD] = values_t[head * HD : (head + 1) * HD]
        vt_ref[head, HD:] = jnp.ones((vt_ref.shape[1] - HD, span), bf16)
    lane_c = lane[:chunk]
    for begin in range(0, span, chunk):
        queries = q_ref[begin : begin + chunk, :]
        mixed = []
        for head in range(2):
            scores = right_dot(kb_ref[head], head_queries(queries, lane_c, head))
            top = jnp.max(scores, axis=0, keepdims=True)
            probs = jnp.exp(scores - top).astype(bf16)
            both = plain_dot(vt_ref[head], probs)
            total = both[HD : HD + 1]
            mixed.append(both[:HD] * (1.0 / total))
            lse_ref[0, head : head + 1, begin : begin + chunk] = top + jnp.log(total)
        o_ref[begin : begin + chunk, :] = jnp.concatenate(mixed, axis=0).T.astype(bf16)


def attend_forward(count, qkv, unit_max):
    span = qkv.shape[0]
    width = qkv.shape[1] // 3
    pair = 2 * HD
    pairs = width // pair

    def block(first):
        return pl.BlockSpec((span, pair), lambda p: (0, first + p))

    return pl.pallas_call(
        functools.partial(attend_kernel, unit_max, 512),
        grid=(pairs,),
        out_shape=(
            jax.ShapeDtypeStruct((span, width), bf16),
            jax.ShapeDtypeStruct((pairs, 8, span), f32),
        ),
        in_specs=[smem(), block(0), block(pairs), block(2 * pairs)],
        out_specs=(block(0), pl.BlockSpec((1, 8, span), lambda p: (p, 0, 0))),
        scratch_shapes=[
            pltpu.VMEM((2, span, pair), bf16),
            pltpu.VMEM((2, HD + 16, span), bf16),
        ],
        compiler_params=params(),
        cost_estimate=cost(4 * span * span * width, 8 << 20, span * span * H),
        name="attend_forward",
    )(count, qkv, qkv, qkv)


def out_kernel(x_ref, o_ref, w_ref, gain_ref, h_ref, n2_ref):
    parts, total, lanes = w_ref.shape
    width = h_ref.shape[1]
    rows = width // parts
    for c in range(width // lanes):
        weight = w_ref[:, c * rows : (c + 1) * rows, :].reshape(width, lanes)
        cols = slice(c * lanes, (c + 1) * lanes)
        h_ref[:, cols] = x_ref[:, cols].astype(f32) + plain_dot(o_ref[...], weight)
    hidden = h_ref[...]
    n2_ref[...] = (hidden * inverse_rms(hidden) * gain_ref[...]).astype(bf16)


def out_project(tokens, mixed, packed, gain, rows):
    span, width = tokens.shape
    parts = packed.shape[0]
    blocks = width // LANES
    return pl.pallas_call(
        out_kernel,
        grid=(1,),
        out_shape=(
            jax.ShapeDtypeStruct((span, width), f32),
            jax.ShapeDtypeStruct((span, width), bf16),
        ),
        in_specs=[
            const_block((span, width)),
            const_block((span, width)),
            pl.BlockSpec((parts, blocks * rows, LANES), lambda i: (0, 3, 0)),
            const_block((1, width)),
        ],
        out_specs=(const_block((span, width)), const_block((span, width))),
        compiler_params=params(),
        cost_estimate=cost(2 * span * width * width, 9 << 20),
        name="out_project",
    )(tokens, mixed, packed, gain)


def spread_gain(total, parts):
    width = total.shape[1]
    own = width // parts
    shape = (parts, GAIN_ROWS, LANES)
    part = lax.broadcasted_iota(jnp.int32, shape, 0)
    row = lax.broadcasted_iota(jnp.int32, shape, 1)
    place = row * LANES + lax.broadcasted_iota(jnp.int32, shape, 2)
    mine = (place >= part * own) & (place < (part + 1) * own)
    out = jnp.zeros(shape, f32)
    for c in range(width // LANES):
        piece = jnp.broadcast_to(total[:, c * LANES : (c + 1) * LANES][None], shape)
        out = jnp.where((row == c) & mine, piece, out)
    return out.astype(bf16)


def ffn_kernel(
    unit_max,
    count_ref,
    h_ref,
    n2_ref,
    d_ref,
    gain_ref,
    wg_ref,
    wu_ref,
    wd_ref,
    out_ref,
    gh_ref,
    ghb_ref,
    pack_ref,
    gb_ref,
    y_ref,
    gn_ref,
    stage_gate,
    stage_up,
    stage_down,
    stage_gain,
    sems,
):
    step = pl.program_id(0)
    steps = pl.num_programs(0)
    slot = lax.rem(step, 2)
    span, width = h_ref.shape
    parts, rows, _ = wg_ref.shape
    few, down_all, _ = wd_ref.shape
    cols = width // LANES
    down = down_all // cols
    ff_blocks = steps

    def copies(which, at):
        return (
            pltpu.make_async_copy(
                stage_gate.at[at],
                pack_ref.at[:, pl.ds(pl.multiple_of(which * rows, 8), rows), :],
                sems.at[0, at],
            ),
            pltpu.make_async_copy(
                stage_up.at[at],
                pack_ref.at[:, pl.ds(pl.multiple_of((ff_blocks + which) * rows, 8), rows), :],
                sems.at[1, at],
            ),
            pltpu.make_async_copy(
                stage_down.at[at],
                pack_ref.at[pl.ds(which * few, few), pl.ds(2 * ff_blocks * rows, down_all), :],
                sems.at[2, at],
            ),
        )

    row = lax.broadcasted_iota(jnp.int32, (span, 1), 0)
    live = lax.rem(row, unit_max) < count_ref[0]

    @pl.when(step == 0)
    def _():
        gb_ref[...] = jnp.where(live, d_ref[...].astype(f32), 0.0).astype(bf16)

    @pl.when(step >= 2)
    def _():
        for copy in copies(step - 2, slot):
            copy.wait()

    n2 = n2_ref[...]
    gb = gb_ref[...]
    w_gate = whole_block(wg_ref)
    w_up = whole_block(wu_ref)
    gate = plain_dot(n2, w_gate)
    up = plain_dot(n2, w_up)
    downs = [
        wd_ref[:, c * down : (c + 1) * down, :].reshape(few * down, LANES) for c in range(cols)
    ]
    g_act = right_dot(gb[:, :LANES], downs[0])
    for c in range(1, cols):
        g_act += right_dot(gb[:, c * LANES : (c + 1) * LANES], downs[c])
    c0 = 0.7978845608028654
    c1 = 0.044715
    square = gate * gate
    tang = jnp.tanh(c0 * gate * (1.0 + c1 * square))
    half = 0.5 * (1.0 + tang)
    gelu = gate * half
    slope = half + (0.5 * c0) * gate * (1.0 - tang * tang) * (1.0 + (3.0 * c1) * square)
    act = (gelu * up).astype(bf16)
    g_gate = (g_act * up * slope).astype(bf16)
    g_up = (g_act * gelu).astype(bf16)
    for c in range(cols):
        place = slice(c * LANES, (c + 1) * LANES)
        add = plain_dot(act, downs[c])
        grad = right_dot(g_gate, w_gate[place]) + right_dot(g_up, w_up[place])
        wide = left_dot(act, gb[:, place]).astype(bf16).reshape(few, down, LANES)
        stage_down[slot, :, c * down : (c + 1) * down, :] = wide

        @pl.when(step == 0)
        def _():
            y_ref[:, place] = add
            gn_ref[:, place] = grad

        @pl.when(step > 0)
        def _():
            y_ref[:, place] += add
            gn_ref[:, place] += grad

    stage_gate[slot] = left_dot(n2, g_gate).astype(bf16).reshape(parts, rows, LANES)
    stage_up[slot] = left_dot(n2, g_up).astype(bf16).reshape(parts, rows, LANES)
    for copy in copies(step, slot):
        copy.start()

    @pl.when(step == steps - 1)
    def _():
        hidden = h_ref[...]
        out_ref[...] = jnp.where(live, hidden + y_ref[...], 0.0).astype(bf16)
        inv = inverse_rms(hidden)
        grad = gn_ref[...]
        scaled = hidden * inv
        total = jnp.sum(grad * scaled, axis=0, keepdims=True)
        stage_gain[...] = spread_gain(total, parts)
        last = pltpu.make_async_copy(
            stage_gain,
            pack_ref.at[:, pl.ds(2 * ff_blocks * rows + down_all, GAIN_ROWS), :],
            sems.at[3, 0],
        )
        last.start()
        weighted = grad * gain_ref[...]
        mean = jnp.mean(scaled * weighted, axis=-1, keepdims=True)
        g_h = gb_ref[...].astype(f32) + inv * (weighted - scaled * mean)
        gh_ref[...] = g_h
        ghb_ref[...] = g_h.astype(bf16)
        for copy in copies(step - 1, 1 - slot) + copies(step, slot):
            copy.wait()
        last.wait()


def ffn_both(count, hidden, normed, d_rows, gain, packed, unit_max, rows, down):
    span, width = hidden.shape
    parts = packed.shape[0]
    ff = parts * down
    blocks = ff // LANES
    cols = width // LANES
    few = LANES // down
    moved = 2 * blocks * rows + cols * down
    full = const_block((span, width))
    return pl.pallas_call(
        functools.partial(ffn_kernel, unit_max),
        grid=(blocks,),
        out_shape=(
            jax.ShapeDtypeStruct((span, width), bf16),
            jax.ShapeDtypeStruct((span, width), f32),
            jax.ShapeDtypeStruct((span, width), bf16),
            jax.ShapeDtypeStruct((parts, moved + GAIN_ROWS, LANES), bf16),
        ),
        in_specs=[
            smem(),
            full,
            full,
            full,
            const_block((1, width)),
            pl.BlockSpec((parts, rows, LANES), lambda j: (0, j, 0)),
            pl.BlockSpec((parts, rows, LANES), lambda j: (0, blocks + j, 0)),
            pl.BlockSpec((few, cols * down, LANES), lambda j: (j, 2 * blocks * rows // (cols * down), 0)),
        ],
        out_specs=(full, full, full, pl.BlockSpec(memory_space=pl.ANY)),
        scratch_shapes=[
            pltpu.VMEM((span, width), bf16),
            pltpu.VMEM((span, width), f32),
            pltpu.VMEM((span, width), f32),
            pltpu.VMEM((2, parts, rows, LANES), bf16),
            pltpu.VMEM((2, parts, rows, LANES), bf16),
            pltpu.VMEM((2, few, cols * down, LANES), bf16),
            pltpu.VMEM((parts, GAIN_ROWS, LANES), bf16),
            pltpu.SemaphoreType.DMA((4, 2)),
        ],
        compiler_params=params(),
        cost_estimate=cost(18 * span * width * ff, 36 << 20, span * ff),
        name="ffn_both",
    )(count, hidden, normed, d_rows, gain, packed, packed, packed)


def attend_back_kernel(
    unit_max,
    chunk,
    count_ref,
    place_ref,
    q_ref,
    k_ref,
    v_ref,
    o_ref,
    lse_ref,
    n1_ref,
    x_ref,
    gh_ref,
    ghb_ref,
    gain_ref,
    wq_ref,
    wk_ref,
    wv_ref,
    wo_ref,
    gx_ref,
    keep_ref,
    send_ref,
    wo_s,
    do_s,
    delta_s,
    kt_s,
    dqt_s,
    dk_s,
    dv_s,
    gn_s,
    stage,
    stage_gain,
    sems,
    gain_sem,
):
    step = pl.program_id(0)
    steps = pl.num_programs(0)
    span, width = x_ref.shape
    parts, rows, _ = wq_ref.shape
    cols = width // LANES
    pair = 2 * HD
    heads = LANES // HD
    lane = lax.broadcasted_iota(jnp.int32, (span, pair), 1)
    lane_c = lane[:chunk]
    mine = pl.ds(pl.multiple_of(step * LANES, LANES), LANES)

    half_parts = parts // 2

    def copies(which):
        return [
            pltpu.make_async_copy(
                stage.at[m, pl.ds(side * half_parts, half_parts)],
                to_ref.at[:, pl.ds(pl.multiple_of((m * cols + which) * rows, 8), rows), :],
                sems.at[m, side],
            )
            for m in range(4)
            for side, to_ref in enumerate((keep_ref, send_ref))
        ]

    def put(m, grad):
        for part in range(parts):
            stage[m, place_ref[part]] = grad[part * rows : (part + 1) * rows].astype(bf16)

    @pl.when(step == 0)
    def _():
        for c in range(cols):
            wo_s[c] = wo_ref[:, c * rows : (c + 1) * rows, :].reshape(width, LANES)

    g_o = right_dot(ghb_ref[:, :LANES], wo_s[0, mine, :])
    for c in range(1, cols):
        g_o += right_dot(ghb_ref[:, c * LANES : (c + 1) * LANES], wo_s[c, mine, :])
    g_o = g_o.astype(bf16)
    do_s[...] = g_o
    prod = g_o.astype(f32) * o_ref[:, mine].astype(f32)
    high = prod.astype(bf16)
    low = (prod - high.astype(f32)).astype(bf16)
    picker = jnp.where(
        lax.broadcasted_iota(jnp.int32, (8, LANES), 1) // HD
        == lax.broadcasted_iota(jnp.int32, (8, LANES), 0),
        1.0,
        0.0,
    ).astype(bf16)
    delta_s[...] = right_dot(picker, high) + right_dot(picker, low)
    kt_s[...] = k_ref[...].T
    dk_s[...] = jnp.zeros_like(dk_s)
    dv_s[...] = jnp.zeros_like(dv_s)
    bias = live_bias(count_ref[0], span, unit_max)

    def one_head(head, carry):
        half = head // 2
        sub = lax.rem(head, 2)
        side = pl.ds(pl.multiple_of(half * pair, pair), pair)
        inside = (lane // HD) == sub
        inside_c = (lane_c // HD) == sub
        zero = jnp.zeros((), bf16)
        keys = head_keys(k_ref[:, side], bias, lane, sub)
        values = jnp.where(inside, v_ref[:, side], zero)
        keys_t = kt_s[pl.ds(pl.multiple_of(head * HD, HD), HD), :]
        d_k = None
        d_v = None
        for begin in range(0, span, chunk):
            part = slice(begin, begin + chunk)
            queries = q_ref[part, side]
            grads = do_s[part, side]
            scores = right_dot(keys, head_queries(queries, lane_c, sub))
            probs = jnp.exp(scores - lse_ref[half, pl.ds(sub, 1), part])
            d_probs = right_dot(values, grads)
            d_scores = (probs * (d_probs - delta_s[pl.ds(head, 1), part])).astype(bf16)
            add_v = plain_dot(probs.astype(bf16), jnp.where(inside_c, grads, zero))
            add_k = plain_dot(d_scores, jnp.where(inside_c, queries, zero))
            d_v = add_v if d_v is None else d_v + add_v
            d_k = add_k if d_k is None else d_k + add_k
            dqt_s[pl.ds(pl.multiple_of(head * HD, HD), HD), part] = plain_dot(keys_t, d_scores)
        dk_s[:, side] += d_k
        dv_s[:, side] += d_v
        return carry

    lax.fori_loop(0, heads, one_head, 0)
    d_q = (dqt_s[...].T * (HD ** (-0.5))).astype(bf16)
    d_k = dk_s[...].astype(bf16)
    d_v = dv_s[...].astype(bf16)

    add = (
        right_dot(d_q, whole_block(wq_ref))
        + right_dot(d_k, whole_block(wk_ref))
        + right_dot(d_v, whole_block(wv_ref))
    )

    @pl.when(step == 0)
    def _():
        gn_s[...] = add

    @pl.when(step > 0)
    def _():
        gn_s[...] += add
        for copy in copies(step - 1):
            copy.wait()

    n1 = n1_ref[...]
    for m, grad in enumerate((d_q, d_k, d_v)):
        put(m, left_dot(n1, grad))
    put(3, left_dot(o_ref[...], ghb_ref[:, mine]))
    for copy in copies(step):
        copy.start()

    @pl.when(step == steps - 1)
    def _():
        tokens = x_ref[...].astype(f32)
        inv = inverse_rms(tokens)
        grad = gn_s[...]
        scaled = tokens * inv
        total = jnp.sum(grad * scaled, axis=0, keepdims=True)
        spread = spread_gain(total, parts)
        for part in range(parts):
            stage_gain[place_ref[part]] = spread[part]
        last = [
            pltpu.make_async_copy(
                stage_gain.at[pl.ds(side * half_parts, half_parts)],
                to_ref.at[:, pl.ds(4 * cols * rows, GAIN_ROWS), :],
                gain_sem.at[side],
            )
            for side, to_ref in enumerate((keep_ref, send_ref))
        ]
        for copy in last:
            copy.start()
        weighted = grad * gain_ref[...]
        mean = jnp.mean(scaled * weighted, axis=-1, keepdims=True)
        gx_ref[...] = (gh_ref[...] + inv * (weighted - scaled * mean)).astype(bf16)
        for copy in copies(step) + last:
            copy.wait()


def attend_back(count, place, qkv, mixed, lse, n1, tokens, g_h, g_hb, gain, packed, unit_max, rows):
    span, width = tokens.shape
    parts = packed.shape[0]
    cols = width // LANES
    full = const_block((span, width))

    def block(first):
        return pl.BlockSpec((span, LANES), lambda p: (0, first + p))

    def weight(first):
        return pl.BlockSpec((parts, rows, LANES), lambda p: (0, first + p, 0))

    return pl.pallas_call(
        functools.partial(attend_back_kernel, unit_max, 512),
        grid=(cols,),
        out_shape=(
            jax.ShapeDtypeStruct((span, width), bf16),
            jax.ShapeDtypeStruct((parts // 2, 4 * cols * rows + GAIN_ROWS, LANES), bf16),
            jax.ShapeDtypeStruct((parts // 2, 4 * cols * rows + GAIN_ROWS, LANES), bf16),
        ),
        in_specs=[
            smem(),
            smem(),
            block(0),
            block(cols),
            block(2 * cols),
            full,
            pl.BlockSpec((2, 8, span), lambda p: (p, 0, 0)),
            full,
            full,
            full,
            full,
            const_block((1, width)),
            weight(0),
            weight(cols),
            weight(2 * cols),
            pl.BlockSpec((parts, cols * rows, LANES), lambda p: (0, 3, 0)),
        ],
        out_specs=(full, pl.BlockSpec(memory_space=pl.ANY), pl.BlockSpec(memory_space=pl.ANY)),
        scratch_shapes=[
            pltpu.VMEM((cols, width, LANES), bf16),
            pltpu.VMEM((span, LANES), bf16),
            pltpu.VMEM((8, span), f32),
            pltpu.VMEM((LANES, span), bf16),
            pltpu.VMEM((LANES, span), f32),
            pltpu.VMEM((span, LANES), f32),
            pltpu.VMEM((span, LANES), f32),
            pltpu.VMEM((span, width), f32),
            pltpu.VMEM((4, parts, rows, LANES), bf16),
            pltpu.VMEM((parts, GAIN_ROWS, LANES), bf16),
            pltpu.SemaphoreType.DMA((4, 2)),
            pltpu.SemaphoreType.DMA((2,)),
        ],
        compiler_params=params(),
        cost_estimate=cost(10 * span * span * width + 16 * span * width * width, 24 << 20, span * span * H),
        name="attend_back",
    )(count, place, qkv, qkv, qkv, mixed, lse, n1, tokens, g_h, g_hb, gain, packed, packed, packed, packed)


def finish_kernel(layout, own, gain_cols, halves, me_ref, mine_ref, other_ref, *outs):
    outs, sum_ref = outs[:-1], outs[-1]
    if halves:
        rows = mine_ref.shape[0]
        first = me_ref[1]
        sum_ref[pl.ds(pl.multiple_of(first * rows, 8), rows), :] = mine_ref[...].astype(f32)
        sum_ref[pl.ds(pl.multiple_of((1 - first) * rows, 8), rows), :] = other_ref[...].astype(f32)
    else:
        sum_ref[...] = mine_ref[...].astype(f32) + other_ref[...].astype(f32)
    begin = 0
    for (rows, blocks), out_ref in zip(layout, outs[:-1]):
        for c in range(blocks):
            out_ref[:, c * LANES : (c + 1) * LANES] = sum_ref[begin : begin + rows]
            begin += rows
    gains = sum_ref[begin : begin + GAIN_ROWS]
    row = lax.broadcasted_iota(jnp.int32, (GAIN_ROWS, own), 0)
    from_lane = lax.broadcasted_iota(jnp.int32, (LANES, own), 0)
    to_lane = lax.broadcasted_iota(jnp.int32, (LANES, own), 1)
    high = gains.astype(bf16)
    low = (gains - high.astype(f32)).astype(bf16)
    total = jnp.zeros((GAIN_ROWS, own), f32)
    for c in range(gain_cols):
        pick = jnp.where(from_lane + c * LANES == to_lane + me_ref[0] * own, 1.0, 0.0).astype(bf16)
        found = plain_dot(high, pick) + plain_dot(low, pick)
        total += jnp.where(row == c, found, 0.0)
    outs[-1][...] = jnp.sum(total, axis=0, keepdims=True)


def relative_places(shard_count):
    along = shard_count // 4
    mine = lax.axis_index("shard")
    part = jnp.arange(shard_count, dtype=jnp.int32)
    core = lax.rem(part, 2) ^ lax.rem(mine, 2)
    side = lax.rem(part // 2, 2) ^ lax.rem(mine // 2, 2)
    steps = lax.rem(part // 4 - mine // 4 + along, along)
    return (core * 2 + side) * along + steps


def to_core(value):
    count = lax.axis_size("shard")
    return lax.ppermute(value, "shard", [(i, i ^ 1) for i in range(count)])


def to_side(value):
    count = lax.axis_size("shard")
    return lax.ppermute(value, "shard", [(i, i ^ 2) for i in range(count)])


def along_z(value, step):
    count = lax.axis_size("shard")
    return lax.ppermute(value, "shard", [(i, (i + 4 * step) % count) for i in range(count)])


def scatter_queue(packed):
    return lax.psum_scatter(packed.reshape(-1, LANES), "shard", scatter_dimension=0, tiled=True)


def to_replica(value):
    return lax.ppermute(value, "replica", [(0, 1), (1, 0)])


def half_of(value, which):
    rows = value.shape[1] // 2
    return lax.dynamic_slice_in_dim(value, which * rows, rows, axis=1)


def scatter_permute(keep, send, later):
    along = keep.shape[0] // 2
    pair = lax.axis_size("replica") == 2
    came = to_core(send)
    parts = (keep, came)
    if pair:
        mine = lax.axis_index("replica")
        pass_y = sum(half_of(p, 1 - mine).astype(f32) for p in parts).astype(bf16)
        came_y = to_replica(pass_y)
        parts = tuple(half_of(p, mine) for p in parts) + (came_y,)
    pass_on = sum(p[along:].astype(f32) for p in parts).astype(bf16)
    crossed = to_side(pass_on)
    column = (sum(p[:along].astype(f32) for p in parts) + crossed.astype(f32)).astype(bf16)
    found = [along_z(column[k], k) for k in range(1, along)]
    total = column[0].astype(f32)
    for piece in found:
        total = total + piece.astype(f32)
    total, later = lax.optimization_barrier((total.astype(bf16), later))
    if pair:
        return total, to_replica(total), later
    return *replica_rounds(total), later


def replica_rounds(share):
    count = lax.axis_size("replica")
    step = 1
    other = jnp.zeros_like(share)
    while step < count:
        if step > 1:
            share = (share.astype(f32) + other.astype(f32)).astype(bf16)
        other = lax.ppermute(share, "replica", [(i, i ^ step) for i in range(count)])
        step *= 2
    return share, other


def finish(share, other, layout, own, parts, halves):
    me = jnp.stack([lax.axis_index("shard"), lax.axis_index("replica")]).astype(jnp.int32)
    rows = share.shape[0] * (2 if halves else 1)
    outs = pl.pallas_call(
        functools.partial(finish_kernel, layout, own, parts * own // LANES, halves),
        out_shape=tuple(jax.ShapeDtypeStruct((r, b * LANES), f32) for r, b in layout)
        + (jax.ShapeDtypeStruct((1, own), f32),),
        in_specs=[smem(), vmem(), vmem()],
        out_specs=(vmem(),) * (len(layout) + 1),
        scratch_shapes=[pltpu.VMEM((rows, LANES), f32)],
        compiler_params=params(),
        cost_estimate=cost(0, 4 << 20),
        name="finish",
    )(me, share, other)
    return outs[:-1] + (outs[-1][0],)


def to_blocks(mat, parts):
    rows = mat.shape[0] // parts
    cols = mat.shape[1] // LANES
    split = mat.reshape(parts, rows, cols, LANES).transpose(0, 2, 1, 3)
    return split.reshape(parts, cols * rows, LANES)


def pack_own(mats):
    return jnp.concatenate([to_blocks(m, 1)[0] for m in mats], axis=0)


def gather_queue(packed):
    whole = lax.all_gather(packed, "shard", axis=0, tiled=True)
    return whole.reshape(-1, packed.shape[0], LANES)


def shards(
    x_in,
    seq_units,
    deal,
    gain_attn,
    w_query,
    w_key,
    w_value,
    w_out,
    gain_ffn,
    w_gate,
    w_up,
    w_down,
    d_out,
):
    shard_count = lax.axis_size("shard")
    my_index = lax.axis_index("shard")
    given, width = x_in.shape[1:]
    span = d_out.shape[2]
    unit_max = span // shard_count
    rows = w_query.shape[0]
    down = w_down.shape[0]
    slot_ids = jnp.arange(shard_count, dtype=jnp.int32)
    outgoing = deal_rows(seq_units, deal, x_in[0], shard_count, unit_max)
    arrived = lax.all_to_all(outgoing, "shard", split_axis=0, concat_axis=0, tiled=True)
    own_seq = jnp.sum(jnp.where(slot_ids == my_index, deal[0], 0))
    count = jnp.sum(jnp.where(slot_ids == own_seq, seq_units[0], 0)).reshape(1)
    attn_own = pack_own((w_query, w_key, w_value, w_out))
    column = [along_z(attn_own, k) for k in range(1, shard_count // 4)]
    ffn_own = pack_own((w_gate, w_up, w_down))
    ffn_own, attn_own, _, *column = lax.optimization_barrier((ffn_own, attn_own, outgoing, *column))
    ffn_pack = gather_queue(ffn_own)
    here = jnp.stack([attn_own, *column])
    beside = to_side(here)
    pieces = (here, beside, to_core(here), to_core(beside))
    tokens = arrived.reshape(span, width)
    gain_one = gain_attn.reshape(1, width)
    gain_two = gain_ffn.reshape(1, width)
    n1, qkv, attn_pack = make_qkv(
        lax.axis_index("shard").reshape(1), tokens, gain_one, pieces, rows
    )
    mixed, lse = attend_forward(count, qkv, unit_max)
    hidden, n2 = out_project(tokens, mixed, attn_pack, gain_two, rows)
    layer_out, g_h, g_hb, ffn_grads = ffn_both(
        count, hidden, n2, d_out[0, 0], gain_two, ffn_pack, unit_max, rows, down
    )
    own = width // shard_count
    cols = width // LANES
    wide = w_gate.shape[1] // LANES
    ffn_share = scatter_queue(ffn_grads)
    place = relative_places(shard_count)
    g_x, keep, send = attend_back(
        count, place, qkv, mixed, lse, n1, tokens, g_h, g_hb, gain_one, attn_pack, unit_max, rows
    )
    returned = lax.all_to_all(
        g_x.reshape(shard_count, unit_max, width), "shard", split_axis=0, concat_axis=0, tiled=True
    )
    grad_x = undeal_rows(seq_units, deal, returned, given)[None]
    attn_mine, attn_other, ffn_share = scatter_permute(keep, send, ffn_share)
    out_wq, out_wk, out_wv, out_wo, out_gain_one = finish(
        attn_mine,
        attn_other,
        ((rows, cols),) * 4,
        own,
        shard_count,
        lax.axis_size("replica") == 2,
    )
    out_wg, out_wu, out_wd, out_gain_two = finish(
        *replica_rounds(ffn_share),
        ((rows, wide), (rows, wide), (down, cols)),
        own,
        shard_count,
        False,
    )
    return (
        layer_out.reshape(1, 1, span, width),
        grad_x,
        out_gain_one,
        out_gain_two,
        out_wq,
        out_wk,
        out_wv,
        out_wo,
        out_wg,
        out_wu,
        out_wd,
    )


def solution(mesh):
    return jax.shard_map(
        shards,
        mesh=mesh,
        in_specs=(
            P("replica", "shard", None),
            P("replica", None),
            P("replica", None),
            P(),
            P("shard", None),
            P("shard", None),
            P("shard", None),
            P("shard", None),
            P(),
            P("shard", None),
            P("shard", None),
            P("shard", None),
            P("replica", "shard", None, None),
        ),
        out_specs=(
            P("replica", "shard", None, None),
            P("replica", "shard", None),
            P("shard"),
            P("shard"),
            P("shard", None),
            P("shard", None),
            P("shard", None),
            P("shard", None),
            P("shard", None),
            P("shard", None),
            P("shard", None),
        ),
        check_vma=False,
    )
```

```python
import functools

import jax
import jax.numpy as jnp
from jax import lax
from jax.experimental import pallas as pl
from jax.experimental.pallas import tpu as pltpu
from jax.sharding import PartitionSpec as P

H = 12
HD = 64
LANES = 256
GAIN_ROWS = 16

norm_eps = 1e-06
neg_big = -1e30
bf16 = jnp.bfloat16
f32 = jnp.float32


def left_dot(lhs_mat, rhs_mat):
    return lax.dot_general(
        lhs_mat, rhs_mat, (((0,), (0,)), ((), ())), preferred_element_type=jnp.float32
    )


def right_dot(lhs_mat, rhs_mat):
    return lax.dot_general(
        lhs_mat, rhs_mat, (((1,), (1,)), ((), ())), preferred_element_type=jnp.float32
    )


def plain_dot(lhs_mat, rhs_mat):
    return jnp.dot(lhs_mat, rhs_mat, preferred_element_type=jnp.float32)


def slot_start(units_ref, order_ref, slot, shard_count):
    wanted = order_ref[0, slot]
    start = jnp.int32(0)
    count = jnp.int32(0)
    for k in range(shard_count):
        units = units_ref[0, k]
        start = start + jnp.where(k < wanted, units, 0)
        count = count + jnp.where(k == wanted, units, 0)
    return start, count


def pick_rows(units_ref, order_ref, pick_ref, shard_count, unit_max):
    given = pick_ref.shape[1]
    row = lax.broadcasted_iota(jnp.int32, (unit_max, given), 0)
    ahead = lax.broadcasted_iota(jnp.int32, (unit_max, given), 1) - row

    def step(slot, carry):
        start, count = slot_start(units_ref, order_ref, slot, shard_count)
        pick = jnp.where((ahead == start) & (row < count), 1.0, 0.0).astype(bf16)
        pick_ref[pl.ds(pl.multiple_of(slot * unit_max, unit_max), unit_max), :] = pick
        return carry

    lax.fori_loop(0, shard_count, step, 0)


def deal_kernel(units_ref, order_ref, rows_ref, out_ref, pick_ref):
    shard_count, unit_max, width = out_ref.shape
    pick_rows(units_ref, order_ref, pick_ref, shard_count, unit_max)
    found = plain_dot(pick_ref[...], rows_ref[...]).astype(bf16)
    out_ref[...] = found.reshape(shard_count, unit_max, width)


def undeal_kernel(units_ref, order_ref, back_ref, out_ref, pick_ref):
    shard_count, unit_max, width = back_ref.shape
    pick_rows(units_ref, order_ref, pick_ref, shard_count, unit_max)
    whole = back_ref[...].reshape(shard_count * unit_max, width)
    out_ref[...] = left_dot(pick_ref[...], whole).astype(bf16)


def smem():
    return pl.BlockSpec(memory_space=pltpu.SMEM)


def vmem():
    return pl.BlockSpec(memory_space=pltpu.VMEM)


def deal_rows(units, order, rows, shard_count, unit_max):
    return pl.pallas_call(
        deal_kernel,
        out_shape=jax.ShapeDtypeStruct((shard_count, unit_max, rows.shape[1]), bf16),
        in_specs=[smem(), smem(), vmem()],
        out_specs=vmem(),
        scratch_shapes=[pltpu.VMEM((shard_count * unit_max, rows.shape[0]), bf16)],
        name="deal_rows",
    )(units, order, rows)


def undeal_rows(units, order, back, given):
    shard_count, unit_max, width = back.shape
    return pl.pallas_call(
        undeal_kernel,
        out_shape=jax.ShapeDtypeStruct((given, width), bf16),
        in_specs=[smem(), smem(), vmem()],
        out_specs=vmem(),
        scratch_shapes=[pltpu.VMEM((shard_count * unit_max, given), bf16)],
        name="undeal_rows",
    )(units, order, back)


def const_block(shape):
    zeros = (0,) * len(shape)
    return pl.BlockSpec(shape, lambda *_: zeros)


def params():
    return pltpu.CompilerParams(vmem_limit_bytes=60 << 20)


def cost(flops, moved, trans=0):
    return pl.CostEstimate(flops=flops, bytes_accessed=moved, transcendentals=trans)


def inverse_rms(rows):
    return lax.rsqrt(jnp.mean(rows * rows, axis=-1, keepdims=True) + norm_eps)


def whole_block(ref):
    parts, rows, lanes = ref.shape
    return ref[...].reshape(parts * rows, lanes)


def qkv_kernel(me_ref, x_ref, gain_ref, a_ref, b_ref, fa_ref, fb_ref, n1_ref, qkv_ref, w_ref):
    block = pl.program_id(0)
    along = a_ref.shape[0]
    width = n1_ref.shape[1]
    me = me_ref[0]
    core = lax.rem(me, 2)
    side = lax.rem(lax.div(me, 2), 2)
    height = lax.div(me, 4)

    @pl.when(block == 0)
    def _():
        rows = x_ref[...].astype(f32)
        n1_ref[...] = (rows * inverse_rms(rows) * gain_ref[...]).astype(bf16)

    for step in range(along):
        there = lax.rem(height - step + along, along) * 4
        w_ref[there + 2 * side + core] = a_ref[step]
        w_ref[there + 2 * side + 1 - core] = fa_ref[step]
        w_ref[there + 2 * (1 - side) + core] = b_ref[step]
        w_ref[there + 2 * (1 - side) + 1 - core] = fb_ref[step]

    @pl.when(block < 3)
    def _():
        factor = jnp.where(block == 0, HD ** (-0.5), 1.0)
        cols = width // LANES
        rows = w_ref.shape[1] // cols
        for c in range(cols):
            weight = w_ref[:, c * rows : (c + 1) * rows, :].reshape(width, LANES)
            made = plain_dot(n1_ref[...], weight).astype(bf16).astype(f32)
            qkv_ref[:, c * LANES : (c + 1) * LANES] = (made * factor).astype(bf16)


def make_qkv(me, tokens, gain, pieces, rows):
    span, width = tokens.shape
    along = pieces[0].shape[0]
    cols = width // LANES
    piece = pl.BlockSpec((along, cols * rows, LANES), lambda j: (0, j, 0))
    return pl.pallas_call(
        qkv_kernel,
        grid=(4,),
        out_shape=(
            jax.ShapeDtypeStruct((span, width), bf16),
            jax.ShapeDtypeStruct((span, 3 * width), bf16),
            jax.ShapeDtypeStruct((4 * along, 4 * cols * rows, LANES), bf16),
        ),
        in_specs=[
            smem(),
            const_block((span, width)),
            const_block((1, width)),
            piece,
            piece,
            piece,
            piece,
        ],
        out_specs=(
            const_block((span, width)),
            pl.BlockSpec((span, width), lambda j: (0, jnp.minimum(j, 2))),
            pl.BlockSpec((4 * along, cols * rows, LANES), lambda j: (0, j, 0)),
        ),
        compiler_params=params(),
        cost_estimate=cost(6 * span * width * width, 14 << 20),
        name="make_qkv",
    )(me, tokens, gain, *pieces)


def live_bias(count, span, unit_max):
    row = lax.broadcasted_iota(jnp.int32, (span, 2 * HD), 0)
    return jnp.where(lax.rem(row, unit_max) < count, 0.0, neg_big).astype(bf16)


def head_keys(keys, bias, lane, head):
    inside = (lane // HD) == head
    return jnp.where(inside, keys, jnp.where(lane == (1 - head) * HD, bias, jnp.zeros_like(keys)))


def head_queries(queries, lane, head):
    inside = (lane // HD) == head
    one = jnp.where(lane == (1 - head) * HD, 1.0, 0.0).astype(bf16)
    return jnp.where(inside, queries, one)


def attend_kernel(unit_max, chunk, count_ref, q_ref, k_ref, v_ref, o_ref, lse_ref, kb_ref, vt_ref, ot_ref):
    span = q_ref.shape[0]
    pair = 2 * HD
    lane = lax.broadcasted_iota(jnp.int32, (span, pair), 1)
    bias = live_bias(count_ref[0], span, unit_max)
    keys = k_ref[...]
    values_t = v_ref[...].T
    for head in range(2):
        kb_ref[head] = head_keys(keys, bias, lane, head)
        vt_ref[head, :HD] = values_t[head * HD : (head + 1) * HD]
        vt_ref[head, HD:] = jnp.ones((vt_ref.shape[1] - HD, span), bf16)
    lane_c = lane[:chunk]
    jobs = [(head, begin) for begin in range(0, span, chunk) for head in range(2)]

    def first(job):
        head, begin = job
        return right_dot(kb_ref[head], head_queries(q_ref[begin : begin + chunk, :], lane_c, head))

    def second(job, scores):
        head, begin = job
        part = slice(begin, begin + chunk)
        top = jnp.max(scores, axis=0, keepdims=True)
        probs = jnp.exp(scores - top).astype(bf16)
        both = plain_dot(vt_ref[head], probs)
        total = both[HD : HD + 1]
        ot_ref[head * HD : (head + 1) * HD, part] = both[:HD] * (1.0 / total)
        lse_ref[0, head : head + 1, part] = top + jnp.log(total)

    held = first(jobs[0])
    for i, job in enumerate(jobs):
        later = first(jobs[i + 1]) if i + 1 < len(jobs) else None
        second(job, held)
        held = later
    o_ref[...] = ot_ref[...].T.astype(bf16)


def attend_forward(count, qkv, unit_max):
    span = qkv.shape[0]
    width = qkv.shape[1] // 3
    pair = 2 * HD
    pairs = width // pair

    def block(first):
        return pl.BlockSpec((span, pair), lambda p: (0, first + p))

    return pl.pallas_call(
        functools.partial(attend_kernel, unit_max, 1024),
        grid=(pairs,),
        out_shape=(
            jax.ShapeDtypeStruct((span, width), bf16),
            jax.ShapeDtypeStruct((pairs, 8, span), f32),
        ),
        in_specs=[smem(), block(0), block(pairs), block(2 * pairs)],
        out_specs=(block(0), pl.BlockSpec((1, 8, span), lambda p: (p, 0, 0))),
        scratch_shapes=[
            pltpu.VMEM((2, span, pair), bf16),
            pltpu.VMEM((2, HD + 16, span), bf16),
            pltpu.VMEM((pair, span), f32),
        ],
        compiler_params=params(),
        cost_estimate=cost(4 * span * span * width, 8 << 20, span * span * H),
        name="attend_forward",
    )(count, qkv, qkv, qkv)


def out_kernel(x_ref, o_ref, w_ref, gain_ref, h_ref, n2_ref):
    parts, total, lanes = w_ref.shape
    width = h_ref.shape[1]
    rows = width // parts
    for c in range(width // lanes):
        weight = w_ref[:, c * rows : (c + 1) * rows, :].reshape(width, lanes)
        cols = slice(c * lanes, (c + 1) * lanes)
        h_ref[:, cols] = x_ref[:, cols].astype(f32) + plain_dot(o_ref[...], weight)
    hidden = h_ref[...]
    n2_ref[...] = (hidden * inverse_rms(hidden) * gain_ref[...]).astype(bf16)


def out_project(tokens, mixed, packed, gain, rows):
    span, width = tokens.shape
    parts = packed.shape[0]
    blocks = width // LANES
    return pl.pallas_call(
        out_kernel,
        grid=(1,),
        out_shape=(
            jax.ShapeDtypeStruct((span, width), f32),
            jax.ShapeDtypeStruct((span, width), bf16),
        ),
        in_specs=[
            const_block((span, width)),
            const_block((span, width)),
            pl.BlockSpec((parts, blocks * rows, LANES), lambda i: (0, 3, 0)),
            const_block((1, width)),
        ],
        out_specs=(const_block((span, width)), const_block((span, width))),
        compiler_params=params(),
        cost_estimate=cost(2 * span * width * width, 9 << 20),
        name="out_project",
    )(tokens, mixed, packed, gain)


def spread_gain(total, parts):
    width = total.shape[1]
    own = width // parts
    shape = (parts, GAIN_ROWS, LANES)
    part = lax.broadcasted_iota(jnp.int32, shape, 0)
    row = lax.broadcasted_iota(jnp.int32, shape, 1)
    place = row * LANES + lax.broadcasted_iota(jnp.int32, shape, 2)
    mine = (place >= part * own) & (place < (part + 1) * own)
    out = jnp.zeros(shape, f32)
    for c in range(width // LANES):
        piece = jnp.broadcast_to(total[:, c * LANES : (c + 1) * LANES][None], shape)
        out = jnp.where((row == c) & mine, piece, out)
    return out.astype(bf16)


def ffn_kernel(
    unit_max,
    count_ref,
    h_ref,
    n2_ref,
    d_ref,
    gain_ref,
    wg_ref,
    wu_ref,
    wd_ref,
    out_ref,
    gh_ref,
    ghb_ref,
    pack_ref,
    gb_ref,
    y_ref,
    gn_ref,
    stage_gate,
    stage_up,
    stage_down,
    stage_gain,
    act_s,
    gg_s,
    gu_s,
    sems,
):
    step = pl.program_id(0)
    steps = pl.num_programs(0)
    slot = lax.rem(step, 2)
    span, width = h_ref.shape
    parts, rows, _ = wg_ref.shape
    few, down_all, _ = wd_ref.shape
    cols = width // LANES
    down = down_all // cols
    ff_blocks = steps

    def copies(which, at):
        return (
            pltpu.make_async_copy(
                stage_gate.at[at],
                pack_ref.at[:, pl.ds(pl.multiple_of(which * rows, 8), rows), :],
                sems.at[0, at],
            ),
            pltpu.make_async_copy(
                stage_up.at[at],
                pack_ref.at[:, pl.ds(pl.multiple_of((ff_blocks + which) * rows, 8), rows), :],
                sems.at[1, at],
            ),
            pltpu.make_async_copy(
                stage_down.at[at],
                pack_ref.at[pl.ds(which * few, few), pl.ds(2 * ff_blocks * rows, down_all), :],
                sems.at[2, at],
            ),
        )

    row = lax.broadcasted_iota(jnp.int32, (span, 1), 0)
    live = lax.rem(row, unit_max) < count_ref[0]

    @pl.when(step == 0)
    def _():
        gb_ref[...] = jnp.where(live, d_ref[...].astype(f32), 0.0).astype(bf16)
        y_ref[...] = jnp.zeros_like(y_ref)
        gn_ref[...] = jnp.zeros_like(gn_ref)

    @pl.when(step >= 2)
    def _():
        for copy in copies(step - 2, slot):
            copy.wait()

    w_gate = whole_block(wg_ref)
    w_up = whole_block(wu_ref)
    downs = [
        wd_ref[:, c * down : (c + 1) * down, :].reshape(few * down, LANES) for c in range(cols)
    ]
    chunk = span // 2

    def first(part):
        n2 = n2_ref[part, :]
        gate = plain_dot(n2, w_gate)
        up = plain_dot(n2, w_up)
        g_act = right_dot(gb_ref[part, :LANES], downs[0])
        for c in range(1, cols):
            g_act += right_dot(gb_ref[part, c * LANES : (c + 1) * LANES], downs[c])
        return gate, up, g_act

    def middle(part, gate, up, g_act):
        c0 = 0.7978845608028654
        c1 = 0.044715
        square = gate * gate
        inner = c0 + (c0 * c1) * square
        tang = jnp.tanh(gate * inner)
        half = 0.5 + 0.5 * tang
        gelu = gate * half
        slope = half + (gate * (0.5 - 0.5 * tang * tang)) * (c0 + (3.0 * c0 * c1) * square)
        act_s[part, :] = (gelu * up).astype(bf16)
        gg_s[part, :] = (g_act * up * slope).astype(bf16)
        gu_s[part, :] = (g_act * gelu).astype(bf16)

    def second(part):
        for c in range(cols):
            place = slice(c * LANES, (c + 1) * LANES)
            add = plain_dot(act_s[part, :], downs[c])
            grad = right_dot(gg_s[part, :], w_gate[place]) + right_dot(gu_s[part, :], w_up[place])
            y_ref[part, place] += add
            gn_ref[part, place] += grad

    parts_of = [slice(i * chunk, (i + 1) * chunk) for i in range(2)]
    held = first(parts_of[0])
    for i, part in enumerate(parts_of):
        later = first(parts_of[i + 1]) if i + 1 < len(parts_of) else None
        middle(part, *held)
        second(part)
        held = later
    for c in range(cols):
        wide = left_dot(act_s[...], gb_ref[:, c * LANES : (c + 1) * LANES]).astype(bf16)
        stage_down[slot, :, c * down : (c + 1) * down, :] = wide.reshape(few, down, LANES)
    stage_gate[slot] = left_dot(n2_ref[...], gg_s[...]).astype(bf16).reshape(parts, rows, LANES)
    stage_up[slot] = left_dot(n2_ref[...], gu_s[...]).astype(bf16).reshape(parts, rows, LANES)
    for copy in copies(step, slot):
        copy.start()

    @pl.when(step == steps - 1)
    def _():
        hidden = h_ref[...]
        out_ref[...] = jnp.where(live, hidden + y_ref[...], 0.0).astype(bf16)
        inv = inverse_rms(hidden)
        grad = gn_ref[...]
        scaled = hidden * inv
        total = jnp.sum(grad * scaled, axis=0, keepdims=True)
        stage_gain[...] = spread_gain(total, parts)
        last = pltpu.make_async_copy(
            stage_gain,
            pack_ref.at[:, pl.ds(2 * ff_blocks * rows + down_all, GAIN_ROWS), :],
            sems.at[3, 0],
        )
        last.start()
        weighted = grad * gain_ref[...]
        mean = jnp.mean(scaled * weighted, axis=-1, keepdims=True)
        g_h = gb_ref[...].astype(f32) + inv * (weighted - scaled * mean)
        gh_ref[...] = g_h
        ghb_ref[...] = g_h.astype(bf16)
        for copy in copies(step - 1, 1 - slot) + copies(step, slot):
            copy.wait()
        last.wait()


def ffn_both(count, hidden, normed, d_rows, gain, packed, unit_max, rows, down):
    span, width = hidden.shape
    parts = packed.shape[0]
    ff = parts * down
    blocks = ff // LANES
    cols = width // LANES
    few = LANES // down
    moved = 2 * blocks * rows + cols * down
    full = const_block((span, width))
    return pl.pallas_call(
        functools.partial(ffn_kernel, unit_max),
        grid=(blocks,),
        out_shape=(
            jax.ShapeDtypeStruct((span, width), bf16),
            jax.ShapeDtypeStruct((span, width), f32),
            jax.ShapeDtypeStruct((span, width), bf16),
            jax.ShapeDtypeStruct((parts, moved + GAIN_ROWS, LANES), bf16),
        ),
        in_specs=[
            smem(),
            full,
            full,
            full,
            const_block((1, width)),
            pl.BlockSpec((parts, rows, LANES), lambda j: (0, j, 0)),
            pl.BlockSpec((parts, rows, LANES), lambda j: (0, blocks + j, 0)),
            pl.BlockSpec((few, cols * down, LANES), lambda j: (j, 2 * blocks * rows // (cols * down), 0)),
        ],
        out_specs=(full, full, full, pl.BlockSpec(memory_space=pl.ANY)),
        scratch_shapes=[
            pltpu.VMEM((span, width), bf16),
            pltpu.VMEM((span, width), f32),
            pltpu.VMEM((span, width), f32),
            pltpu.VMEM((2, parts, rows, LANES), bf16),
            pltpu.VMEM((2, parts, rows, LANES), bf16),
            pltpu.VMEM((2, few, cols * down, LANES), bf16),
            pltpu.VMEM((parts, GAIN_ROWS, LANES), bf16),
            pltpu.VMEM((span, LANES), bf16),
            pltpu.VMEM((span, LANES), bf16),
            pltpu.VMEM((span, LANES), bf16),
            pltpu.SemaphoreType.DMA((4, 2)),
        ],
        compiler_params=params(),
        cost_estimate=cost(18 * span * width * ff, 36 << 20, span * ff),
        name="ffn_both",
    )(count, hidden, normed, d_rows, gain, packed, packed, packed)


def attend_back_kernel(
    unit_max,
    chunk,
    count_ref,
    place_ref,
    q_ref,
    k_ref,
    v_ref,
    o_ref,
    lse_ref,
    n1_ref,
    x_ref,
    gh_ref,
    ghb_ref,
    gain_ref,
    wq_ref,
    wk_ref,
    wv_ref,
    wo_ref,
    gx_ref,
    keep_ref,
    send_ref,
    wo_s,
    do_s,
    delta_s,
    kt_s,
    dqt_s,
    dk_s,
    dv_s,
    gn_s,
    stage,
    stage_gain,
    sems,
    gain_sem,
):
    step = pl.program_id(0)
    steps = pl.num_programs(0)
    span, width = x_ref.shape
    parts, rows, _ = wq_ref.shape
    cols = width // LANES
    pair = 2 * HD
    heads = LANES // HD
    lane = lax.broadcasted_iota(jnp.int32, (span, pair), 1)
    lane_c = lane[:chunk]
    mine = pl.ds(pl.multiple_of(step * LANES, LANES), LANES)

    half_parts = parts // 2

    def copies(which):
        return [
            pltpu.make_async_copy(
                stage.at[m, pl.ds(side * half_parts, half_parts)],
                to_ref.at[:, pl.ds(pl.multiple_of((m * cols + which) * rows, 8), rows), :],
                sems.at[m, side],
            )
            for m in range(4)
            for side, to_ref in enumerate((keep_ref, send_ref))
        ]

    def put(m, grad):
        for part in range(parts):
            stage[m, place_ref[part]] = grad[part * rows : (part + 1) * rows].astype(bf16)

    @pl.when(step == 0)
    def _():
        gn_s[...] = jnp.zeros_like(gn_s)
        for c in range(cols):
            wo_s[c] = wo_ref[:, c * rows : (c + 1) * rows, :].reshape(width, LANES)

    g_o = right_dot(ghb_ref[:, :LANES], wo_s[0, mine, :])
    for c in range(1, cols):
        g_o += right_dot(ghb_ref[:, c * LANES : (c + 1) * LANES], wo_s[c, mine, :])
    g_o = g_o.astype(bf16)
    do_s[...] = g_o
    prod = g_o.astype(f32) * o_ref[:, mine].astype(f32)
    high = prod.astype(bf16)
    low = (prod - high.astype(f32)).astype(bf16)
    picker = jnp.where(
        lax.broadcasted_iota(jnp.int32, (8, LANES), 1) // HD
        == lax.broadcasted_iota(jnp.int32, (8, LANES), 0),
        1.0,
        0.0,
    ).astype(bf16)
    delta_s[...] = right_dot(picker, high) + right_dot(picker, low)
    kt_s[...] = k_ref[...].T
    dk_s[...] = jnp.zeros_like(dk_s)
    dv_s[...] = jnp.zeros_like(dv_s)
    bias = live_bias(count_ref[0], span, unit_max)

    zero = jnp.zeros((), bf16)

    def some_heads(turn, carry):
        jobs = []
        for u in range(2):
            head = turn * 2 + u
            half = head // 2
            sub = u % 2 if 2 > 1 else lax.rem(head, 2)
            side = pl.ds(pl.multiple_of(half * pair, pair), pair)
            inside = (lane // HD) == sub
            keys = head_keys(k_ref[:, side], bias, lane, sub)
            values = jnp.where(inside, v_ref[:, side], zero)
            for begin in range(0, span, chunk):
                jobs.append((head, half, sub, side, keys, values, slice(begin, begin + chunk)))

        def first(job):
            head, half, sub, side, keys, values, part = job
            scores = right_dot(keys, head_queries(q_ref[part, side], lane_c, sub))
            d_probs = right_dot(values, do_s[part, side])
            return scores, d_probs

        def second(job, scores, d_probs):
            head, half, sub, side, keys, values, part = job
            inside_c = (lane_c // HD) == sub
            probs = jnp.exp(scores - lse_ref[half, pl.ds(sub, 1), part])
            d_scores = (probs * (d_probs - delta_s[pl.ds(head, 1), part])).astype(bf16)
            dv_s[:, side] += plain_dot(probs.astype(bf16), jnp.where(inside_c, do_s[part, side], zero))
            dk_s[:, side] += plain_dot(d_scores, jnp.where(inside_c, q_ref[part, side], zero))
            rows_t = pl.ds(pl.multiple_of(head * HD, HD), HD)
            dqt_s[rows_t, part] = plain_dot(kt_s[rows_t, :], d_scores)

        held = first(jobs[0])
        for i, job in enumerate(jobs):
            later = first(jobs[i + 1]) if i + 1 < len(jobs) else None
            second(job, *held)
            held = later
        return carry

    lax.fori_loop(0, heads // 2, some_heads, 0)
    d_q = (dqt_s[...].T * (HD ** (-0.5))).astype(bf16)
    d_k = dk_s[...].astype(bf16)
    d_v = dv_s[...].astype(bf16)

    add = (
        right_dot(d_q, whole_block(wq_ref))
        + right_dot(d_k, whole_block(wk_ref))
        + right_dot(d_v, whole_block(wv_ref))
    )

    gn_s[...] += add

    @pl.when(step > 0)
    def _():
        for copy in copies(step - 1):
            copy.wait()

    n1 = n1_ref[...]
    for m, grad in enumerate((d_q, d_k, d_v)):
        put(m, left_dot(n1, grad))
    put(3, left_dot(o_ref[...], ghb_ref[:, mine]))
    for copy in copies(step):
        copy.start()

    @pl.when(step == steps - 1)
    def _():
        tokens = x_ref[...].astype(f32)
        inv = inverse_rms(tokens)
        grad = gn_s[...]
        scaled = tokens * inv
        total = jnp.sum(grad * scaled, axis=0, keepdims=True)
        spread = spread_gain(total, parts)
        for part in range(parts):
            stage_gain[place_ref[part]] = spread[part]
        last = [
            pltpu.make_async_copy(
                stage_gain.at[pl.ds(side * half_parts, half_parts)],
                to_ref.at[:, pl.ds(4 * cols * rows, GAIN_ROWS), :],
                gain_sem.at[side],
            )
            for side, to_ref in enumerate((keep_ref, send_ref))
        ]
        for copy in last:
            copy.start()
        weighted = grad * gain_ref[...]
        mean = jnp.mean(scaled * weighted, axis=-1, keepdims=True)
        gx_ref[...] = (gh_ref[...] + inv * (weighted - scaled * mean)).astype(bf16)
        for copy in copies(step) + last:
            copy.wait()


def attend_back(count, place, qkv, mixed, lse, n1, tokens, g_h, g_hb, gain, packed, unit_max, rows):
    span, width = tokens.shape
    parts = packed.shape[0]
    cols = width // LANES
    full = const_block((span, width))

    def block(first):
        return pl.BlockSpec((span, LANES), lambda p: (0, first + p))

    def weight(first):
        return pl.BlockSpec((parts, rows, LANES), lambda p: (0, first + p, 0))

    return pl.pallas_call(
        functools.partial(attend_back_kernel, unit_max, 512),
        grid=(cols,),
        out_shape=(
            jax.ShapeDtypeStruct((span, width), bf16),
            jax.ShapeDtypeStruct((parts // 2, 4 * cols * rows + GAIN_ROWS, LANES), bf16),
            jax.ShapeDtypeStruct((parts // 2, 4 * cols * rows + GAIN_ROWS, LANES), bf16),
        ),
        in_specs=[
            smem(),
            smem(),
            block(0),
            block(cols),
            block(2 * cols),
            full,
            pl.BlockSpec((2, 8, span), lambda p: (p, 0, 0)),
            full,
            full,
            full,
            full,
            const_block((1, width)),
            weight(0),
            weight(cols),
            weight(2 * cols),
            pl.BlockSpec((parts, cols * rows, LANES), lambda p: (0, 3, 0)),
        ],
        out_specs=(full, pl.BlockSpec(memory_space=pl.ANY), pl.BlockSpec(memory_space=pl.ANY)),
        scratch_shapes=[
            pltpu.VMEM((cols, width, LANES), bf16),
            pltpu.VMEM((span, LANES), bf16),
            pltpu.VMEM((8, span), f32),
            pltpu.VMEM((LANES, span), bf16),
            pltpu.VMEM((LANES, span), f32),
            pltpu.VMEM((span, LANES), f32),
            pltpu.VMEM((span, LANES), f32),
            pltpu.VMEM((span, width), f32),
            pltpu.VMEM((4, parts, rows, LANES), bf16),
            pltpu.VMEM((parts, GAIN_ROWS, LANES), bf16),
            pltpu.SemaphoreType.DMA((4, 2)),
            pltpu.SemaphoreType.DMA((2,)),
        ],
        compiler_params=params(),
        cost_estimate=cost(10 * span * span * width + 16 * span * width * width, 24 << 20, span * span * H),
        name="attend_back",
    )(count, place, qkv, qkv, qkv, mixed, lse, n1, tokens, g_h, g_hb, gain, packed, packed, packed, packed)


def finish_kernel(layout, own, gain_cols, halves, me_ref, mine_ref, other_ref, *outs):
    outs, sum_ref = outs[:-1], outs[-1]
    if halves:
        rows = mine_ref.shape[0]
        first = me_ref[1]
        sum_ref[pl.ds(pl.multiple_of(first * rows, 8), rows), :] = mine_ref[...].astype(f32)
        sum_ref[pl.ds(pl.multiple_of((1 - first) * rows, 8), rows), :] = other_ref[...].astype(f32)
    else:
        sum_ref[...] = mine_ref[...].astype(f32) + other_ref[...].astype(f32)
    begin = 0
    for (rows, blocks), out_ref in zip(layout, outs[:-1]):
        for c in range(blocks):
            out_ref[:, c * LANES : (c + 1) * LANES] = sum_ref[begin : begin + rows]
            begin += rows
    gains = sum_ref[begin : begin + GAIN_ROWS]
    row = lax.broadcasted_iota(jnp.int32, (GAIN_ROWS, own), 0)
    from_lane = lax.broadcasted_iota(jnp.int32, (LANES, own), 0)
    to_lane = lax.broadcasted_iota(jnp.int32, (LANES, own), 1)
    high = gains.astype(bf16)
    low = (gains - high.astype(f32)).astype(bf16)
    total = jnp.zeros((GAIN_ROWS, own), f32)
    for c in range(gain_cols):
        pick = jnp.where(from_lane + c * LANES == to_lane + me_ref[0] * own, 1.0, 0.0).astype(bf16)
        found = plain_dot(high, pick) + plain_dot(low, pick)
        total += jnp.where(row == c, found, 0.0)
    outs[-1][...] = jnp.sum(total, axis=0, keepdims=True)


def relative_places(shard_count):
    along = shard_count // 4
    mine = lax.axis_index("shard")
    part = jnp.arange(shard_count, dtype=jnp.int32)
    core = lax.rem(part, 2) ^ lax.rem(mine, 2)
    side = lax.rem(part // 2, 2) ^ lax.rem(mine // 2, 2)
    steps = lax.rem(part // 4 - mine // 4 + along, along)
    return (core * 2 + side) * along + steps


def to_core(value):
    count = lax.axis_size("shard")
    return lax.ppermute(value, "shard", [(i, i ^ 1) for i in range(count)])


def to_side(value):
    count = lax.axis_size("shard")
    return lax.ppermute(value, "shard", [(i, i ^ 2) for i in range(count)])


def along_z(value, step):
    count = lax.axis_size("shard")
    return lax.ppermute(value, "shard", [(i, (i + 4 * step) % count) for i in range(count)])


def scatter_queue(packed):
    return lax.psum_scatter(packed.reshape(-1, LANES), "shard", scatter_dimension=0, tiled=True)


def to_replica(value):
    return lax.ppermute(value, "replica", [(0, 1), (1, 0)])


def half_of(value, which):
    rows = value.shape[1] // 2
    return lax.dynamic_slice_in_dim(value, which * rows, rows, axis=1)


def scatter_permute(keep, send, later):
    along = keep.shape[0] // 2
    pair = lax.axis_size("replica") == 2
    came = to_core(send)
    parts = (keep, came)
    if pair:
        mine = lax.axis_index("replica")
        pass_y = sum(half_of(p, 1 - mine).astype(f32) for p in parts).astype(bf16)
        came_y = to_replica(pass_y)
        parts = tuple(half_of(p, mine) for p in parts) + (came_y,)
    pass_on = sum(p[along:].astype(f32) for p in parts).astype(bf16)
    crossed = to_side(pass_on)
    column = (sum(p[:along].astype(f32) for p in parts) + crossed.astype(f32)).astype(bf16)
    found = [along_z(column[k], k) for k in range(1, along)]
    total = column[0].astype(f32)
    for piece in found:
        total = total + piece.astype(f32)
    total, later = lax.optimization_barrier((total.astype(bf16), later))
    if pair:
        return total, to_replica(total), later
    return *replica_rounds(total), later


def replica_rounds(share):
    count = lax.axis_size("replica")
    step = 1
    other = jnp.zeros_like(share)
    while step < count:
        if step > 1:
            share = (share.astype(f32) + other.astype(f32)).astype(bf16)
        other = lax.ppermute(share, "replica", [(i, i ^ step) for i in range(count)])
        step *= 2
    return share, other


def finish(share, other, layout, own, parts, halves):
    me = jnp.stack([lax.axis_index("shard"), lax.axis_index("replica")]).astype(jnp.int32)
    rows = share.shape[0] * (2 if halves else 1)
    outs = pl.pallas_call(
        functools.partial(finish_kernel, layout, own, parts * own // LANES, halves),
        out_shape=tuple(jax.ShapeDtypeStruct((r, b * LANES), f32) for r, b in layout)
        + (jax.ShapeDtypeStruct((1, own), f32),),
        in_specs=[smem(), vmem(), vmem()],
        out_specs=(vmem(),) * (len(layout) + 1),
        scratch_shapes=[pltpu.VMEM((rows, LANES), f32)],
        compiler_params=params(),
        cost_estimate=cost(0, 4 << 20),
        name="finish",
    )(me, share, other)
    return outs[:-1] + (outs[-1][0],)


def to_blocks(mat, parts):
    rows = mat.shape[0] // parts
    cols = mat.shape[1] // LANES
    split = mat.reshape(parts, rows, cols, LANES).transpose(0, 2, 1, 3)
    return split.reshape(parts, cols * rows, LANES)


def pack_own(mats):
    return jnp.concatenate([to_blocks(m, 1)[0] for m in mats], axis=0)


def gather_queue(packed):
    whole = lax.all_gather(packed, "shard", axis=0, tiled=True)
    return whole.reshape(-1, packed.shape[0], LANES)


def shards(
    x_in,
    seq_units,
    deal,
    gain_attn,
    w_query,
    w_key,
    w_value,
    w_out,
    gain_ffn,
    w_gate,
    w_up,
    w_down,
    d_out,
):
    shard_count = lax.axis_size("shard")
    my_index = lax.axis_index("shard")
    given, width = x_in.shape[1:]
    span = d_out.shape[2]
    unit_max = span // shard_count
    rows = w_query.shape[0]
    down = w_down.shape[0]
    slot_ids = jnp.arange(shard_count, dtype=jnp.int32)
    outgoing = deal_rows(seq_units, deal, x_in[0], shard_count, unit_max)
    arrived = lax.all_to_all(outgoing, "shard", split_axis=0, concat_axis=0, tiled=True)
    own_seq = jnp.sum(jnp.where(slot_ids == my_index, deal[0], 0))
    count = jnp.sum(jnp.where(slot_ids == own_seq, seq_units[0], 0)).reshape(1)
    attn_own = pack_own((w_query, w_key, w_value, w_out))
    column = [along_z(attn_own, k) for k in range(1, shard_count // 4)]
    ffn_own = pack_own((w_gate, w_up, w_down))
    ffn_own, attn_own, _, *column = lax.optimization_barrier((ffn_own, attn_own, outgoing, *column))
    ffn_pack = gather_queue(ffn_own)
    here = jnp.stack([attn_own, *column])
    beside = to_side(here)
    pieces = (here, beside, to_core(here), to_core(beside))
    tokens = arrived.reshape(span, width)
    gain_one = gain_attn.reshape(1, width)
    gain_two = gain_ffn.reshape(1, width)
    n1, qkv, attn_pack = make_qkv(
        lax.axis_index("shard").reshape(1), tokens, gain_one, pieces, rows
    )
    mixed, lse = attend_forward(count, qkv, unit_max)
    hidden, n2 = out_project(tokens, mixed, attn_pack, gain_two, rows)
    layer_out, g_h, g_hb, ffn_grads = ffn_both(
        count, hidden, n2, d_out[0, 0], gain_two, ffn_pack, unit_max, rows, down
    )
    own = width // shard_count
    cols = width // LANES
    wide = w_gate.shape[1] // LANES
    ffn_share = scatter_queue(ffn_grads)
    place = relative_places(shard_count)
    g_x, keep, send = attend_back(
        count, place, qkv, mixed, lse, n1, tokens, g_h, g_hb, gain_one, attn_pack, unit_max, rows
    )
    returned = lax.all_to_all(
        g_x.reshape(shard_count, unit_max, width), "shard", split_axis=0, concat_axis=0, tiled=True
    )
    grad_x = undeal_rows(seq_units, deal, returned, given)[None]
    attn_mine, attn_other, ffn_share = scatter_permute(keep, send, ffn_share)
    out_wq, out_wk, out_wv, out_wo, out_gain_one = finish(
        attn_mine,
        attn_other,
        ((rows, cols),) * 4,
        own,
        shard_count,
        lax.axis_size("replica") == 2,
    )
    out_wg, out_wu, out_wd, out_gain_two = finish(
        *replica_rounds(ffn_share),
        ((rows, wide), (rows, wide), (down, cols)),
        own,
        shard_count,
        False,
    )
    return (
        layer_out.reshape(1, 1, span, width),
        grad_x,
        out_gain_one,
        out_gain_two,
        out_wq,
        out_wk,
        out_wv,
        out_wo,
        out_wg,
        out_wu,
        out_wd,
    )


def solution(mesh):
    return jax.shard_map(
        shards,
        mesh=mesh,
        in_specs=(
            P("replica", "shard", None),
            P("replica", None),
            P("replica", None),
            P(),
            P("shard", None),
            P("shard", None),
            P("shard", None),
            P("shard", None),
            P(),
            P("shard", None),
            P("shard", None),
            P("shard", None),
            P("replica", "shard", None, None),
        ),
        out_specs=(
            P("replica", "shard", None, None),
            P("replica", "shard", None),
            P("shard"),
            P("shard"),
            P("shard", None),
            P("shard", None),
            P("shard", None),
            P("shard", None),
            P("shard", None),
            P("shard", None),
            P("shard", None),
        ),
        check_vma=False,
    )
```

```python
import functools

import jax
import jax.numpy as jnp
from jax import lax
from jax.experimental import pallas as pl
from jax.experimental.pallas import tpu as pltpu
from jax.sharding import PartitionSpec as P

H = 12
HD = 64
LANES = 256
GAIN_ROWS = 16

norm_eps = 1e-06
neg_big = -1e30
bf16 = jnp.bfloat16
f32 = jnp.float32


def left_dot(lhs_mat, rhs_mat):
    return lax.dot_general(
        lhs_mat, rhs_mat, (((0,), (0,)), ((), ())), preferred_element_type=jnp.float32
    )


def right_dot(lhs_mat, rhs_mat):
    return lax.dot_general(
        lhs_mat, rhs_mat, (((1,), (1,)), ((), ())), preferred_element_type=jnp.float32
    )


def plain_dot(lhs_mat, rhs_mat):
    return jnp.dot(lhs_mat, rhs_mat, preferred_element_type=jnp.float32)


def slot_start(units_ref, order_ref, slot, shard_count):
    wanted = order_ref[0, slot]
    start = jnp.int32(0)
    count = jnp.int32(0)
    for k in range(shard_count):
        units = units_ref[0, k]
        start = start + jnp.where(k < wanted, units, 0)
        count = count + jnp.where(k == wanted, units, 0)
    return start, count


def pick_rows(units_ref, order_ref, pick_ref, shard_count, unit_max):
    given = pick_ref.shape[1]
    row = lax.broadcasted_iota(jnp.int32, (unit_max, given), 0)
    ahead = lax.broadcasted_iota(jnp.int32, (unit_max, given), 1) - row

    def step(slot, carry):
        start, count = slot_start(units_ref, order_ref, slot, shard_count)
        pick = jnp.where((ahead == start) & (row < count), 1.0, 0.0).astype(bf16)
        pick_ref[pl.ds(pl.multiple_of(slot * unit_max, unit_max), unit_max), :] = pick
        return carry

    lax.fori_loop(0, shard_count, step, 0)


def deal_kernel(units_ref, order_ref, rows_ref, out_ref, pick_ref):
    shard_count, unit_max, width = out_ref.shape
    pick_rows(units_ref, order_ref, pick_ref, shard_count, unit_max)
    found = plain_dot(pick_ref[...], rows_ref[...]).astype(bf16)
    out_ref[...] = found.reshape(shard_count, unit_max, width)


def undeal_kernel(units_ref, order_ref, back_ref, out_ref, pick_ref):
    shard_count, unit_max, width = back_ref.shape
    pick_rows(units_ref, order_ref, pick_ref, shard_count, unit_max)
    whole = back_ref[...].reshape(shard_count * unit_max, width)
    out_ref[...] = left_dot(pick_ref[...], whole).astype(bf16)


def smem():
    return pl.BlockSpec(memory_space=pltpu.SMEM)


def vmem():
    return pl.BlockSpec(memory_space=pltpu.VMEM)


def deal_rows(units, order, rows, shard_count, unit_max):
    return pl.pallas_call(
        deal_kernel,
        out_shape=jax.ShapeDtypeStruct((shard_count, unit_max, rows.shape[1]), bf16),
        in_specs=[smem(), smem(), vmem()],
        out_specs=vmem(),
        scratch_shapes=[pltpu.VMEM((shard_count * unit_max, rows.shape[0]), bf16)],
        name="deal_rows",
    )(units, order, rows)


def undeal_rows(units, order, back, given):
    shard_count, unit_max, width = back.shape
    return pl.pallas_call(
        undeal_kernel,
        out_shape=jax.ShapeDtypeStruct((given, width), bf16),
        in_specs=[smem(), smem(), vmem()],
        out_specs=vmem(),
        scratch_shapes=[pltpu.VMEM((shard_count * unit_max, given), bf16)],
        name="undeal_rows",
    )(units, order, back)


def const_block(shape):
    zeros = (0,) * len(shape)
    return pl.BlockSpec(shape, lambda *_: zeros)


def params(mib):
    return pltpu.CompilerParams(vmem_limit_bytes=mib << 20)


def cost(flops, moved, trans=0):
    return pl.CostEstimate(flops=flops, bytes_accessed=moved, transcendentals=trans)


def inverse_rms(rows):
    return lax.rsqrt(jnp.mean(rows * rows, axis=-1, keepdims=True) + norm_eps)


def whole_block(ref):
    parts, rows, lanes = ref.shape
    return ref[...].reshape(parts * rows, lanes)


def qkv_kernel(me_ref, x_ref, gain_ref, a_ref, b_ref, fa_ref, fb_ref, n1_ref, qkv_ref, w_ref):
    block = pl.program_id(0)
    along = a_ref.shape[0]
    width = n1_ref.shape[1]
    me = me_ref[0]
    core = lax.rem(me, 2)
    side = lax.rem(lax.div(me, 2), 2)
    height = lax.div(me, 4)

    @pl.when(block == 0)
    def _():
        rows = x_ref[...].astype(f32)
        n1_ref[...] = (rows * inverse_rms(rows) * gain_ref[...]).astype(bf16)

    for step in range(along):
        there = lax.rem(height - step + along, along) * 4
        w_ref[there + 2 * side + core] = a_ref[step]
        w_ref[there + 2 * side + 1 - core] = fa_ref[step]
        w_ref[there + 2 * (1 - side) + core] = b_ref[step]
        w_ref[there + 2 * (1 - side) + 1 - core] = fb_ref[step]

    @pl.when(block < 3)
    def _():
        factor = jnp.where(block == 0, HD ** (-0.5), 1.0)
        cols = width // LANES
        rows = w_ref.shape[1] // cols
        for c in range(cols):
            weight = w_ref[:, c * rows : (c + 1) * rows, :].reshape(width, LANES)
            made = plain_dot(n1_ref[...], weight).astype(bf16).astype(f32)
            qkv_ref[:, c * LANES : (c + 1) * LANES] = (made * factor).astype(bf16)


def make_qkv(me, tokens, gain, pieces, rows):
    span, width = tokens.shape
    along = pieces[0].shape[0]
    cols = width // LANES
    piece = pl.BlockSpec((along, cols * rows, LANES), lambda j: (0, j, 0))
    return pl.pallas_call(
        qkv_kernel,
        grid=(4,),
        out_shape=(
            jax.ShapeDtypeStruct((span, width), bf16),
            jax.ShapeDtypeStruct((span, 3 * width), bf16),
            jax.ShapeDtypeStruct((4 * along, 4 * cols * rows, LANES), bf16),
        ),
        in_specs=[
            smem(),
            const_block((span, width)),
            const_block((1, width)),
            piece,
            piece,
            piece,
            piece,
        ],
        out_specs=(
            const_block((span, width)),
            pl.BlockSpec((span, width), lambda j: (0, jnp.minimum(j, 2))),
            pl.BlockSpec((4 * along, cols * rows, LANES), lambda j: (0, j, 0)),
        ),
        compiler_params=params(24),
        cost_estimate=cost(6 * span * width * width, 14 << 20),
        name="make_qkv",
    )(me, tokens, gain, *pieces)


def live_bias(count, span, unit_max):
    row = lax.broadcasted_iota(jnp.int32, (span, 2 * HD), 0)
    return jnp.where(lax.rem(row, unit_max) < count, 0.0, neg_big).astype(bf16)


def head_keys(keys, bias, lane, head):
    inside = (lane // HD) == head
    return jnp.where(inside, keys, jnp.where(lane == (1 - head) * HD, bias, jnp.zeros_like(keys)))


def head_queries(queries, lane, head):
    inside = (lane // HD) == head
    one = jnp.where(lane == (1 - head) * HD, 1.0, 0.0).astype(bf16)
    return jnp.where(inside, queries, one)


def attend_kernel(unit_max, chunk, count_ref, q_ref, k_ref, v_ref, o_ref, lse_ref, kb_ref, vt_ref, ot_ref):
    span = q_ref.shape[0]
    pair = 2 * HD
    lane = lax.broadcasted_iota(jnp.int32, (span, pair), 1)
    bias = live_bias(count_ref[0], span, unit_max)
    keys = k_ref[...]
    values_t = v_ref[...].T
    for head in range(2):
        kb_ref[head] = head_keys(keys, bias, lane, head)
        vt_ref[head, :HD] = values_t[head * HD : (head + 1) * HD]
        vt_ref[head, HD:] = jnp.ones((vt_ref.shape[1] - HD, span), bf16)
    lane_c = lane[:chunk]
    jobs = [(head, begin) for begin in range(0, span, chunk) for head in range(2)]

    def first(job):
        head, begin = job
        return right_dot(kb_ref[head], head_queries(q_ref[begin : begin + chunk, :], lane_c, head))

    def second(job, scores):
        head, begin = job
        part = slice(begin, begin + chunk)
        top = jnp.max(scores, axis=0, keepdims=True)
        probs = jnp.exp(scores - top).astype(bf16)
        both = plain_dot(vt_ref[head], probs)
        total = both[HD : HD + 1]
        ot_ref[head * HD : (head + 1) * HD, part] = both[:HD] * (1.0 / total)
        lse_ref[0, head : head + 1, part] = top + jnp.log(total)

    held = first(jobs[0])
    for i, job in enumerate(jobs):
        later = first(jobs[i + 1]) if i + 1 < len(jobs) else None
        second(job, held)
        held = later
    o_ref[...] = ot_ref[...].T.astype(bf16)


def attend_forward(count, qkv, unit_max):
    span = qkv.shape[0]
    width = qkv.shape[1] // 3
    pair = 2 * HD
    pairs = width // pair

    def block(first):
        return pl.BlockSpec((span, pair), lambda p: (0, first + p))

    return pl.pallas_call(
        functools.partial(attend_kernel, unit_max, 1024),
        grid=(pairs,),
        out_shape=(
            jax.ShapeDtypeStruct((span, width), bf16),
            jax.ShapeDtypeStruct((pairs, 8, span), f32),
        ),
        in_specs=[smem(), block(0), block(pairs), block(2 * pairs)],
        out_specs=(block(0), pl.BlockSpec((1, 8, span), lambda p: (p, 0, 0))),
        scratch_shapes=[
            pltpu.VMEM((2, span, pair), bf16),
            pltpu.VMEM((2, HD + 16, span), bf16),
            pltpu.VMEM((pair, span), f32),
        ],
        compiler_params=params(32),
        cost_estimate=cost(4 * span * span * width, 8 << 20, span * span * H),
        name="attend_forward",
    )(count, qkv, qkv, qkv)


def out_kernel(x_ref, o_ref, w_ref, gain_ref, h_ref, n2_ref):
    parts, total, lanes = w_ref.shape
    width = h_ref.shape[1]
    rows = width // parts
    for c in range(width // lanes):
        weight = w_ref[:, c * rows : (c + 1) * rows, :].reshape(width, lanes)
        cols = slice(c * lanes, (c + 1) * lanes)
        h_ref[:, cols] = x_ref[:, cols].astype(f32) + plain_dot(o_ref[...], weight)
    hidden = h_ref[...]
    n2_ref[...] = (hidden * inverse_rms(hidden) * gain_ref[...]).astype(bf16)


def out_project(tokens, mixed, packed, gain, rows):
    span, width = tokens.shape
    parts = packed.shape[0]
    blocks = width // LANES
    return pl.pallas_call(
        out_kernel,
        grid=(1,),
        out_shape=(
            jax.ShapeDtypeStruct((span, width), f32),
            jax.ShapeDtypeStruct((span, width), bf16),
        ),
        in_specs=[
            const_block((span, width)),
            const_block((span, width)),
            pl.BlockSpec((parts, blocks * rows, LANES), lambda i: (0, 3, 0)),
            const_block((1, width)),
        ],
        out_specs=(const_block((span, width)), const_block((span, width))),
        compiler_params=params(24),
        cost_estimate=cost(2 * span * width * width, 9 << 20),
        name="out_project",
    )(tokens, mixed, packed, gain)


def spread_gain(total, parts):
    width = total.shape[1]
    own = width // parts
    shape = (parts, GAIN_ROWS, LANES)
    part = lax.broadcasted_iota(jnp.int32, shape, 0)
    row = lax.broadcasted_iota(jnp.int32, shape, 1)
    place = row * LANES + lax.broadcasted_iota(jnp.int32, shape, 2)
    mine = (place >= part * own) & (place < (part + 1) * own)
    out = jnp.zeros(shape, f32)
    for c in range(width // LANES):
        piece = jnp.broadcast_to(total[:, c * LANES : (c + 1) * LANES][None], shape)
        out = jnp.where((row == c) & mine, piece, out)
    return out.astype(bf16)


def ffn_kernel(
    unit_max,
    count_ref,
    h_ref,
    n2_ref,
    d_ref,
    gain_ref,
    wg_ref,
    wu_ref,
    wd_ref,
    out_ref,
    ghb_ref,
    pack_ref,
    gb_ref,
    y_ref,
    gn_ref,
    stage_gate,
    stage_up,
    stage_down,
    stage_gain,
    act_s,
    gg_s,
    gu_s,
    sems,
):
    step = pl.program_id(0)
    steps = pl.num_programs(0)
    slot = lax.rem(step, 2)
    span, width = h_ref.shape
    parts, rows, _ = wg_ref.shape
    few, down_all, _ = wd_ref.shape
    cols = width // LANES
    down = down_all // cols
    ff_blocks = steps

    def copies(which, at):
        return (
            pltpu.make_async_copy(
                stage_gate.at[at],
                pack_ref.at[:, pl.ds(pl.multiple_of(which * rows, 8), rows), :],
                sems.at[0, at],
            ),
            pltpu.make_async_copy(
                stage_up.at[at],
                pack_ref.at[:, pl.ds(pl.multiple_of((ff_blocks + which) * rows, 8), rows), :],
                sems.at[1, at],
            ),
            pltpu.make_async_copy(
                stage_down.at[at],
                pack_ref.at[pl.ds(which * few, few), pl.ds(2 * ff_blocks * rows, down_all), :],
                sems.at[2, at],
            ),
        )

    row = lax.broadcasted_iota(jnp.int32, (span, 1), 0)
    live = lax.rem(row, unit_max) < count_ref[0]

    @pl.when(step == 0)
    def _():
        gb_ref[...] = jnp.where(live, d_ref[...].astype(f32), 0.0).astype(bf16)
        y_ref[...] = jnp.zeros_like(y_ref)
        gn_ref[...] = jnp.zeros_like(gn_ref)

    @pl.when(step >= 2)
    def _():
        for copy in copies(step - 2, slot):
            copy.wait()

    w_gate = whole_block(wg_ref)
    w_up = whole_block(wu_ref)
    downs = [
        wd_ref[:, c * down : (c + 1) * down, :].reshape(few * down, LANES) for c in range(cols)
    ]
    chunk = span // 2

    def first(part):
        n2 = n2_ref[part, :]
        gate = plain_dot(n2, w_gate)
        up = plain_dot(n2, w_up)
        g_act = right_dot(gb_ref[part, :LANES], downs[0])
        for c in range(1, cols):
            g_act += right_dot(gb_ref[part, c * LANES : (c + 1) * LANES], downs[c])
        return gate, up, g_act

    def middle(part, gate, up, g_act):
        c0 = 0.7978845608028654
        c1 = 0.044715
        square = gate * gate
        inner = c0 + (c0 * c1) * square
        tang = jnp.tanh(gate * inner)
        half = 0.5 + 0.5 * tang
        gelu = gate * half
        slope = half + (gate * (0.5 - 0.5 * tang * tang)) * (c0 + (3.0 * c0 * c1) * square)
        act_s[part, :] = (gelu * up).astype(bf16)
        gg_s[part, :] = (g_act * up * slope).astype(bf16)
        gu_s[part, :] = (g_act * gelu).astype(bf16)

    def second(part):
        for c in range(cols):
            place = slice(c * LANES, (c + 1) * LANES)
            add = plain_dot(act_s[part, :], downs[c])
            grad = right_dot(gg_s[part, :], w_gate[place]) + right_dot(gu_s[part, :], w_up[place])
            y_ref[part, place] += add
            gn_ref[part, place] += grad

    parts_of = [slice(i * chunk, (i + 1) * chunk) for i in range(2)]
    held = first(parts_of[0])
    for i, part in enumerate(parts_of):
        later = first(parts_of[i + 1]) if i + 1 < len(parts_of) else None
        middle(part, *held)
        second(part)
        held = later
    for c in range(cols):
        wide = left_dot(act_s[...], gb_ref[:, c * LANES : (c + 1) * LANES]).astype(bf16)
        stage_down[slot, :, c * down : (c + 1) * down, :] = wide.reshape(few, down, LANES)
    stage_gate[slot] = left_dot(n2_ref[...], gg_s[...]).astype(bf16).reshape(parts, rows, LANES)
    stage_up[slot] = left_dot(n2_ref[...], gu_s[...]).astype(bf16).reshape(parts, rows, LANES)
    for copy in copies(step, slot):
        copy.start()

    @pl.when(step == steps - 1)
    def _():
        hidden = h_ref[...]
        out_ref[...] = jnp.where(live, hidden + y_ref[...], 0.0).astype(bf16)
        inv = inverse_rms(hidden)
        grad = gn_ref[...]
        scaled = hidden * inv
        total = jnp.sum(grad * scaled, axis=0, keepdims=True)
        stage_gain[...] = spread_gain(total, parts)
        last = pltpu.make_async_copy(
            stage_gain,
            pack_ref.at[:, pl.ds(2 * ff_blocks * rows + down_all, GAIN_ROWS), :],
            sems.at[3, 0],
        )
        last.start()
        weighted = grad * gain_ref[...]
        mean = jnp.mean(scaled * weighted, axis=-1, keepdims=True)
        g_h = gb_ref[...].astype(f32) + inv * (weighted - scaled * mean)
        ghb_ref[...] = g_h.astype(bf16)
        for copy in copies(step - 1, 1 - slot) + copies(step, slot):
            copy.wait()
        last.wait()


def ffn_both(count, hidden, normed, d_rows, gain, packed, unit_max, rows, down):
    span, width = hidden.shape
    parts = packed.shape[0]
    ff = parts * down
    blocks = ff // LANES
    cols = width // LANES
    few = LANES // down
    moved = 2 * blocks * rows + cols * down
    full = const_block((span, width))
    return pl.pallas_call(
        functools.partial(ffn_kernel, unit_max),
        grid=(blocks,),
        out_shape=(
            jax.ShapeDtypeStruct((span, width), bf16),
            jax.ShapeDtypeStruct((span, width), bf16),
            jax.ShapeDtypeStruct((parts, moved + GAIN_ROWS, LANES), bf16),
        ),
        in_specs=[
            smem(),
            full,
            full,
            full,
            const_block((1, width)),
            pl.BlockSpec((parts, rows, LANES), lambda j: (0, j, 0)),
            pl.BlockSpec((parts, rows, LANES), lambda j: (0, blocks + j, 0)),
            pl.BlockSpec((few, cols * down, LANES), lambda j: (j, 2 * blocks * rows // (cols * down), 0)),
        ],
        out_specs=(full, full, pl.BlockSpec(memory_space=pl.ANY)),
        scratch_shapes=[
            pltpu.VMEM((span, width), bf16),
            pltpu.VMEM((span, width), f32),
            pltpu.VMEM((span, width), f32),
            pltpu.VMEM((2, parts, rows, LANES), bf16),
            pltpu.VMEM((2, parts, rows, LANES), bf16),
            pltpu.VMEM((2, few, cols * down, LANES), bf16),
            pltpu.VMEM((parts, GAIN_ROWS, LANES), bf16),
            pltpu.VMEM((span, LANES), bf16),
            pltpu.VMEM((span, LANES), bf16),
            pltpu.VMEM((span, LANES), bf16),
            pltpu.SemaphoreType.DMA((4, 2)),
        ],
        compiler_params=params(60),
        cost_estimate=cost(18 * span * width * ff, 36 << 20, span * ff),
        name="ffn_both",
    )(count, hidden, normed, d_rows, gain, packed, packed, packed)


def attend_back_kernel(
    unit_max,
    chunk,
    count_ref,
    place_ref,
    q_ref,
    k_ref,
    v_ref,
    o_ref,
    lse_ref,
    n1_ref,
    x_ref,
    ghb_ref,
    gain_ref,
    wq_ref,
    wk_ref,
    wv_ref,
    wo_ref,
    gx_ref,
    keep_ref,
    send_ref,
    wo_s,
    do_s,
    delta_s,
    kt_s,
    dqt_s,
    dk_s,
    dv_s,
    gn_s,
    stage,
    stage_gain,
    sems,
    gain_sem,
):
    step = pl.program_id(0)
    steps = pl.num_programs(0)
    span, width = x_ref.shape
    parts, rows, _ = wq_ref.shape
    cols = width // LANES
    pair = 2 * HD
    heads = LANES // HD
    lane = lax.broadcasted_iota(jnp.int32, (span, pair), 1)
    lane_c = lane[:chunk]
    mine = pl.ds(pl.multiple_of(step * LANES, LANES), LANES)

    half_parts = parts // 2

    def copies(which):
        return [
            pltpu.make_async_copy(
                stage.at[m, pl.ds(side * half_parts, half_parts)],
                to_ref.at[:, pl.ds(pl.multiple_of((m * cols + which) * rows, 8), rows), :],
                sems.at[m, side],
            )
            for m in range(4)
            for side, to_ref in enumerate((keep_ref, send_ref))
        ]

    def put(m, grad):
        for part in range(parts):
            stage[m, place_ref[part]] = grad[part * rows : (part + 1) * rows].astype(bf16)

    @pl.when(step == 0)
    def _():
        gn_s[...] = jnp.zeros_like(gn_s)
        for c in range(cols):
            wo_s[c] = wo_ref[:, c * rows : (c + 1) * rows, :].reshape(width, LANES)

    g_o = right_dot(ghb_ref[:, :LANES], wo_s[0, mine, :])
    for c in range(1, cols):
        g_o += right_dot(ghb_ref[:, c * LANES : (c + 1) * LANES], wo_s[c, mine, :])
    g_o = g_o.astype(bf16)
    do_s[...] = g_o
    prod = g_o.astype(f32) * o_ref[:, mine].astype(f32)
    high = prod.astype(bf16)
    low = (prod - high.astype(f32)).astype(bf16)
    picker = jnp.where(
        lax.broadcasted_iota(jnp.int32, (8, LANES), 1) // HD
        == lax.broadcasted_iota(jnp.int32, (8, LANES), 0),
        1.0,
        0.0,
    ).astype(bf16)
    delta_s[...] = right_dot(picker, high) + right_dot(picker, low)
    kt_s[...] = k_ref[...].T
    dk_s[...] = jnp.zeros_like(dk_s)
    dv_s[...] = jnp.zeros_like(dv_s)
    bias = live_bias(count_ref[0], span, unit_max)

    zero = jnp.zeros((), bf16)

    def some_heads(turn, carry):
        jobs = []
        for u in range(2):
            head = turn * 2 + u
            half = head // 2
            sub = u % 2 if 2 > 1 else lax.rem(head, 2)
            side = pl.ds(pl.multiple_of(half * pair, pair), pair)
            inside = (lane // HD) == sub
            keys = head_keys(k_ref[:, side], bias, lane, sub)
            values = jnp.where(inside, v_ref[:, side], zero)
            for begin in range(0, span, chunk):
                jobs.append((head, half, sub, side, keys, values, slice(begin, begin + chunk)))

        def first(job):
            head, half, sub, side, keys, values, part = job
            scores = right_dot(keys, head_queries(q_ref[part, side], lane_c, sub))
            d_probs = right_dot(values, do_s[part, side])
            return scores, d_probs

        def second(job, scores, d_probs):
            head, half, sub, side, keys, values, part = job
            inside_c = (lane_c // HD) == sub
            probs = jnp.exp(scores - lse_ref[half, pl.ds(sub, 1), part])
            d_scores = (probs * (d_probs - delta_s[pl.ds(head, 1), part])).astype(bf16)
            dv_s[:, side] += plain_dot(probs.astype(bf16), jnp.where(inside_c, do_s[part, side], zero))
            dk_s[:, side] += plain_dot(d_scores, jnp.where(inside_c, q_ref[part, side], zero))
            rows_t = pl.ds(pl.multiple_of(head * HD, HD), HD)
            dqt_s[rows_t, part] = plain_dot(kt_s[rows_t, :], d_scores)

        held = first(jobs[0])
        for i, job in enumerate(jobs):
            later = first(jobs[i + 1]) if i + 1 < len(jobs) else None
            second(job, *held)
            held = later
        return carry

    lax.fori_loop(0, heads // 2, some_heads, 0)
    d_q = (dqt_s[...].T * (HD ** (-0.5))).astype(bf16)
    d_k = dk_s[...].astype(bf16)
    d_v = dv_s[...].astype(bf16)

    add = (
        right_dot(d_q, whole_block(wq_ref))
        + right_dot(d_k, whole_block(wk_ref))
        + right_dot(d_v, whole_block(wv_ref))
    )

    gn_s[...] += add

    @pl.when(step > 0)
    def _():
        for copy in copies(step - 1):
            copy.wait()

    n1 = n1_ref[...]
    for m, grad in enumerate((d_q, d_k, d_v)):
        put(m, left_dot(n1, grad))
    put(3, left_dot(o_ref[...], ghb_ref[:, mine]))
    for copy in copies(step):
        copy.start()

    @pl.when(step == steps - 1)
    def _():
        tokens = x_ref[...].astype(f32)
        inv = inverse_rms(tokens)
        grad = gn_s[...]
        scaled = tokens * inv
        total = jnp.sum(grad * scaled, axis=0, keepdims=True)
        spread = spread_gain(total, parts)
        for part in range(parts):
            stage_gain[place_ref[part]] = spread[part]
        last = [
            pltpu.make_async_copy(
                stage_gain.at[pl.ds(side * half_parts, half_parts)],
                to_ref.at[:, pl.ds(4 * cols * rows, GAIN_ROWS), :],
                gain_sem.at[side],
            )
            for side, to_ref in enumerate((keep_ref, send_ref))
        ]
        for copy in last:
            copy.start()
        weighted = grad * gain_ref[...]
        mean = jnp.mean(scaled * weighted, axis=-1, keepdims=True)
        gx_ref[...] = (ghb_ref[...].astype(f32) + inv * (weighted - scaled * mean)).astype(bf16)
        for copy in copies(step) + last:
            copy.wait()


def attend_back(count, place, qkv, mixed, lse, n1, tokens, g_hb, gain, packed, unit_max, rows):
    span, width = tokens.shape
    parts = packed.shape[0]
    cols = width // LANES
    full = const_block((span, width))

    def block(first):
        return pl.BlockSpec((span, LANES), lambda p: (0, first + p))

    def weight(first):
        return pl.BlockSpec((parts, rows, LANES), lambda p: (0, first + p, 0))

    return pl.pallas_call(
        functools.partial(attend_back_kernel, unit_max, 512),
        grid=(cols,),
        out_shape=(
            jax.ShapeDtypeStruct((span, width), bf16),
            jax.ShapeDtypeStruct((parts // 2, 4 * cols * rows + GAIN_ROWS, LANES), bf16),
            jax.ShapeDtypeStruct((parts // 2, 4 * cols * rows + GAIN_ROWS, LANES), bf16),
        ),
        in_specs=[
            smem(),
            smem(),
            block(0),
            block(cols),
            block(2 * cols),
            full,
            pl.BlockSpec((2, 8, span), lambda p: (p, 0, 0)),
            full,
            full,
            full,
            const_block((1, width)),
            weight(0),
            weight(cols),
            weight(2 * cols),
            pl.BlockSpec((parts, cols * rows, LANES), lambda p: (0, 3, 0)),
        ],
        out_specs=(full, pl.BlockSpec(memory_space=pl.ANY), pl.BlockSpec(memory_space=pl.ANY)),
        scratch_shapes=[
            pltpu.VMEM((cols, width, LANES), bf16),
            pltpu.VMEM((span, LANES), bf16),
            pltpu.VMEM((8, span), f32),
            pltpu.VMEM((LANES, span), bf16),
            pltpu.VMEM((LANES, span), f32),
            pltpu.VMEM((span, LANES), f32),
            pltpu.VMEM((span, LANES), f32),
            pltpu.VMEM((span, width), f32),
            pltpu.VMEM((4, parts, rows, LANES), bf16),
            pltpu.VMEM((parts, GAIN_ROWS, LANES), bf16),
            pltpu.SemaphoreType.DMA((4, 2)),
            pltpu.SemaphoreType.DMA((2,)),
        ],
        compiler_params=params(48),
        cost_estimate=cost(10 * span * span * width + 16 * span * width * width, 24 << 20, span * span * H),
        name="attend_back",
    )(count, place, qkv, qkv, qkv, mixed, lse, n1, tokens, g_hb, gain, packed, packed, packed, packed)


def finish_kernel(layout, own, gain_cols, halves, me_ref, mine_ref, other_ref, *outs):
    outs, sum_ref = outs[:-1], outs[-1]
    if halves:
        rows = mine_ref.shape[0]
        first = me_ref[1]
        sum_ref[pl.ds(pl.multiple_of(first * rows, 8), rows), :] = mine_ref[...].astype(f32)
        sum_ref[pl.ds(pl.multiple_of((1 - first) * rows, 8), rows), :] = other_ref[...].astype(f32)
    else:
        sum_ref[...] = mine_ref[...].astype(f32) + other_ref[...].astype(f32)
    begin = 0
    for (rows, blocks), out_ref in zip(layout, outs[:-1]):
        for c in range(blocks):
            out_ref[:, c * LANES : (c + 1) * LANES] = sum_ref[begin : begin + rows]
            begin += rows
    gains = sum_ref[begin : begin + GAIN_ROWS]
    row = lax.broadcasted_iota(jnp.int32, (GAIN_ROWS, own), 0)
    from_lane = lax.broadcasted_iota(jnp.int32, (LANES, own), 0)
    to_lane = lax.broadcasted_iota(jnp.int32, (LANES, own), 1)
    high = gains.astype(bf16)
    low = (gains - high.astype(f32)).astype(bf16)
    total = jnp.zeros((GAIN_ROWS, own), f32)
    for c in range(gain_cols):
        pick = jnp.where(from_lane + c * LANES == to_lane + me_ref[0] * own, 1.0, 0.0).astype(bf16)
        found = plain_dot(high, pick) + plain_dot(low, pick)
        total += jnp.where(row == c, found, 0.0)
    outs[-1][...] = jnp.sum(total, axis=0, keepdims=True)


def relative_places(shard_count):
    along = shard_count // 4
    mine = lax.axis_index("shard")
    part = jnp.arange(shard_count, dtype=jnp.int32)
    core = lax.rem(part, 2) ^ lax.rem(mine, 2)
    side = lax.rem(part // 2, 2) ^ lax.rem(mine // 2, 2)
    steps = lax.rem(part // 4 - mine // 4 + along, along)
    return (core * 2 + side) * along + steps


def to_core(value):
    count = lax.axis_size("shard")
    return lax.ppermute(value, "shard", [(i, i ^ 1) for i in range(count)])


def to_side(value):
    count = lax.axis_size("shard")
    return lax.ppermute(value, "shard", [(i, i ^ 2) for i in range(count)])


def along_z(value, step):
    count = lax.axis_size("shard")
    return lax.ppermute(value, "shard", [(i, (i + 4 * step) % count) for i in range(count)])


def scatter_queue(packed):
    return lax.psum_scatter(packed.reshape(-1, LANES), "shard", scatter_dimension=0, tiled=True)


def to_replica(value):
    return lax.ppermute(value, "replica", [(0, 1), (1, 0)])


def half_of(value, which):
    rows = value.shape[1] // 2
    return lax.dynamic_slice_in_dim(value, which * rows, rows, axis=1)


def scatter_permute(keep, send, later):
    along = keep.shape[0] // 2
    pair = lax.axis_size("replica") == 2
    came = to_core(send)
    parts = (keep, came)
    if pair:
        mine = lax.axis_index("replica")
        pass_y = sum(half_of(p, 1 - mine).astype(f32) for p in parts).astype(bf16)
        came_y = to_replica(pass_y)
        parts = tuple(half_of(p, mine) for p in parts) + (came_y,)
    pass_on = sum(p[along:].astype(f32) for p in parts).astype(bf16)
    crossed = to_side(pass_on)
    column = (sum(p[:along].astype(f32) for p in parts) + crossed.astype(f32)).astype(bf16)
    column, later = lax.optimization_barrier((column, later))
    found = [along_z(column[k], k) for k in range(1, along)]
    total = column[0].astype(f32)
    for piece in found:
        total = total + piece.astype(f32)
    total = total.astype(bf16)
    if pair:
        return total, to_replica(total), later
    return *replica_rounds(total), later


def replica_rounds(share):
    count = lax.axis_size("replica")
    step = 1
    other = jnp.zeros_like(share)
    while step < count:
        if step > 1:
            share = (share.astype(f32) + other.astype(f32)).astype(bf16)
        other = lax.ppermute(share, "replica", [(i, i ^ step) for i in range(count)])
        step *= 2
    return share, other


def finish(share, other, layout, own, parts, halves):
    me = jnp.stack([lax.axis_index("shard"), lax.axis_index("replica")]).astype(jnp.int32)
    rows = share.shape[0] * (2 if halves else 1)
    outs = pl.pallas_call(
        functools.partial(finish_kernel, layout, own, parts * own // LANES, halves),
        out_shape=tuple(jax.ShapeDtypeStruct((r, b * LANES), f32) for r, b in layout)
        + (jax.ShapeDtypeStruct((1, own), f32),),
        in_specs=[smem(), vmem(), vmem()],
        out_specs=(vmem(),) * (len(layout) + 1),
        scratch_shapes=[pltpu.VMEM((rows, LANES), f32)],
        compiler_params=params(40),
        cost_estimate=cost(0, 4 << 20),
        name="finish",
    )(me, share, other)
    return outs[:-1] + (outs[-1][0],)


def pack_kernel(*refs):
    out_ref, sems = refs[-2:]
    begin = 0
    copies = []
    for mat_ref in refs[:-2]:
        rows, cols = mat_ref.shape
        for c in range(cols // LANES):
            copies.append(
                pltpu.make_async_copy(
                    mat_ref.at[:, pl.ds(c * LANES, LANES)],
                    out_ref.at[pl.ds(begin, rows), :],
                    sems.at[len(copies)],
                )
            )
            begin += rows
    for copy in copies:
        copy.start()
    for copy in copies:
        copy.wait()


def pack_own(mats):
    total = sum(m.shape[0] * m.shape[1] for m in mats) // LANES
    blocks = sum(m.shape[1] for m in mats) // LANES
    return pl.pallas_call(
        pack_kernel,
        out_shape=jax.ShapeDtypeStruct((total, LANES), bf16),
        in_specs=[pl.BlockSpec(memory_space=pl.ANY)] * len(mats),
        out_specs=vmem(),
        scratch_shapes=[pltpu.SemaphoreType.DMA((blocks,))],
        compiler_params=params(62),
        cost_estimate=cost(0, 4 * total * LANES),
        name="pack_own",
    )(*mats)


def gather_queue(packed):
    whole = lax.all_gather(packed, "shard", axis=0, tiled=True)
    return whole.reshape(-1, packed.shape[0], LANES)


def shards(
    x_in,
    seq_units,
    deal,
    gain_attn,
    w_query,
    w_key,
    w_value,
    w_out,
    gain_ffn,
    w_gate,
    w_up,
    w_down,
    d_out,
):
    shard_count = lax.axis_size("shard")
    my_index = lax.axis_index("shard")
    given, width = x_in.shape[1:]
    span = d_out.shape[2]
    unit_max = span // shard_count
    rows = w_query.shape[0]
    down = w_down.shape[0]
    slot_ids = jnp.arange(shard_count, dtype=jnp.int32)
    outgoing = deal_rows(seq_units, deal, x_in[0], shard_count, unit_max)
    arrived = lax.all_to_all(outgoing, "shard", split_axis=0, concat_axis=0, tiled=True)
    own_seq = jnp.sum(jnp.where(slot_ids == my_index, deal[0], 0))
    count = jnp.sum(jnp.where(slot_ids == own_seq, seq_units[0], 0)).reshape(1)
    attn_own = pack_own((w_query, w_key, w_value, w_out))
    column = [along_z(attn_own, k) for k in range(1, shard_count // 4)]
    ffn_own = pack_own((w_gate, w_up, w_down))
    ffn_own, attn_own, _, *column = lax.optimization_barrier((ffn_own, attn_own, outgoing, *column))
    ffn_pack = gather_queue(ffn_own)
    here = jnp.stack([attn_own, *column])
    beside = to_side(here)
    pieces = (here, beside, to_core(here), to_core(beside))
    tokens = arrived.reshape(span, width)
    gain_one = gain_attn.reshape(1, width)
    gain_two = gain_ffn.reshape(1, width)
    n1, qkv, attn_pack = make_qkv(
        lax.axis_index("shard").reshape(1), tokens, gain_one, pieces, rows
    )
    mixed, lse = attend_forward(count, qkv, unit_max)
    hidden, n2 = out_project(tokens, mixed, attn_pack, gain_two, rows)
    layer_out, g_hb, ffn_grads = ffn_both(
        count, hidden, n2, d_out[0, 0], gain_two, ffn_pack, unit_max, rows, down
    )
    own = width // shard_count
    cols = width // LANES
    wide = w_gate.shape[1] // LANES
    ffn_share = scatter_queue(ffn_grads)
    place = relative_places(shard_count)
    g_x, keep, send = attend_back(
        count, place, qkv, mixed, lse, n1, tokens, g_hb, gain_one, attn_pack, unit_max, rows
    )
    returned = lax.all_to_all(
        g_x.reshape(shard_count, unit_max, width), "shard", split_axis=0, concat_axis=0, tiled=True
    )
    grad_x = undeal_rows(seq_units, deal, returned, given)[None]
    attn_mine, attn_other, ffn_share = scatter_permute(keep, send, ffn_share)
    out_wg, out_wu, out_wd, out_gain_two = finish(
        *replica_rounds(ffn_share),
        ((rows, wide), (rows, wide), (down, cols)),
        own,
        shard_count,
        False,
    )
    attn_other, out_gain_two = lax.optimization_barrier((attn_other, out_gain_two))
    out_wq, out_wk, out_wv, out_wo, out_gain_one = finish(
        attn_mine,
        attn_other,
        ((rows, cols),) * 4,
        own,
        shard_count,
        lax.axis_size("replica") == 2,
    )
    return (
        layer_out.reshape(1, 1, span, width),
        grad_x,
        out_gain_one,
        out_gain_two,
        out_wq,
        out_wk,
        out_wv,
        out_wo,
        out_wg,
        out_wu,
        out_wd,
    )


def solution(mesh):
    return jax.shard_map(
        shards,
        mesh=mesh,
        in_specs=(
            P("replica", "shard", None),
            P("replica", None),
            P("replica", None),
            P(),
            P("shard", None),
            P("shard", None),
            P("shard", None),
            P("shard", None),
            P(),
            P("shard", None),
            P("shard", None),
            P("shard", None),
            P("replica", "shard", None, None),
        ),
        out_specs=(
            P("replica", "shard", None, None),
            P("replica", "shard", None),
            P("shard"),
            P("shard"),
            P("shard", None),
            P("shard", None),
            P("shard", None),
            P("shard", None),
            P("shard", None),
            P("shard", None),
            P("shard", None),
        ),
        check_vma=False,
    )
```
